32 devices in a mesh: seq: 8 (over z, y), tp: 4 (over x, core).
Axes of the slice: x: 2, y: 2, z: 4, core: 2. Of those that a mesh axis runs over, the one named last changes fastest.
Arguments:
- hidden_in: bfloat16 [8192, 1024], P(('seq', 'tp')), may hold values from -6 to 6
- memory: bfloat16 [8, 588, 1024], P('seq'), may hold values from -6 to 6
- page_ids: int32 [8192], P('seq'), may hold values from 0 to 7, as said below
- token_offsets: int32 [8192], P('seq'), may hold values from 0 to 1535, as said below
- memory_mask: int32 [8, 588], P('seq'), may hold values from 0 to 1, as said below
- attn_query: bfloat16 [1024, 1024], P(None, 'tp'), may hold values from -0.1875 to 0.1875
- attn_key: bfloat16 [1024, 1024], P(None, 'tp'), may hold values from -0.1875 to 0.1875
- attn_value: bfloat16 [1024, 1024], P(None, 'tp'), may hold values from -0.1875 to 0.1875
- attn_output: bfloat16 [1024, 1024], P('tp'), may hold values from -0.75 to 0.75
- cross_query: bfloat16 [1024, 1024], P(None, 'tp'), may hold values from -0.1875 to 0.1875
- cross_key: bfloat16 [1024, 1024], P(None, 'tp'), may hold values from -0.1875 to 0.1875
- cross_value: bfloat16 [1024, 1024], P(None, 'tp'), may hold values from -0.1875 to 0.1875
- cross_output: bfloat16 [1024, 1024], P('tp'), may hold values from -0.75 to 0.75
- ffn_up: bfloat16 [1024, 4096], P(None, 'tp'), may hold values from -0.1875 to 0.1875
- ffn_down: bfloat16 [4096, 1024], P('tp'), may hold values from -0.125 to 0.125
- self_gain: float32 [1024], replicated, may hold values from 0.5 to 1.5
- self_shift: float32 [1024], replicated, may hold values from -1.8 to 1.8
- cross_gain: float32 [1024], replicated, may hold values from 0.5 to 1.5
- cross_shift: float32 [1024], replicated, may hold values from -1.8 to 1.8
- ffn_gain: float32 [1024], replicated, may hold values from 0.5 to 1.5
- ffn_shift: float32 [1024], replicated, may hold values from -1.8 to 1.8
- out_grad: bfloat16 [8192, 1024], P(('seq', 'tp')), may hold values from -6 to 6
Outputs:
- hidden_out: bfloat16 [8192, 1024], P(('seq', 'tp'))
- grad_hidden: float32 [8192, 1024], P(('seq', 'tp'))
- grad_memory: float32 [8, 588, 1024], P('seq', None, 'tp')
- grad_attn_query: float32 [1024, 1024], P('seq', 'tp')
- grad_attn_key: float32 [1024, 1024], P('seq', 'tp')
- grad_attn_value: float32 [1024, 1024], P('seq', 'tp')
- grad_attn_output: float32 [1024, 1024], P('tp', 'seq')
- grad_cross_query: float32 [1024, 1024], P('seq', 'tp')
- grad_cross_key: float32 [1024, 1024], P('seq', 'tp')
- grad_cross_value: float32 [1024, 1024], P('seq', 'tp')
- grad_cross_output: float32 [1024, 1024], P('tp', 'seq')
- grad_ffn_up: float32 [1024, 4096], P('seq', 'tp')
- grad_ffn_down: float32 [4096, 1024], P('tp', 'seq')
- grad_self_gain: float32 [1024], P(('seq', 'tp'))
- grad_self_shift: float32 [1024], P(('seq', 'tp'))
- grad_cross_gain: float32 [1024], P(('seq', 'tp'))
- grad_cross_shift: float32 [1024], P(('seq', 'tp'))
- grad_ffn_gain: float32 [1024], P(('seq', 'tp'))
- grad_ffn_shift: float32 [1024], P(('seq', 'tp'))
The draws below stay inside these ranges and needn't reach their ends.
Inputs may be any that keep to these rules, and one draw needn't show every extreme that they name: `page_ids`: tokens are packed page after page, each page's tokens contiguous; half of the 8 pages hold 1536 tokens and half 512; which page comes at which place in the pack is drawn from the seed, except that page 4 always comes first. `token_offsets`: each token's position in its page, counting from 0. `memory_mask`: A page of 1536 tokens has all 588 memory positions valid, a page of 512 tokens the first 147.
All inputs are finite; a program needn't handle non-finite values.
Results may differ from the reference program's by a relative error of at most 0.023.
Values may be sent and summed in bfloat16 or wider, within the bound.
A program may use at most 256 MiB of HBM per device.

```python
import jax
import jax.numpy as jnp
from jax import lax

D = 1024
HEADS = 16
HEAD_DIM = 64
FF = 4096
MEM = 588
MEM_SHORT = 147
LONG = 1536
SHORT = 512
PAGES = 8
TOKENS = 8192


def page_layout(key):
    long_pick = jax.random.permutation(jax.random.fold_in(key, 7), PAGES)
    page_long = long_pick < PAGES // 2
    shuffled = jax.random.permutation(jax.random.fold_in(key, 11), PAGES).astype(jnp.int32)
    slots = jnp.arange(PAGES, dtype=jnp.int32)
    middle = PAGES // 2
    slot_page = jnp.where(slots == 0, middle, jnp.where(shuffled == middle, shuffled[0], shuffled)).astype(jnp.int32)
    lengths = jnp.where(page_long[slot_page], LONG, SHORT).astype(jnp.int32)
    ends = jnp.cumsum(lengths).astype(jnp.int32)
    starts = ends - lengths
    positions = jnp.arange(TOKENS, dtype=jnp.int32)
    slot_of = jnp.sum((positions[:, None] >= ends[None, :]).astype(jnp.int32), axis=1).astype(jnp.int32)
    page_of = slot_page[slot_of]
    offsets_in = positions - starts[slot_of]
    return (page_long, page_of, offsets_in)


def draw_page_ids(key, part):
    page_long, page_of, offsets_in = page_layout(key)
    return page_of


def draw_token_offsets(key, part):
    page_long, page_of, offsets_in = page_layout(key)
    return offsets_in


def draw_memory_mask(key, part):
    page_long, page_of, offsets_in = page_layout(key)
    spots = jnp.arange(MEM, dtype=jnp.int32)
    valid = jnp.where(page_long[:, None], spots[None, :] < MEM, spots[None, :] < MEM_SHORT)
    return valid.astype(jnp.int32)


def steps_of(rng, extent, pieces, low, largest):
    level, own = 1.0, jax.random.fold_in(rng, 6)
    for dim, shards_of in pieces:
        draws = jnp.exp(jax.random.uniform(jax.random.fold_in(own, dim), (shards_of,), jnp.float32, low / len(pieces), largest / len(pieces)))
        level = level * jnp.repeat(draws, extent[dim] // shards_of).reshape([-1 if axis == dim else 1 for axis in range(len(extent))])
    return level


def scatter_about(stream_key, shape, scale, most, split=(), kind=jnp.bfloat16):
    loudness = steps_of(stream_key, shape, split, -0.22, 0.18) if split else 1.0
    array = jax.random.normal(stream_key, shape, jnp.float32) * scale * loudness
    return jnp.minimum(jnp.maximum(array, -most), most).astype(kind)


def setup_inputs(seed: int = 0) -> dict:
    streams_of = jax.random.split(jax.random.key(seed), 23)
    hidden_in = scatter_about(streams_of[0], (TOKENS, D), 1.0, 6.0, ((0, 32),))
    memory = scatter_about(streams_of[1], (PAGES, MEM, D), 1.0, 6.0, ((0, 8),))
    page_ids = draw_page_ids(jax.random.fold_in(streams_of[22], 71), 0)
    token_offsets = draw_token_offsets(jax.random.fold_in(streams_of[22], 71), 0)
    memory_mask = draw_memory_mask(jax.random.fold_in(streams_of[22], 71), 0)
    attn_query = scatter_about(streams_of[5], (D, D), D ** -0.5, 0.1875, ((1, 4),))
    attn_key = scatter_about(streams_of[6], (D, D), D ** -0.5, 0.1875, ((1, 4),))
    attn_value = scatter_about(streams_of[7], (D, D), D ** -0.5, 0.1875, ((1, 4),))
    attn_output = scatter_about(streams_of[8], (D, D), (D // 16) ** -0.5, 0.75, ((0, 4),))
    cross_query = scatter_about(streams_of[9], (D, D), D ** -0.5, 0.1875, ((1, 4),))
    cross_key = scatter_about(streams_of[10], (D, D), D ** -0.5, 0.1875, ((1, 4),))
    cross_value = scatter_about(streams_of[11], (D, D), D ** -0.5, 0.1875, ((1, 4),))
    cross_output = scatter_about(streams_of[12], (D, D), (D // 16) ** -0.5, 0.75, ((0, 4),))
    ffn_up = scatter_about(streams_of[13], (D, FF), D ** -0.5, 0.1875, ((1, 4),))
    ffn_down = scatter_about(streams_of[14], (FF, D), (FF // 2) ** -0.5, 0.125, ((0, 4),))
    self_gain = jnp.clip(1.0 + 0.1 * jax.random.normal(streams_of[15], (D,), jnp.float32), 0.5, 1.5)
    self_shift = scatter_about(streams_of[16], (D,), 0.3, 1.8, (), jnp.float32)
    cross_gain = jnp.clip(1.0 + 0.1 * jax.random.normal(streams_of[17], (D,), jnp.float32), 0.5, 1.5)
    cross_shift = scatter_about(streams_of[18], (D,), 0.3, 1.8, (), jnp.float32)
    ffn_gain = jnp.clip(1.0 + 0.1 * jax.random.normal(streams_of[19], (D,), jnp.float32), 0.5, 1.5)
    ffn_shift = scatter_about(streams_of[20], (D,), 0.3, 1.8, (), jnp.float32)
    out_grad = scatter_about(streams_of[21], (TOKENS, D), 1.0, 6.0, ((0, 32),))
    return {"hidden_in": hidden_in, "memory": memory, "page_ids": page_ids, "token_offsets": token_offsets, "memory_mask": memory_mask, "attn_query": attn_query, "attn_key": attn_key, "attn_value": attn_value, "attn_output": attn_output, "cross_query": cross_query, "cross_key": cross_key, "cross_value": cross_value, "cross_output": cross_output, "ffn_up": ffn_up, "ffn_down": ffn_down, "self_gain": self_gain, "self_shift": self_shift, "cross_gain": cross_gain, "cross_shift": cross_shift, "ffn_gain": ffn_gain, "ffn_shift": ffn_shift, "out_grad": out_grad}


EPS = 1e-05
NEG = -1e+30
HIGH = lax.Precision.HIGHEST

@jax.custom_vjp
def low(v):
    return lax.optimization_barrier(v.astype(jnp.bfloat16)).astype(jnp.float32)

@jax.custom_vjp
def low_back(v):
    return v

def low_keep(v):
    return (low(v), None)

def low_pass(kept, grad):
    return (grad,)

def back_keep(v):
    return (v, None)

def back_low(kept, grad):
    return (low(grad),)
low.defvjp(low_keep, low_pass)
low_back.defvjp(back_keep, back_low)

def both_ways(value):
    return low_back(low(value))

def matmul(left, right):
    return jnp.dot(left, right, precision=HIGH, preferred_element_type=jnp.float32)

def layer_norm(rows, gain, shift):
    center = rows - lax.optimization_barrier(jnp.mean(rows, axis=-1, keepdims=True))
    variance = lax.optimization_barrier(jnp.mean(center * center, axis=-1, keepdims=True))
    return center * lax.rsqrt(variance + EPS) * gain + shift

def self_attention(queries, key_rows, value_rows, page_ids, token_offsets):
    tok_total = queries.shape[0]
    block_rows = min(512, tok_total)
    window = ((LONG - 1) // block_rows + 1) * block_rows
    key_pad = jnp.concatenate([jnp.zeros((window, D), jnp.float32), key_rows], axis=0)
    value_pad = jnp.concatenate([jnp.zeros((window, D), jnp.float32), value_rows], axis=0)
    ids_pad = jnp.concatenate([jnp.full((window,), -1, jnp.int32), page_ids.astype(jnp.int32)])
    offsets_pad = jnp.concatenate([jnp.zeros((window,), jnp.int32), token_offsets.astype(jnp.int32)])
    score_scale = HEAD_DIM ** (-0.5)

    def one_block(index):
        first_row = (index * block_rows).astype(jnp.int32)
        query_block = lax.dynamic_slice_in_dim(queries, first_row, block_rows, 0).reshape(block_rows, HEADS, HEAD_DIM)
        key_block = lax.dynamic_slice_in_dim(key_pad, first_row, window + block_rows, 0).reshape(-1, HEADS, HEAD_DIM)
        value_block = lax.dynamic_slice_in_dim(value_pad, first_row, window + block_rows, 0).reshape(-1, HEADS, HEAD_DIM)
        query_ids = lax.dynamic_slice_in_dim(page_ids.astype(jnp.int32), first_row, block_rows, 0)
        query_offsets = lax.dynamic_slice_in_dim(token_offsets.astype(jnp.int32), first_row, block_rows, 0)
        key_ids = lax.dynamic_slice_in_dim(ids_pad, first_row, window + block_rows, 0)
        key_offsets = lax.dynamic_slice_in_dim(offsets_pad, first_row, window + block_rows, 0)
        scores = low_back(jnp.einsum('qhd,khd->hqk', query_block, key_block, precision=HIGH) * score_scale)
        allowed = (key_ids[None, :] == query_ids[:, None]) & (key_offsets[None, :] <= query_offsets[:, None])
        scores = jnp.where(allowed[None], scores, NEG)
        weights = low(jax.nn.softmax(scores, axis=-1))
        mixed = jnp.einsum('hqk,khd->qhd', weights, value_block, precision=HIGH)
        return mixed.reshape(block_rows, D)
    mixed_all = lax.map(jax.checkpoint(one_block), jnp.arange(tok_total // block_rows, dtype=jnp.int32))
    return both_ways(mixed_all.reshape(tok_total, D))

def cross_attention(queries, memory_keys, memory_values, page_ids, memory_mask):
    tok_total = queries.shape[0]
    block_rows = min(512, tok_total)
    key_heads = memory_keys.reshape(PAGES * MEM, HEADS, HEAD_DIM)
    value_heads = memory_values.reshape(PAGES * MEM, HEADS, HEAD_DIM)
    key_page = jnp.repeat(jnp.arange(PAGES, dtype=jnp.int32), MEM)
    key_valid = memory_mask.reshape(PAGES * MEM)
    score_scale = HEAD_DIM ** (-0.5)

    def one_block(index):
        first_row = (index * block_rows).astype(jnp.int32)
        query_block = lax.dynamic_slice_in_dim(queries, first_row, block_rows, 0).reshape(block_rows, HEADS, HEAD_DIM)
        query_ids = lax.dynamic_slice_in_dim(page_ids.astype(jnp.int32), first_row, block_rows, 0)
        scores = low_back(jnp.einsum('qhd,khd->hqk', query_block, key_heads, precision=HIGH) * score_scale)
        allowed = (key_page[None, :] == query_ids[:, None]) & (key_valid[None, :] > 0)
        scores = jnp.where(allowed[None], scores, NEG)
        weights = low(jax.nn.softmax(scores, axis=-1))
        mixed = jnp.einsum('hqk,khd->qhd', weights, value_heads, precision=HIGH)
        return mixed.reshape(block_rows, D)
    mixed_all = lax.map(jax.checkpoint(one_block), jnp.arange(tok_total // block_rows, dtype=jnp.int32))
    return both_ways(mixed_all.reshape(tok_total, D))

def reference(hidden_in, memory, page_ids, token_offsets, memory_mask, attn_query, attn_key, attn_value, attn_output, cross_query, cross_key, cross_value, cross_output, ffn_up, ffn_down, self_gain, self_shift, cross_gain, cross_shift, ffn_gain, ffn_shift, out_grad):
    floats = [value_in.astype(jnp.float32) for value_in in (hidden_in, memory, attn_query, attn_key, attn_value, attn_output, cross_query, cross_key, cross_value, cross_output, ffn_up, ffn_down, self_gain, self_shift, cross_gain, cross_shift, ffn_gain, ffn_shift)]

    def forward(hidden_f, memory_f, attn_query_f, attn_key_f, attn_value_f, attn_output_f, cross_query_f, cross_key_f, cross_value_f, cross_output_f, ffn_up_f, ffn_down_f, self_gain_f, self_shift_f, cross_gain_f, cross_shift_f, ffn_gain_f, ffn_shift_f):
        normed_self = low(layer_norm(hidden_f, self_gain_f, self_shift_f))
        self_queries = both_ways(matmul(normed_self, attn_query_f))
        self_keys = both_ways(matmul(normed_self, attn_key_f))
        self_values = both_ways(matmul(normed_self, attn_value_f))
        self_mixed = self_attention(self_queries, self_keys, self_values, page_ids, token_offsets)
        residual_one = hidden_f + low_back(matmul(self_mixed, attn_output_f))
        normed_cross = low(layer_norm(residual_one, cross_gain_f, cross_shift_f))
        cross_queries = both_ways(matmul(normed_cross, cross_query_f))
        flat_memory = memory_f.reshape(PAGES * MEM, D)
        memory_keys = both_ways(matmul(flat_memory, cross_key_f))
        memory_values = both_ways(matmul(flat_memory, cross_value_f))
        cross_mixed = cross_attention(cross_queries, memory_keys, memory_values, page_ids, memory_mask)
        residual_two = residual_one + low_back(matmul(cross_mixed, cross_output_f))
        normed_ffn = low(layer_norm(residual_two, ffn_gain_f, ffn_shift_f))
        ffn_pre = low_back(matmul(normed_ffn, ffn_up_f))
        ffn_act = low(jax.nn.gelu(ffn_pre, approximate=False))
        return residual_two + low_back(matmul(ffn_act, ffn_down_f))
    output, pullback = jax.vjp(forward, *floats)
    gradients = pullback(out_grad.astype(jnp.float32))
    return (output.astype(jnp.bfloat16), gradients[0], gradients[1], gradients[2], gradients[3], gradients[4], gradients[5], gradients[6], gradients[7], gradients[8], gradients[9], gradients[10], gradients[11], gradients[12], gradients[13], gradients[14], gradients[15], gradients[16], gradients[17])
```

```python
import functools

import jax
import jax.numpy as jnp
from jax import lax
from jax.experimental import pallas as pl
from jax.experimental.pallas import tpu as pltpu
from jax.sharding import PartitionSpec as P

HEAD_DIM = 64
BLOCK = 512
REACH = 2
CHUNK = 128
EPS = 1e-05
NEG = -1e30
F32 = jnp.float32
BF16 = jnp.bfloat16
MESH = pl.DeviceIdType.MESH
VMEM = pl.BlockSpec(memory_space=pltpu.VMEM)
SMEM = pl.BlockSpec(memory_space=pltpu.SMEM)


def dot(left, right):
    return jnp.dot(left, right, preferred_element_type=F32)


def dot_nt(left, right):
    return lax.dot_general(left, right, (((1,), (1,)), ((), ())), preferred_element_type=F32)


def dot_tn(left, right):
    return lax.dot_general(left, right, (((0,), (0,)), ((), ())), preferred_element_type=F32)


def hat_of(rows):
    center = rows - jnp.mean(rows, axis=-1, keepdims=True)
    inv_std = lax.rsqrt(jnp.mean(center * center, axis=-1, keepdims=True) + EPS)
    return center * inv_std, inv_std


def norm_back(grad_rows, hat, inv_std, gain):
    grad_hat = grad_rows * gain
    inner = jnp.mean(grad_hat * hat, axis=-1, keepdims=True)
    grad_input = inv_std * (grad_hat - jnp.mean(grad_hat, axis=-1, keepdims=True) - hat * inner)
    gain_sum = jnp.sum(grad_rows * hat, axis=0, keepdims=True)
    shift_sum = jnp.sum(grad_rows, axis=0, keepdims=True)
    return grad_input, gain_sum, shift_sum


def remote(src, dst, send_sem, recv_sem, device):
    return pltpu.make_async_remote_copy(
        src_ref=src, dst_ref=dst, send_sem=send_sem, recv_sem=recv_sem, device_id=device, device_id_type=MESH
    )


class Place:
    def __init__(self, chips, rows):
        self.chips = chips
        self.piece = rows // (2 * chips)
        self.per_piece = self.piece // CHUNK
        self.chunks = chips * self.per_piece
        tp = lax.axis_index("tp")
        self.x = tp // 2
        self.core = lax.rem(tp, 2)
        self.mate = {"tp": self.x * 2 + 1 - self.core}

    def chip(self, ahead):
        return lax.rem(self.x + ahead, self.chips)

    def peer(self, ahead):
        return {"tp": self.chip(ahead) * 2 + self.core}

    def piece_row(self, chip, core):
        return pl.multiple_of((chip * 2 + core) * self.piece, CHUNK)

    def row(self, index, core):
        chip, part = divmod(index, self.per_piece)
        return pl.multiple_of((chip * 2 + core) * self.piece + part * CHUNK, CHUNK)

    def enter(self, seq_count=0):
        barrier = pltpu.get_barrier_semaphore()
        pl.semaphore_signal(barrier, inc=1, device_id=self.mate, device_id_type=MESH)
        for ahead in range(1, self.chips):
            pl.semaphore_signal(barrier, inc=1, device_id=self.peer(ahead), device_id_type=MESH)
        count = self.chips
        if seq_count:
            place = lax.axis_index("seq")
            has_prev, has_next = place > 0, place < seq_count - 1

            @pl.when(has_prev)
            def _():
                pl.semaphore_signal(barrier, inc=1, device_id={"seq": place - 1}, device_id_type=MESH)

            @pl.when(has_next)
            def _():
                pl.semaphore_signal(barrier, inc=1, device_id={"seq": place + 1}, device_id_type=MESH)

            count = count + jnp.where(has_prev, 1, 0) + jnp.where(has_next, 1, 0)
        pl.semaphore_wait(barrier, count)


def sum_scratch(chips, rows, width):
    chunks = rows // 2 // CHUNK
    dma = pltpu.SemaphoreType.DMA
    return [
        pltpu.VMEM((chunks, CHUNK, width), BF16),
        pltpu.VMEM((chunks, CHUNK, width), BF16),
        pltpu.VMEM((chunks, CHUNK, width), F32),
        pltpu.VMEM((chunks, CHUNK, width), BF16),
        pltpu.VMEM((chips - 1, chunks, CHUNK, width), BF16),
        dma((chunks,)),
        dma((chunks,)),
        dma((chips - 1, chunks)),
        dma((chips - 1, chunks)),
    ]


SUM_REFS = 9


class Sums:
    def __init__(self, place, refs):
        self.place = place
        (self.out, self.mate, self.own, self.low, self.far, self.s1, self.r1, self.s2, self.r2) = refs

    def core_copy(self, slot):
        return remote(self.out.at[slot], self.mate.at[slot], self.s1.at[slot], self.r1.at[slot], self.place.mate)

    def far_copy(self, ahead, slot):
        return remote(
            self.low.at[slot],
            self.far.at[ahead - 1, slot],
            self.s2.at[ahead - 1, slot],
            self.r2.at[ahead - 1, slot],
            self.place.peer(ahead),
        )

    def give(self, slot, rows):
        self.out[slot] = rows.astype(BF16)
        self.core_copy(slot).start()

    def keep(self, slot, rows):
        self.own[slot] = rows

    def join(self, slot):
        self.core_copy(slot).wait_recv()
        self.own[slot] = self.own[slot] + self.mate[slot].astype(F32)

    def send(self, slot, aheads):
        self.low[slot] = self.own[slot].astype(BF16)
        for ahead in aheads:
            self.far_copy(ahead, slot).start()

    def total(self, slot):
        rows = self.own[slot]
        for ahead in range(1, self.place.chips):
            self.far_copy(ahead, slot).wait_recv()
            rows = rows + self.far[ahead - 1, slot].astype(F32)
        return rows


def all_sums(sums, piece_terms, after=None):
    place = sums.place
    n = place.per_piece
    for chip in range(place.chips):
        rows = piece_terms(place.piece_row(chip, 1 - place.core))
        for part in range(n):
            sums.give(chip * n + part, rows[part * CHUNK : (part + 1) * CHUNK])
        rows = piece_terms(place.piece_row(chip, place.core))
        for part in range(n):
            sums.keep(chip * n + part, rows[part * CHUNK : (part + 1) * CHUNK])
        for part in range(n):
            sums.join(chip * n + part)
            sums.send(chip * n + part, range(1, place.chips))


def all_sums_end(sums):
    place = sums.place
    for slot in range(place.chunks):
        sums.core_copy(slot).wait_send()
        for ahead in range(1, place.chips):
            sums.far_copy(ahead, slot).wait_send()


def own_sums(sums, piece_terms):
    place = sums.place
    n = place.per_piece
    for ahead in [*range(1, place.chips), 0]:
        chip = place.chip(ahead)
        rows = piece_terms(place.piece_row(chip, 1 - place.core))
        for part in range(n):
            sums.give(ahead * n + part, rows[part * CHUNK : (part + 1) * CHUNK])
        rows = piece_terms(place.piece_row(chip, place.core))
        for part in range(n):
            sums.keep(ahead * n + part, rows[part * CHUNK : (part + 1) * CHUNK])
        for part in range(n):
            sums.join(ahead * n + part)
            if ahead:
                sums.send(ahead * n + part, [ahead])


def own_total(sums, part):
    place = sums.place
    n = place.per_piece
    rows = sums.own[part]
    for ahead in range(1, place.chips):
        slot = ahead * n + part
        sums.far_copy(ahead, slot).wait_recv()
        rows = rows + sums.far[ahead - 1, slot].astype(F32)
    return rows


def own_sums_end(sums):
    place = sums.place
    n = place.per_piece
    for slot in range(place.chunks):
        sums.core_copy(slot).wait_send()
        if slot >= n:
            sums.far_copy(slot // n, slot).wait_send()


class Share:
    def __init__(self, place, ref, send_sems, recv_sems):
        self.place, self.ref, self.s, self.r = place, ref, send_sems, recv_sems

    def copy(self, slot):
        rows = pl.ds(self.place.row(slot, self.place.core), CHUNK)
        return remote(self.ref.at[rows], self.ref.at[rows], self.s.at[slot], self.r.at[slot], self.place.mate)

    def put(self, slot, rows):
        self.ref[pl.ds(self.place.row(slot, self.place.core), CHUNK), :] = rows
        self.copy(slot).start()

    def end(self):
        for slot in range(self.place.chunks):
            self.copy(slot).wait()


def half_rows(slot):
    return pl.ds(slot * CHUNK, CHUNK)


def head_masks():
    lane = lax.broadcasted_iota(jnp.int32, (1, 2 * HEAD_DIM), 1)
    first = (lane < HEAD_DIM).astype(F32)
    return first, 1.0 - first


def causal_tile(keys_first):
    rows = lax.broadcasted_iota(jnp.int32, (BLOCK, BLOCK), 0)
    columns = lax.broadcasted_iota(jnp.int32, (BLOCK, BLOCK), 1)
    allowed = rows <= columns if keys_first else columns <= rows
    return jnp.where(allowed, 0.0, NEG)


def attend(q_ref, row0, key_tiles, value_tiles, biases, mixed_ref, o_ref, lse_ref):
    pairs = q_ref.shape[1] // (2 * HEAD_DIM)
    masks = head_masks()
    rows = pl.ds(row0, BLOCK)
    lane = lax.broadcasted_iota(jnp.int32, (BLOCK, 128), 1)
    lse_block = jnp.zeros((BLOCK, 128), F32)
    for pair in range(pairs):
        lanes = pl.ds(pair * 2 * HEAD_DIM, 2 * HEAD_DIM)
        queries = q_ref[rows, lanes]
        pair_out = jnp.zeros((BLOCK, 2 * HEAD_DIM), F32)
        for head in range(2):
            head_queries = queries * masks[head].astype(BF16)
            scores = [
                dot_nt(head_queries, key_tiles(tile, lanes)) + bias() for tile, bias in enumerate(biases)
            ]
            top = functools.reduce(jnp.maximum, [jnp.max(s, axis=-1, keepdims=True) for s in scores])
            total, out = 0.0, 0.0
            for tile, s in enumerate(scores):
                weights = jnp.exp(s - top)
                total = total + jnp.sum(weights, axis=-1, keepdims=True)
                out = out + dot(weights.astype(BF16), value_tiles(tile, lanes))
            pair_out = pair_out + out * masks[head] / total
            lse_block = jnp.where(lane == pair * 2 + head, top + jnp.log(total), lse_block)
        o_ref[rows, lanes] = pair_out
        mixed_ref[rows, lanes] = pair_out.astype(BF16)
    lse_ref[:, rows] = jnp.transpose(lse_block)[:8]


def dots_out(grad_ref, o_ref, row0):
    pairs = grad_ref.shape[1] // (2 * HEAD_DIM)
    masks = head_masks()
    rows = pl.ds(row0, BLOCK)
    lane = lax.broadcasted_iota(jnp.int32, (BLOCK, 128), 1)
    block = jnp.zeros((BLOCK, 128), F32)
    for pair in range(pairs):
        lanes = pl.ds(pair * 2 * HEAD_DIM, 2 * HEAD_DIM)
        product = grad_ref[rows, lanes].astype(F32) * o_ref[rows, lanes]
        for head in range(2):
            value = jnp.sum(product * masks[head], axis=-1, keepdims=True)
            block = jnp.where(lane == pair * 2 + head, value, block)
    return jnp.transpose(block)[:8]


def attend_back(q_ref, grad_ref, lse_ref, dots_ref, row0, pair, keys, values, bias):
    masks = head_masks()
    lanes = pl.ds(pair * 2 * HEAD_DIM, 2 * HEAD_DIM)
    rows = pl.ds(row0, BLOCK)
    queries, grads = q_ref[rows, lanes], grad_ref[rows, lanes]
    dq = dk = dv = 0.0
    for head in range(2):
        mask = masks[head].astype(BF16)
        head_queries, head_grads, head_keys = queries * mask, grads * mask, keys * mask
        index = pair * 2 + head
        scores = dot_nt(keys, head_queries) + bias()
        weights = jnp.exp(scores - lse_ref[index : index + 1, rows])
        grad_weights = dot_nt(values, head_grads)
        grad_scores = (weights * (grad_weights - dots_ref[index : index + 1, rows])).astype(BF16)
        dv = dv + dot(weights.astype(BF16), head_grads)
        dk = dk + dot(grad_scores, head_queries)
        dq = dq + dot_tn(grad_scores, head_keys)
    return dq * HEAD_DIM ** (-0.5), dk, dv


def call(body, name, out_shapes, in_specs, scratch, collective_id, flops, args):
    return pl.pallas_call(
        body,
        name=name,
        out_shape=out_shapes,
        in_specs=in_specs,
        out_specs=[VMEM] * len(out_shapes),
        scratch_shapes=scratch,
        cost_estimate=pl.CostEstimate(flops=flops, bytes_accessed=16 << 20, transcendentals=0),
        compiler_params=pltpu.CompilerParams(
            collective_id=collective_id, has_side_effects=True, vmem_limit_bytes=56 << 20
        ),
    )(*args)


def shape(*dims, dtype=BF16):
    return jax.ShapeDtypeStruct(dims, dtype)


def open_body(chips, x_ref, gain, shift, wq, wk, wv, n_ref, half_ref, q_ref, k_ref, v_ref, s1, r1, s2, r2):
    place = Place(chips, n_ref.shape[0])
    place.enter()
    n, piece = place.per_piece, place.piece

    def far(ahead, part):
        dst = half_ref.at[pl.ds(pl.multiple_of(place.x * piece + part * CHUNK, CHUNK), CHUNK)]
        return remote(
            x_ref.at[pl.ds(part * CHUNK, CHUNK)],
            dst,
            s2.at[ahead - 1, part],
            r2.at[ahead - 1, part],
            place.peer(ahead),
        )

    for part in range(n):
        for ahead in range(1, chips):
            far(ahead, part).start()
    half_ref[pl.ds(pl.multiple_of(place.x * piece, CHUNK), piece), :] = x_ref[...]

    def near(ahead, part):
        chip = lax.rem(place.x + chips - ahead, chips)
        row = pl.multiple_of((chip * 2 + place.core) * piece + part * CHUNK, CHUNK)
        rows = pl.ds(row, CHUNK)
        return remote(n_ref.at[rows], n_ref.at[rows], s1.at[ahead, part], r1.at[ahead, part], place.mate)

    def normed(ahead, part):
        chip = lax.rem(place.x + chips - ahead, chips)
        rows = half_ref[pl.ds(pl.multiple_of(chip * piece + part * CHUNK, CHUNK), CHUNK), :].astype(F32)
        hat, _ = hat_of(rows)
        row = pl.multiple_of((chip * 2 + place.core) * piece + part * CHUNK, CHUNK)
        n_ref[pl.ds(row, CHUNK), :] = (hat * gain[...] + shift[...]).astype(BF16)
        near(ahead, part).start()

    def project(ahead):
        chip = lax.rem(place.x + chips - ahead, chips)
        rows = pl.ds(pl.multiple_of(chip * 2 * piece, CHUNK), 2 * piece)
        rows_in = n_ref[rows, :]
        q_ref[rows, :] = (dot(rows_in, wq[...]).astype(BF16).astype(F32) * HEAD_DIM ** (-0.5)).astype(BF16)
        k_ref[rows, :] = dot(rows_in, wk[...]).astype(BF16)
        v_ref[rows, :] = dot(rows_in, wv[...]).astype(BF16)

    for ahead in range(chips):
        for part in range(n):
            if ahead:
                far(ahead, part).wait_recv()
            normed(ahead, part)
        for part in range(n):
            near(ahead, part).wait_recv()
        project(ahead)
    for part in range(n):
        for ahead in range(1, chips):
            far(ahead, part).wait_send()
        for ahead in range(chips):
            near(ahead, part).wait_send()


def opening(chips, tokens, x, gain, shift, wq, wk, wv):
    width, dim = wq.shape[1], x.shape[1]
    n = tokens // (2 * chips) // CHUNK
    dma = pltpu.SemaphoreType.DMA
    return call(
        functools.partial(open_body, chips),
        "opening",
        [shape(tokens, dim), shape(tokens // 2, dim)] + [shape(tokens, width)] * 3,
        [VMEM] * 6,
        [dma((chips, n)), dma((chips, n)), dma((chips - 1, n)), dma((chips - 1, n))],
        0,
        6 * tokens * dim * width,
        (x, gain, shift, wq, wk, wv),
    )


def self_body(
    chips,
    seqs,
    flags,
    q_ref,
    k_ref,
    v_ref,
    og_own,
    half_ref,
    wo,
    gain,
    shift,
    kext_ref,
    vext_ref,
    mixed_ref,
    o_ref,
    lse_ref,
    res_ref,
    n_ref,
    og_ref,
    *scratch,
):
    sum_refs, (causal, ks, kr, s1, r1, gs1, gr1, gs2, gr2) = scratch[:SUM_REFS], scratch[SUM_REFS:]
    tokens = q_ref.shape[0]
    place = Place(chips, tokens)
    seq = lax.axis_index("seq")
    has_prev, has_next = seq > 0, seq < seqs - 1
    place.enter(seqs)
    blocks = REACH

    def shift_copy(which, part):
        src, dst = ((k_ref, kext_ref), (v_ref, vext_ref))[which]
        rows = pl.ds(part * BLOCK, BLOCK)
        return remote(src.at[rows], dst.at[rows], ks.at[which, part], kr.at[which, part], {"seq": seq + 1})

    @pl.when(has_next)
    def _():
        for part in range(blocks):
            for which in range(2):
                shift_copy(which, part).start()

    @pl.when(seq == 0)
    def _():
        kext_ref[:tokens, :] = jnp.zeros((tokens, kext_ref.shape[1]), BF16)
        vext_ref[:tokens, :] = jnp.zeros((tokens, kext_ref.shape[1]), BF16)

    kext_ref[tokens:, :] = k_ref[...]
    vext_ref[tokens:, :] = v_ref[...]

    n, piece = place.per_piece, place.piece

    def og_far(ahead, part):
        rows = pl.ds(pl.multiple_of(place.piece_row(place.x, place.core) + part * CHUNK, CHUNK), CHUNK)
        return remote(
            og_own.at[pl.ds(part * CHUNK, CHUNK)],
            og_ref.at[rows],
            gs2.at[ahead - 1, part],
            gr2.at[ahead - 1, part],
            place.peer(ahead),
        )

    def og_near(ahead, part):
        chip = lax.rem(place.x + chips - ahead, chips)
        rows = pl.ds(pl.multiple_of(place.piece_row(chip, place.core) + part * CHUNK, CHUNK), CHUNK)
        return remote(og_ref.at[rows], og_ref.at[rows], gs1.at[ahead, part], gr1.at[ahead, part], place.mate)

    for part in range(n):
        for ahead in range(1, chips):
            og_far(ahead, part).start()
    og_ref[pl.ds(place.piece_row(place.x, place.core), piece), :] = og_own[...]
    for part in range(n):
        og_near(0, part).start()
    causal[...] = causal_tile(False)

    @pl.when(has_prev)
    def _():
        for part in range(blocks):
            for which in range(2):
                shift_copy(which, part).wait_recv()

    sums = Sums(place, sum_refs)
    for block in range(tokens // BLOCK):
        biases = [functools.partial(lambda index: flags[index], block * 3 + tile) for tile in range(REACH)]
        attend(
            q_ref,
            block * BLOCK,
            lambda tile, lanes, block=block: kext_ref[pl.ds((block + tile) * BLOCK, BLOCK), lanes],
            lambda tile, lanes, block=block: vext_ref[pl.ds((block + tile) * BLOCK, BLOCK), lanes],
            biases + [lambda: causal[...]],
            mixed_ref,
            o_ref,
            lse_ref,
        )
    all_sums(sums, lambda row: dot(mixed_ref[pl.ds(row, piece), :], wo[...]))

    for ahead in range(1, chips):
        for part in range(n):
            og_far(ahead, part).wait_recv()
            og_near(ahead, part).start()

    share = Share(place, n_ref, s1, r1)
    for slot in range(place.chunks):
        rows = half_ref[half_rows(slot), :].astype(F32) + sums.total(slot)
        res_ref[half_rows(slot), :] = rows
        hat, _ = hat_of(rows)
        share.put(slot, (hat * gain[...] + shift[...]).astype(BF16))
    share.end()
    all_sums_end(sums)
    for part in range(n):
        for ahead in range(1, chips):
            og_far(ahead, part).wait_send()
        for ahead in range(chips):
            og_near(ahead, part).wait()

    @pl.when(has_next)
    def _():
        for part in range(blocks):
            for which in range(2):
                shift_copy(which, part).wait_send()


def self_forward(chips, seqs, flags, q, k, v, out_grad, half, wo, gain, shift):
    tokens, width = q.shape
    dim = wo.shape[1]
    chunks = tokens // 2 // CHUNK
    n = tokens // (2 * chips) // CHUNK
    dma = pltpu.SemaphoreType.DMA
    return call(
        functools.partial(self_body, chips, seqs),
        "self_forward",
        [
            shape(2 * tokens, width),
            shape(2 * tokens, width),
            shape(tokens, width),
            shape(tokens, width, dtype=F32),
            shape(8, tokens, dtype=F32),
            shape(tokens // 2, dim, dtype=F32),
            shape(tokens, dim),
            shape(tokens, dim),
        ],
        [SMEM] + [VMEM] * 8,
        sum_scratch(chips, tokens, dim)
        + [
            pltpu.VMEM((BLOCK, BLOCK), F32),
            dma((2, REACH)),
            dma((2, REACH)),
            dma((chunks,)),
            dma((chunks,)),
            dma((chips, n)),
            dma((chips, n)),
            dma((chips - 1, n)),
            dma((chips - 1, n)),
        ],
        1,
        8 * tokens * 3 * BLOCK * width,
        (flags, q, k, v, out_grad, half, wo, gain, shift),
    )


def cross_body(
    chips,
    n2_ref,
    wq,
    keys,
    values,
    bias,
    wo,
    res_in,
    gain,
    shift,
    q_ref,
    mixed_ref,
    o_ref,
    lse_ref,
    res_ref,
    n_ref,
    *scratch,
):
    sum_refs, (s1, r1) = scratch[:SUM_REFS], scratch[SUM_REFS:]
    tokens = n2_ref.shape[0]
    place = Place(chips, tokens)
    place.enter()
    piece = place.piece
    for block in range(tokens // BLOCK):
        rows = pl.ds(block * BLOCK, BLOCK)
        q_ref[rows, :] = (
            dot(n2_ref[rows, :], wq[...]).astype(BF16).astype(F32) * HEAD_DIM ** (-0.5)
        ).astype(BF16)
        attend(
            q_ref,
            block * BLOCK,
            lambda tile, lanes, block=block: keys[block, :, lanes],
            lambda tile, lanes, block=block: values[block, :, lanes],
            [lambda block=block: bias[block]],
            mixed_ref,
            o_ref,
            lse_ref,
        )
    sums = Sums(place, sum_refs)
    all_sums(sums, lambda row: dot(mixed_ref[pl.ds(row, piece), :], wo[...]))
    share = Share(place, n_ref, s1, r1)
    for slot in range(place.chunks):
        rows = res_in[half_rows(slot), :] + sums.total(slot)
        res_ref[half_rows(slot), :] = rows
        hat, _ = hat_of(rows)
        share.put(slot, (hat * gain[...] + shift[...]).astype(BF16))
    share.end()
    all_sums_end(sums)


def cross_forward(chips, n2, wq, keys, values, bias, wo, res, gain, shift):
    tokens, dim = n2.shape
    width = wq.shape[1]
    chunks = tokens // 2 // CHUNK
    dma = pltpu.SemaphoreType.DMA
    return call(
        functools.partial(cross_body, chips),
        "cross_forward",
        [
            shape(tokens, width),
            shape(tokens, width),
            shape(tokens, width, dtype=F32),
            shape(8, tokens, dtype=F32),
            shape(tokens // 2, dim, dtype=F32),
            shape(tokens, dim),
        ],
        [VMEM] * 9,
        sum_scratch(chips, tokens, dim) + [dma((chunks,)), dma((chunks,))],
        2,
        4 * tokens * dim * width,
        (n2, wq, keys, values, bias, wo, res, gain, shift),
    )


def ffn_body(
    chips, n3_ref, og_ref, up, down, res_ref, gain, act_ref, gpre_ref, grad_ref, g_ref, norm_ref, *scratch
):
    sum_refs, (s1, r1) = scratch[:SUM_REFS], scratch[SUM_REFS:]
    tokens = n3_ref.shape[0]
    place = Place(chips, tokens)
    place.enter()
    piece = place.piece

    def term(row):
        rows = pl.ds(row, piece)
        pre = dot(n3_ref[rows, :], up[...])
        half_erf = 0.5 * lax.erf(pre * (0.5**0.5)) + 0.5
        act_ref[rows, :] = (pre * half_erf).astype(BF16)
        slope = half_erf + pre * jnp.exp(-0.5 * pre * pre) * (0.15915494309189535**0.5)
        grad_act = dot_nt(og_ref[rows, :], down[...])
        low = (grad_act * slope).astype(BF16)
        gpre_ref[rows, :] = low
        return dot_nt(low, up[...])

    sums = Sums(place, sum_refs)
    all_sums(sums, term)
    share = Share(place, g_ref, s1, r1)
    gain_sum = shift_sum = 0.0
    for slot in range(place.chunks):
        hat, inv_std = hat_of(res_ref[half_rows(slot), :])
        grad_in, more_gain, more_shift = norm_back(sums.total(slot), hat, inv_std, gain[...])
        gain_sum, shift_sum = gain_sum + more_gain, shift_sum + more_shift
        rows = og_ref[pl.ds(place.row(slot, place.core), CHUNK), :].astype(F32) + grad_in
        grad_ref[half_rows(slot), :] = rows
        share.put(slot, rows.astype(BF16))
    norm_ref[0:1, :] = gain_sum
    norm_ref[1:2, :] = shift_sum
    share.end()
    all_sums_end(sums)


def ffn(chips, n3, og, up, down, res, gain):
    tokens, dim = n3.shape
    hidden = up.shape[1]
    chunks = tokens // 2 // CHUNK
    dma = pltpu.SemaphoreType.DMA
    return call(
        functools.partial(ffn_body, chips),
        "ffn",
        [
            shape(tokens, hidden),
            shape(tokens, hidden),
            shape(tokens // 2, dim, dtype=F32),
            shape(tokens, dim),
            shape(2, dim, dtype=F32),
        ],
        [VMEM] * 6,
        sum_scratch(chips, tokens, dim) + [dma((chunks,)), dma((chunks,))],
        3,
        6 * tokens * dim * hidden,
        (n3, og, up, down, res, gain),
    )


def cross_back_body(
    chips,
    g_in,
    wo,
    q_ref,
    keys,
    values,
    bias,
    o_ref,
    lse_ref,
    wq,
    res_ref,
    grad_in_ref,
    gain,
    gq_ref,
    gk_ref,
    gv_ref,
    grad_ref,
    g_ref,
    norm_ref,
    *scratch,
):
    sum_refs, (dout, dots, s1, r1) = scratch[:SUM_REFS], scratch[SUM_REFS:]
    tokens = g_in.shape[0]
    place = Place(chips, tokens)
    place.enter()
    piece = place.piece
    pairs = q_ref.shape[1] // (2 * HEAD_DIM)
    for block in range(tokens // BLOCK):
        rows = pl.ds(block * BLOCK, BLOCK)
        dout[rows, :] = dot_nt(g_in[rows, :], wo[...]).astype(BF16)
        dots[:, rows] = dots_out(dout, o_ref, block * BLOCK)
        for pair in range(pairs):
            lanes = pl.ds(pair * 2 * HEAD_DIM, 2 * HEAD_DIM)
            dq, dk, dv = attend_back(
                q_ref,
                dout,
                lse_ref,
                dots,
                block * BLOCK,
                pair,
                keys[block, :, lanes],
                values[block, :, lanes],
                lambda block=block: bias[block],
            )
            gq_ref[rows, lanes] = dq.astype(BF16)
            gk_ref[block, :, lanes] = dk.astype(BF16)
            gv_ref[block, :, lanes] = dv.astype(BF16)
    sums = Sums(place, sum_refs)
    all_sums(sums, lambda row: dot_nt(gq_ref[pl.ds(row, piece), :], wq[...]))
    share = Share(place, g_ref, s1, r1)
    gain_sum = shift_sum = 0.0
    for slot in range(place.chunks):
        hat, inv_std = hat_of(res_ref[half_rows(slot), :])
        grad_in, more_gain, more_shift = norm_back(sums.total(slot), hat, inv_std, gain[...])
        gain_sum, shift_sum = gain_sum + more_gain, shift_sum + more_shift
        rows = grad_in_ref[half_rows(slot), :] + grad_in
        grad_ref[half_rows(slot), :] = rows
        share.put(slot, rows.astype(BF16))
    norm_ref[0:1, :] = gain_sum
    norm_ref[1:2, :] = shift_sum
    share.end()
    all_sums_end(sums)


def cross_back(chips, g_in, wo, q, keys, values, bias, o, lse, wq, res, grad_in, gain):
    tokens, dim = g_in.shape
    width = q.shape[1]
    chunks = tokens // 2 // CHUNK
    dma = pltpu.SemaphoreType.DMA
    return call(
        functools.partial(cross_back_body, chips),
        "cross_back",
        [
            shape(tokens, width),
            shape(*keys.shape),
            shape(*keys.shape),
            shape(tokens // 2, dim, dtype=F32),
            shape(tokens, dim),
            shape(2, dim, dtype=F32),
        ],
        [VMEM] * 12,
        sum_scratch(chips, tokens, dim)
        + [pltpu.VMEM((tokens, width), BF16), pltpu.VMEM((8, tokens), F32), dma((chunks,)), dma((chunks,))],
        4,
        4 * tokens * dim * width,
        (g_in, wo, q, keys, values, bias, o, lse, wq, res, grad_in, gain),
    )


def close_body(
    chips,
    seqs,
    flags,
    g_in,
    wo,
    q_ref,
    kext_ref,
    vext_ref,
    o_ref,
    lse_ref,
    wq,
    wk,
    wv,
    half_ref,
    grad_in_ref,
    gain,
    act_ref,
    down,
    res_ref,
    gq_ref,
    gk_ref,
    gv_ref,
    grad_ref,
    out_ref,
    norm_ref,
    *scratch,
):
    hidden_refs, sum_refs = scratch[:SUM_REFS], scratch[SUM_REFS : 2 * SUM_REFS]
    (causal, dout, dots, dq_ref, dk_ref, dv_ref, kv_out, kv_in, ks, kr) = scratch[2 * SUM_REFS :]
    tokens, width = q_ref.shape
    place = Place(chips, tokens)
    seq = lax.axis_index("seq")
    has_prev, has_next = seq > 0, seq < seqs - 1
    place.enter(seqs)
    piece, n = place.piece, place.per_piece
    pairs = width // (2 * HEAD_DIM)

    hidden = Sums(place, hidden_refs)
    own_sums(hidden, lambda row: dot(act_ref[pl.ds(row, piece), :], down[...]))

    causal[...] = causal_tile(True)
    blocks = tokens // BLOCK
    for block in range(blocks):
        rows = pl.ds(block * BLOCK, BLOCK)
        dout[rows, :] = dot_nt(g_in[rows, :], wo[...]).astype(BF16)
        dots[:, rows] = dots_out(dout, o_ref, block * BLOCK)
    dq_ref[...] = jnp.zeros_like(dq_ref)
    dk_ref[...] = jnp.zeros_like(dk_ref)
    dv_ref[...] = jnp.zeros_like(dv_ref)

    def tile_back(block, tile):
        rows, key_rows = pl.ds(block * BLOCK, BLOCK), pl.ds((block + tile) * BLOCK, BLOCK)
        bias = (lambda: causal[...]) if tile == REACH else (lambda: flags[block * 3 + tile])
        for pair in range(pairs):
            lanes = pl.ds(pair * 2 * HEAD_DIM, 2 * HEAD_DIM)
            dq, dk, dv = attend_back(
                q_ref,
                dout,
                lse_ref,
                dots,
                block * BLOCK,
                pair,
                kext_ref[key_rows, lanes],
                vext_ref[key_rows, lanes],
                bias,
            )
            dq_ref[rows, lanes] = dq_ref[rows, lanes] + dq
            dk_ref[key_rows, lanes] = dk_ref[key_rows, lanes] + dk
            dv_ref[key_rows, lanes] = dv_ref[key_rows, lanes] + dv

    def shift_copy(which, part):
        rows = pl.ds(part * BLOCK, BLOCK)
        return remote(
            kv_out.at[which, rows],
            kv_in.at[which, rows],
            ks.at[which, part],
            kr.at[which, part],
            {"seq": seq - 1},
        )

    tiles = [(block, tile) for block in range(blocks) for tile in range(REACH + 1)]
    earlier = [pair for pair in tiles if sum(pair) < blocks]
    for block, tile in earlier:
        tile_back(block, tile)
    kv_out[0] = dk_ref[:tokens, :].astype(BF16)
    kv_out[1] = dv_ref[:tokens, :].astype(BF16)

    @pl.when(has_prev)
    def _():
        for part in range(blocks):
            for which in range(2):
                shift_copy(which, part).start()

    @pl.when(jnp.logical_not(has_next))
    def _():
        kv_in[...] = jnp.zeros_like(kv_in)

    for block, tile in tiles:
        if (block, tile) not in earlier:
            tile_back(block, tile)

    @pl.when(has_next)
    def _():
        for part in range(blocks):
            for which in range(2):
                shift_copy(which, part).wait_recv()

    gq_ref[...] = dq_ref[...].astype(BF16)
    gk_ref[...] = (dk_ref[tokens:, :] + kv_in[0].astype(F32)).astype(BF16)
    gv_ref[...] = (dv_ref[tokens:, :] + kv_in[1].astype(F32)).astype(BF16)

    def term(row):
        rows = pl.ds(row, piece)
        return (
            dot_nt(gq_ref[rows, :], wq[...]) + dot_nt(gk_ref[rows, :], wk[...]) + dot_nt(gv_ref[rows, :], wv[...])
        )

    sums = Sums(place, sum_refs)
    own_sums(sums, term)
    for part in range(n):
        rows = pl.ds(part * CHUNK, CHUNK)
        mine = pl.ds(pl.multiple_of(place.x * piece + part * CHUNK, CHUNK), CHUNK)
        out_ref[rows, :] = (res_ref[mine, :] + own_total(hidden, part)).astype(BF16)
    own_sums_end(hidden)
    gain_sum = shift_sum = 0.0
    for part in range(n):
        rows = pl.ds(part * CHUNK, CHUNK)
        mine = pl.ds(pl.multiple_of(place.x * piece + part * CHUNK, CHUNK), CHUNK)
        hat, inv_std = hat_of(half_ref[mine, :].astype(F32))
        grad_in, more_gain, more_shift = norm_back(own_total(sums, part), hat, inv_std, gain[...])
        gain_sum, shift_sum = gain_sum + more_gain, shift_sum + more_shift
        grad_ref[rows, :] = grad_in_ref[mine, :] + grad_in
    norm_ref[0:1, :] = gain_sum
    norm_ref[1:2, :] = shift_sum
    own_sums_end(sums)

    @pl.when(has_prev)
    def _():
        for part in range(blocks):
            for which in range(2):
                shift_copy(which, part).wait_send()


def closing(chips, seqs, flags, g_in, wo, q, kext, vext, o, lse, wq, wk, wv, half, grad_in, gain, act, down, res):
    tokens, width = q.shape
    dim = wo.shape[1]
    dma = pltpu.SemaphoreType.DMA
    blocks = tokens // BLOCK
    return call(
        functools.partial(close_body, chips, seqs),
        "closing",
        [
            shape(tokens, width),
            shape(tokens, width),
            shape(tokens, width),
            shape(tokens // (2 * chips), dim, dtype=F32),
            shape(tokens // (2 * chips), dim),
            shape(2, dim, dtype=F32),
        ],
        [SMEM] + [VMEM] * 16,
        sum_scratch(chips, tokens, dim)
        + sum_scratch(chips, tokens, dim)
        + [
            pltpu.VMEM((BLOCK, BLOCK), F32),
            pltpu.VMEM((tokens, width), BF16),
            pltpu.VMEM((8, tokens), F32),
            pltpu.VMEM((tokens, width), F32),
            pltpu.VMEM((2 * tokens, width), F32),
            pltpu.VMEM((2 * tokens, width), F32),
            pltpu.VMEM((2, tokens, width), BF16),
            pltpu.VMEM((2, tokens, width), BF16),
            dma((2, blocks)),
            dma((2, blocks)),
        ],
        5,
        20 * tokens * 3 * BLOCK * width,
        (flags, g_in, wo, q, kext, vext, o, lse, wq, wk, wv, half, grad_in, gain, act, down, res),
    )


def on_device(
    hidden_in,
    memory,
    page_ids,
    token_offsets,
    memory_mask,
    attn_query,
    attn_key,
    attn_value,
    attn_output,
    cross_query,
    cross_key,
    cross_value,
    cross_output,
    ffn_up,
    ffn_down,
    self_gain,
    self_shift,
    cross_gain,
    cross_shift,
    ffn_gain,
    ffn_shift,
    out_grad,
):
    tps, seqs = lax.axis_size("tp"), lax.axis_size("seq")
    chips = tps // 2
    tokens, dim = page_ids.shape[0], hidden_in.shape[1]
    width, hidden = attn_query.shape[1], ffn_up.shape[1]
    blocks = tokens // BLOCK
    core = lax.rem(lax.axis_index("tp"), 2)
    row = lambda vector: vector.reshape(1, -1)

    mem_rows = memory.shape[1]
    mem_pad = -(-mem_rows // 128) * 128
    half_dim = dim // 2
    mem_half = lax.dynamic_slice_in_dim(memory, core * half_dim, half_dim, axis=2)
    all_half = lax.all_gather(mem_half, "seq", axis=0, tiled=True)
    all_mask = lax.all_gather(memory_mask, "seq", axis=0, tiled=True)
    block_pages = page_ids.reshape(blocks, BLOCK)[:, 0]
    picked = jnp.stack(
        [lax.dynamic_index_in_dim(all_half, block_pages[b], 0, keepdims=False) for b in range(blocks)]
    )
    picked_mask = jnp.stack(
        [lax.dynamic_index_in_dim(all_mask, block_pages[b], 0, keepdims=False) for b in range(blocks)]
    )
    picked = jnp.pad(picked, ((0, 0), (0, mem_pad - mem_rows), (0, 0)))
    other = lax.ppermute(picked, "tp", [(i, i + 1 - 2 * (i % 2)) for i in range(tps)])
    low = jnp.where(core == 0, picked, other)
    high = jnp.where(core == 0, other, picked)
    mem = jnp.concatenate([low, high], axis=2).reshape(blocks * mem_pad, dim)
    mem_keys = dot(mem, cross_key).astype(BF16).reshape(blocks, mem_pad, width)
    mem_values = dot(mem, cross_value).astype(BF16).reshape(blocks, mem_pad, width)
    mem_bias = jnp.pad(jnp.where(picked_mask > 0, 0.0, NEG), ((0, 0), (0, mem_pad - mem_rows)), constant_values=NEG)

    order = token_offsets.reshape(blocks, BLOCK)[:, :1] // BLOCK
    reach = jnp.arange(REACH, -1, -1, dtype=jnp.int32)
    flags = jnp.where(order >= reach[None, :], 0.0, NEG).astype(F32).reshape(-1)

    n1, half, q1, k1, v1 = opening(
        chips, tokens, hidden_in, row(self_gain), row(self_shift), attn_query, attn_key, attn_value
    )
    kext, vext, mixed1, o1, lse1, res1, n2, og = self_forward(
        chips, seqs, flags, q1, k1, v1, out_grad, half, attn_output, row(cross_gain), row(cross_shift)
    )
    q2, mixed2, o2, lse2, res2, n3 = cross_forward(
        chips,
        n2,
        cross_query,
        mem_keys,
        mem_values,
        mem_bias[:, None, :],
        cross_output,
        res1,
        row(ffn_gain),
        row(ffn_shift),
    )
    act, gpre, grad2, g2, norm3 = ffn(chips, n3, og, ffn_up, ffn_down, res2, row(ffn_gain))

    def reduced(parts):
        whole = jnp.concatenate([part.astype(BF16) for part in parts], axis=1)
        whole = lax.psum_scatter(whole, "seq", scatter_dimension=0, tiled=True).astype(F32)
        ends = [0]
        for part in parts:
            ends.append(ends[-1] + part.shape[1])
        return [whole[:, first:last] for first, last in zip(ends[:-1], ends[1:])]

    grad_up, grad_down = reduced([dot_tn(n3, gpre), dot_tn(og, act)])
    gq2, gk2, gv2, grad1, g1, norm2 = cross_back(
        chips,
        g2,
        cross_output,
        q2,
        mem_keys,
        mem_values,
        mem_bias[:, :, None],
        o2,
        lse2,
        cross_query,
        res1,
        grad2,
        row(cross_gain),
    )
    gk2, gv2 = gk2.reshape(blocks * mem_pad, width), gv2.reshape(blocks * mem_pad, width)
    grad_cq, grad_ck, grad_cv, grad_co = reduced(
        [dot_tn(n2, gq2), dot_tn(mem, gk2), dot_tn(mem, gv2), dot_tn(g2, mixed2)]
    )
    mem_part = (dot_nt(gk2, cross_key) + dot_nt(gv2, cross_value)).reshape(blocks, mem_pad, dim)[:, :mem_rows]
    mem_part = lax.psum_scatter(mem_part.astype(BF16), "tp", scatter_dimension=2, tiled=True)
    chosen = block_pages[None, :] == jnp.arange(all_half.shape[0], dtype=jnp.int32)[:, None]
    routed = sum(
        jnp.where(chosen[:, b, None, None], mem_part[b][None].astype(F32), 0.0) for b in range(blocks)
    ).astype(BF16)
    grad_memory = lax.psum_scatter(routed, "seq", scatter_dimension=0, tiled=True).astype(F32)

    gq1, gk1, gv1, grad_hidden, hidden_out, norm1 = closing(
        chips,
        seqs,
        flags,
        g1,
        attn_output,
        q1,
        kext,
        vext,
        o1,
        lse1,
        attn_query,
        attn_key,
        attn_value,
        half,
        grad1,
        row(self_gain),
        act,
        ffn_down,
        res2,
    )
    grad_q, grad_k, grad_v, grad_o = reduced([dot_tn(n1, gq1), dot_tn(n1, gk1), dot_tn(n1, gv1), dot_tn(g1, mixed1)])
    norms = jnp.concatenate([norm1, norm2 * (1.0 / chips), norm3 * (1.0 / chips)], axis=0)
    norms = lax.psum_scatter(norms, ("seq", "tp"), scatter_dimension=1, tiled=True)
    return (
        hidden_out,
        grad_hidden,
        grad_memory,
        grad_q,
        grad_k,
        grad_v,
        grad_o.T,
        grad_cq,
        grad_ck,
        grad_cv,
        grad_co.T,
        grad_up,
        grad_down.T,
        norms[0],
        norms[1],
        norms[2],
        norms[3],
        norms[4],
        norms[5],
    )


def solution(mesh):
    both = ("seq", "tp")
    in_specs = (
        P(both, None),
        P("seq", None, None),
        P("seq"),
        P("seq"),
        P("seq", None),
        P(None, "tp"),
        P(None, "tp"),
        P(None, "tp"),
        P("tp", None),
        P(None, "tp"),
        P(None, "tp"),
        P(None, "tp"),
        P("tp", None),
        P(None, "tp"),
        P("tp", None),
        P(),
        P(),
        P(),
        P(),
        P(),
        P(),
        P(both, None),
    )
    out_specs = (
        P(both, None),
        P(both, None),
        P("seq", None, "tp"),
        P("seq", "tp"),
        P("seq", "tp"),
        P("seq", "tp"),
        P("tp", "seq"),
        P("seq", "tp"),
        P("seq", "tp"),
        P("seq", "tp"),
        P("tp", "seq"),
        P("seq", "tp"),
        P("tp", "seq"),
        P(both),
        P(both),
        P(both),
        P(both),
        P(both),
        P(both),
    )
    return jax.shard_map(on_device, mesh=mesh, in_specs=in_specs, out_specs=out_specs, check_vma=False)
```

```python
import functools

import jax
import jax.numpy as jnp
from jax import lax
from jax.experimental import pallas as pl
from jax.experimental.pallas import tpu as pltpu
from jax.sharding import PartitionSpec as P

HEAD_DIM = 64
PAIR = 2 * HEAD_DIM
BLOCK = 512
REACH = 2
CHUNK = 128
EPS = 1e-05
NEG = -1e30
F32 = jnp.float32
BF16 = jnp.bfloat16
MESH = pl.DeviceIdType.MESH
VMEM = pl.BlockSpec(memory_space=pltpu.VMEM)
SMEM = pl.BlockSpec(memory_space=pltpu.SMEM)


def dot(left, right):
    return jnp.dot(left, right, preferred_element_type=F32)


def dot_nt(left, right):
    return lax.dot_general(left, right, (((1,), (1,)), ((), ())), preferred_element_type=F32)


def dot_tn(left, right):
    return lax.dot_general(left, right, (((0,), (0,)), ((), ())), preferred_element_type=F32)


def hat_of(rows):
    center = rows - jnp.mean(rows, axis=-1, keepdims=True)
    inv_std = lax.rsqrt(jnp.mean(center * center, axis=-1, keepdims=True) + EPS)
    return center * inv_std, inv_std


def norm_back(grad_rows, hat, inv_std, gain):
    grad_hat = grad_rows * gain
    inner = jnp.mean(grad_hat * hat, axis=-1, keepdims=True)
    grad_input = inv_std * (grad_hat - jnp.mean(grad_hat, axis=-1, keepdims=True) - hat * inner)
    gain_sum = jnp.sum(grad_rows * hat, axis=0, keepdims=True)
    shift_sum = jnp.sum(grad_rows, axis=0, keepdims=True)
    return grad_input, gain_sum, shift_sum


def remote(src, dst, send_sem, recv_sem, device):
    return pltpu.make_async_remote_copy(
        src_ref=src, dst_ref=dst, send_sem=send_sem, recv_sem=recv_sem, device_id=device, device_id_type=MESH
    )


class Late:
    def __init__(self, hbm, ref, sem, out):
        self.hbm, self.ref, self.sem, self.out, self.started, self.waited = hbm, ref, sem, out, False, False

    def copy(self):
        ends = (self.ref, self.hbm) if self.out else (self.hbm, self.ref)
        return pltpu.make_async_copy(*ends, self.sem)

    def start(self):
        self.copy().start()
        self.started = True

    def wait(self):
        if self.started and not self.waited:
            self.copy().wait()
            self.waited = True
        return self.ref


class Refs:
    pass


def call(body, name, ins, outs, scratch, collective_id, flops):
    dma = pltpu.SemaphoreType.DMA
    specs = {"vmem": VMEM, "smem": SMEM, "hbm": pl.BlockSpec(memory_space=pltpu.HBM)}
    specs["late"] = specs["hbm"]
    late_in = [key for key, (_, mode) in ins.items() if mode == "late"]
    late_out = [key for key, (_, _, mode) in outs.items() if mode == "late"]
    places = [pltpu.VMEM(ins[key][0].shape, ins[key][0].dtype) for key in late_in]
    places += [pltpu.VMEM(outs[key][0], outs[key][1]) for key in late_out]
    lates = len(places)

    def kernel(*refs):
        r = Refs()
        count = len(ins) + len(outs)
        for key, ref in zip([*ins, *outs], refs[:count]):
            setattr(r, key, ref)
        for key, ref in zip(scratch, refs[count : count + len(scratch)]):
            setattr(r, key, ref)
        rest = refs[count + len(scratch) :]
        all_late = []
        for index, key in enumerate(late_in + late_out):
            late = Late(getattr(r, key), rest[index], rest[-1].at[index], index >= len(late_in))
            setattr(r, key, late)
            all_late.append(late)
            if not late.out:
                late.start()
        body(r)
        for late in all_late:
            late.wait()

    result = pl.pallas_call(
        kernel,
        name=name,
        out_shape=[jax.ShapeDtypeStruct(dims, dtype) for dims, dtype, _ in outs.values()],
        in_specs=[specs[mode] for _, mode in ins.values()],
        out_specs=[specs[mode] for _, _, mode in outs.values()],
        scratch_shapes=[*scratch.values(), *places] + ([dma((lates,))] if lates else []),
        cost_estimate=pl.CostEstimate(flops=flops, bytes_accessed=16 << 20, transcendentals=0),
        compiler_params=pltpu.CompilerParams(
            collective_id=collective_id, has_side_effects=True, vmem_limit_bytes=62 << 20
        ),
    )(*[array for array, _ in ins.values()])
    out = Refs()
    for key, value in zip(outs, result):
        setattr(out, key, value)
    return out


def loop(count, step):
    lax.fori_loop(0, count, lambda index, carry: (step(index), carry)[1], 0)


class Place:
    def __init__(self, chips, seqs, rows):
        self.chips, self.seqs = chips, seqs
        self.piece = rows // (2 * chips)
        self.per_piece = self.piece // CHUNK
        self.chunks = chips * self.per_piece
        self.tp = lax.axis_index("tp")
        self.seq = lax.axis_index("seq")
        self.x = self.tp // 2
        self.core = lax.rem(self.tp, 2)
        self.mate = {"tp": self.x * 2 + 1 - self.core}
        self.has_prev, self.has_next = self.seq > 0, self.seq < seqs - 1

    def chip(self, ahead):
        return lax.rem(self.x + ahead, self.chips)

    def peer(self, ahead):
        return {"tp": self.chip(ahead) * 2 + self.core}

    def shard(self, ahead):
        return lax.rem(self.seq + ahead, self.seqs)

    def piece_row(self, chip, core):
        return pl.multiple_of((chip * 2 + core) * self.piece, CHUNK)

    def row(self, slot, core):
        chip, part = slot // self.per_piece, lax.rem(slot, self.per_piece)
        return pl.multiple_of((chip * 2 + core) * self.piece + part * CHUNK, CHUNK)

    def enter(self, seq="", all_tp=False):
        barrier = pltpu.get_barrier_semaphore()

        def greet(device):
            pl.semaphore_signal(barrier, inc=1, device_id=device, device_id_type=MESH)

        count = self.chips
        if all_tp:
            count = 2 * self.chips - 1
            for ahead in range(1, 2 * self.chips):
                greet({"tp": lax.rem(self.tp + ahead, 2 * self.chips)})
        else:
            greet(self.mate)
            for ahead in range(1, self.chips):
                greet(self.peer(ahead))
        if seq == "all":
            for ahead in range(1, self.seqs):
                greet({"seq": self.shard(ahead)})
            count = count + self.seqs - 1
        if seq == "near":
            pl.when(self.has_prev)(lambda: greet({"seq": self.seq - 1}))
            pl.when(self.has_next)(lambda: greet({"seq": self.seq + 1}))
            count = count + jnp.where(self.has_prev, 1, 0) + jnp.where(self.has_next, 1, 0)
        pl.semaphore_wait(barrier, count)


def sum_scratch(chips, rows, width, name="sums_", stages=1):
    chunks = rows // 2 // CHUNK
    dma = pltpu.SemaphoreType.DMA
    specs = [
        pltpu.VMEM((chunks, CHUNK, width), BF16),
        pltpu.VMEM((chunks, CHUNK, width), BF16),
        pltpu.VMEM((chunks, CHUNK, width), F32),
        dma((chunks,)),
        dma((chunks,)),
        pltpu.VMEM((stages, chips - 1, chunks, CHUNK, width), BF16),
        dma((stages, chips - 1, chunks)),
        dma((stages, chips - 1, chunks)),
    ]
    return {name + str(index): spec for index, spec in enumerate(specs)}


class Sums:
    def __init__(self, place, r, name="sums_", stage=0):
        self.place, self.stage = place, stage
        (self.out, self.mate, self.own, self.s1, self.r1, self.far, self.s2, self.r2) = [
            getattr(r, name + str(index)) for index in range(8)
        ]
        self.low = self.mate

    def core_copy(self, slot):
        return remote(self.out.at[slot], self.mate.at[slot], self.s1.at[slot], self.r1.at[slot], self.place.mate)

    def far_copy(self, ahead, slot):
        at = (self.stage, ahead - 1, slot)
        return remote(self.low.at[slot], self.far.at[at], self.s2.at[at], self.r2.at[at], self.place.peer(ahead))

    def near(self, slot, who, rows):
        n = self.place.per_piece

        @pl.when(who == 0)
        def _():
            for part in range(n):
                self.out[slot + part] = rows[part * CHUNK : (part + 1) * CHUNK].astype(BF16)
                self.core_copy(slot + part).start()

        @pl.when(who == 1)
        def _():
            for part in range(n):
                self.core_copy(slot + part).wait_recv()
                self.own[slot + part] = rows[part * CHUNK : (part + 1) * CHUNK] + self.mate[slot + part].astype(F32)

    def all_pieces(self, first, count, term):
        place = self.place
        n = place.per_piece

        def step(index):
            chip, who = first + index // 2, lax.rem(index, 2)
            core = jnp.where(who == 0, 1 - place.core, place.core)
            self.near(chip * n, who, term(place.piece_row(chip, core)))

            @pl.when(who == 1)
            def _():
                for part in range(n):
                    self.low[chip * n + part] = self.own[chip * n + part].astype(BF16)
                    for ahead in range(1, place.chips):
                        self.far_copy(ahead, chip * n + part).start()

        loop(2 * count, step)

    def take(self, slot):
        rows = self.own[slot]
        for ahead in range(1, self.place.chips):
            self.far_copy(ahead, slot).wait_recv()
            rows = rows + self.far[self.stage, ahead - 1, slot].astype(F32)
        self.core_copy(slot).wait_send()
        for ahead in range(1, self.place.chips):
            self.far_copy(ahead, slot).wait_send()
        return rows

    def own_pieces(self, term):
        place = self.place
        n = place.per_piece

        def step(index):
            ahead, who = lax.rem(index // 2 + 1, place.chips), lax.rem(index, 2)
            core = jnp.where(who == 0, 1 - place.core, place.core)
            self.near(ahead * n, who, term(place.piece_row(place.chip(ahead), core)))

            @pl.when(jnp.logical_and(who == 1, ahead > 0))
            def _():
                for part in range(n):
                    self.low[ahead * n + part] = self.own[ahead * n + part].astype(BF16)
                    self.far_copy(ahead, ahead * n + part).start()

        loop(2 * place.chips, step)

    def own_total(self, part):
        n = self.place.per_piece
        rows = self.own[part]
        for ahead in range(1, self.place.chips):
            slot = ahead * n + part
            self.far_copy(ahead, slot).wait_recv()
            rows = rows + self.far[self.stage, ahead - 1, slot].astype(F32)
        return rows

    def own_end(self):
        n = self.place.per_piece
        for slot in range(self.place.chunks):
            self.core_copy(slot).wait_send()
            if slot >= n:
                self.far_copy(slot // n, slot).wait_send()


class Share:
    def __init__(self, place, ref, send_sems, recv_sems, stage=0):
        self.place, self.ref, self.s, self.r, self.stage = place, ref, send_sems, recv_sems, stage

    def copy(self, slot):
        rows = pl.ds(self.place.row(slot, self.place.core), CHUNK)
        at = (self.stage, slot)
        return remote(self.ref.at[rows], self.ref.at[rows], self.s.at[at], self.r.at[at], self.place.mate)

    def put(self, slot, rows):
        self.ref[pl.ds(self.place.row(slot, self.place.core), CHUNK), :] = rows
        self.copy(slot).start()

    def end(self, first, count):
        loop(count, lambda index: self.copy(first + index).wait())


class Gather:
    def __init__(self, place, own, ref, parts, sems):
        self.place, self.own, self.ref, self.parts = place, own, ref, parts
        self.size = own.shape[0] // parts
        self.s1, self.r1, self.s2, self.r2, self.local = sems

    @staticmethod
    def scratch(chips, parts, name):
        dma = pltpu.SemaphoreType.DMA
        specs = [dma((chips, parts)), dma((chips, parts)), dma((chips - 1, parts)), dma((chips - 1, parts)), dma((1,))]
        return {name + str(index): spec for index, spec in enumerate(specs)}

    def far(self, ahead, part):
        rows = pl.ds(part * self.size, self.size)
        sems = (self.s2.at[ahead - 1, part], self.r2.at[ahead - 1, part])
        return remote(self.own.at[rows], self.ref.at[self.place.tp, rows], *sems, self.place.peer(ahead))

    def near(self, ahead, part):
        place = self.place
        rows = pl.ds(part * self.size, self.size)
        device = lax.rem(place.x + place.chips - ahead, place.chips) * 2 + place.core
        src = self.ref.at[device, rows] if ahead else self.own.at[rows]
        sems = (self.s1.at[ahead, part], self.r1.at[ahead, part])
        return remote(src, self.ref.at[device, rows], *sems, place.mate)

    def keep(self):
        return pltpu.make_async_copy(self.own, self.ref.at[self.place.tp], self.local.at[0])

    def start(self):
        self.keep().start()
        for part in range(self.parts):
            for ahead in range(1, self.place.chips):
                self.far(ahead, part).start()
            self.near(0, part).start()

    def relay(self):
        for ahead in range(1, self.place.chips):
            for part in range(self.parts):
                self.far(ahead, part).wait_recv()
                self.near(ahead, part).start()

    def end(self):
        self.keep().wait()
        for part in range(self.parts):
            for ahead in range(self.place.chips):
                self.near(ahead, part).wait_recv()

    def drain(self):
        for part in range(self.parts):
            for ahead in range(1, self.place.chips):
                self.far(ahead, part).wait_send()
            for ahead in range(self.place.chips):
                self.near(ahead, part).wait_send()


class SeqSum:
    ROWS = 4

    def __init__(self, place, slot, r, name):
        self.place, self.slot = place, slot
        self.near_recv, self.low, self.far_recv, self.ns, self.nr, self.fs, self.fr = [
            getattr(r, name + str(index), None) for index in range(7)
        ]
        self.inner = place.seqs // self.ROWS
        self.row, self.column = place.seq // self.inner, lax.rem(place.seq, self.inner)

    @staticmethod
    def scratch(seqs, dims, dtype, name, near=True, far=True):
        dma = pltpu.SemaphoreType.DMA
        rows, inner = SeqSum.ROWS, seqs // SeqSum.ROWS
        specs = [
            pltpu.VMEM((inner - 1, rows, *dims), dtype) if near else None,
            pltpu.VMEM((rows, *dims), dtype) if near and far else None,
            pltpu.VMEM((rows - 1, *dims), dtype) if far else None,
            dma((inner - 1, rows)) if near else None,
            dma((inner - 1, rows)) if near else None,
            dma((rows - 1,)) if far else None,
            dma((rows - 1,)) if far else None,
        ]
        return {name + str(index): spec for index, spec in enumerate(specs) if spec is not None}

    def shard(self, row_ahead, column_ahead=0):
        row = lax.rem(self.row + row_ahead, self.ROWS)
        return row * self.inner + lax.rem(self.column + column_ahead, self.inner)

    def near(self, ahead, row_ahead):
        at = (ahead - 1, row_ahead)
        to = {"seq": self.shard(0, ahead)}
        return remote(self.slot(self.shard(row_ahead, ahead)), self.near_recv.at[at], self.ns.at[at], self.nr.at[at], to)

    def far(self, row_ahead):
        at = row_ahead - 1
        to = {"seq": self.shard(row_ahead)}
        return remote(self.low.at[row_ahead], self.far_recv.at[at], self.fs.at[at], self.fr.at[at], to)

    def each_near(self, act):
        def step(index):
            act(self.near(index // self.ROWS + 1, lax.rem(index, self.ROWS)))

        loop((self.inner - 1) * self.ROWS, step)

    def each_far(self, act):
        loop(self.ROWS - 1, lambda index: act(self.far(index + 1)))

    def start(self):
        self.each_near(lambda copy: copy.start())

    def fetch(self, sems):
        return [
            pltpu.make_async_copy(self.slot(self.shard(ahead)), self.low.at[ahead], sems.at[ahead])
            for ahead in range(self.ROWS)
        ]

    def combine(self, out, far=True, fetched=False):
        def rows_of(row_ahead):
            here = self.low.at[row_ahead] if fetched else self.slot(self.shard(row_ahead))
            rows = here[...].astype(F32)
            for ahead in range(1, self.inner):
                self.near(ahead, row_ahead).wait_recv()
                rows = rows + self.near_recv[ahead - 1, row_ahead].astype(F32)
            return rows

        def step(index):
            self.low[index + 1] = rows_of(index + 1).astype(self.low.dtype)
            if far:
                self.far(index + 1).start()

        loop(self.ROWS - 1, step)
        out[...] = rows_of(0)

    def finish(self, out):
        def step(index):
            self.far(index + 1).wait_recv()
            out[...] = out[...] + self.far_recv[index].astype(F32)

        loop(self.ROWS - 1, step)

    def end(self, near=True, far=True):
        if near:
            self.each_near(lambda copy: copy.wait_send())
        if far:
            self.each_far(lambda copy: copy.wait_send())


def head_masks():
    lane = lax.broadcasted_iota(jnp.int32, (1, PAIR), 1)
    first = (lane < HEAD_DIM).astype(F32)
    return first, 1.0 - first


def pair_lanes(pair):
    return pl.ds(pl.multiple_of(pair * PAIR, PAIR), PAIR)


def block_rows(block):
    return pl.ds(pl.multiple_of(block * BLOCK, BLOCK), BLOCK)


def causal_tile(keys_first):
    rows = lax.broadcasted_iota(jnp.int32, (BLOCK, BLOCK), 0)
    columns = lax.broadcasted_iota(jnp.int32, (BLOCK, BLOCK), 1)
    allowed = rows <= columns if keys_first else columns <= rows
    return jnp.where(allowed, 0.0, NEG)


def attend(q_ref, block, keys, values, biases, mixed_ref, lse_ref):
    masks = head_masks()
    rows = block_rows(block)
    lane = lax.broadcasted_iota(jnp.int32, (BLOCK, 128), 1)

    def step(pair):
        lanes = pair_lanes(pair)
        queries = q_ref[rows, lanes]
        pair_out = jnp.zeros((BLOCK, PAIR), F32)
        lse_block = jnp.zeros((BLOCK, 128), F32)
        for head in range(2):
            head_queries = queries * masks[head].astype(BF16)
            scores = [dot_nt(head_queries, keys(tile, lanes)) + bias() for tile, bias in enumerate(biases)]
            top = functools.reduce(jnp.maximum, [jnp.max(s, axis=-1, keepdims=True) for s in scores])
            total, out = 0.0, 0.0
            for tile, s in enumerate(scores):
                weights = jnp.exp(s - top)
                total = total + jnp.sum(weights, axis=-1, keepdims=True)
                out = out + dot(weights.astype(BF16), values(tile, lanes))
            pair_out = pair_out + out * masks[head] / total
            lse_block = jnp.where(lane == head, top + jnp.log(total), lse_block)
        mixed_ref[rows, lanes] = pair_out.astype(BF16)
        lse_ref[pair, :, rows] = jnp.transpose(lse_block)[:8]

    loop(q_ref.shape[1] // PAIR, step)


def dots_out(grad_ref, mixed_ref, block, dots_ref):
    masks = head_masks()
    rows = block_rows(block)
    lane = lax.broadcasted_iota(jnp.int32, (BLOCK, 128), 1)
    for pair in range(grad_ref.shape[1] // PAIR):
        lanes = pair_lanes(pair)
        product = grad_ref[rows, lanes].astype(F32) * mixed_ref[rows, lanes].astype(F32)
        values = jnp.zeros((BLOCK, 128), F32)
        for head in range(2):
            value = jnp.sum(product * masks[head], axis=-1, keepdims=True)
            values = jnp.where(lane == head, value, values)
        dots_ref[pair, :, rows] = jnp.transpose(values)[:8]


def attend_back(q_ref, grad_ref, lse_ref, dots_ref, block, pair, keys, values, bias):
    masks = head_masks()
    lanes, rows = pair_lanes(pair), block_rows(block)
    queries, grads = q_ref[rows, lanes], grad_ref[rows, lanes]
    dq = dk = dv = 0.0
    for head in range(2):
        mask = masks[head].astype(BF16)
        head_queries, head_grads, head_keys = queries * mask, grads * mask, keys * mask
        scores = dot_nt(keys, head_queries) + bias()
        weights = jnp.exp(scores - lse_ref[pair, head : head + 1, rows])
        grad_weights = dot_nt(values, head_grads)
        grad_scores = (weights * (grad_weights - dots_ref[pair, head : head + 1, rows])).astype(BF16)
        dv = dv + dot(weights.astype(BF16), head_grads)
        dk = dk + dot(grad_scores, head_queries)
        dq = dq + dot_tn(grad_scores, head_keys)
    return dq * HEAD_DIM ** (-0.5), dk, dv


def grad_weight(out_ref, first, left_ref, right, rows=None):
    count = left_ref.shape[1]
    step_size = min(256, count)
    width = right.shape[1]

    def step(index):
        columns = pl.ds(pl.multiple_of(index * step_size, step_size), step_size)
        out_ref[columns, first : first + width] = dot_tn(left_ref[:, columns], right[...]).astype(BF16)

    loop(count // step_size, step)


def scaled(queries):
    return (queries.astype(BF16).astype(F32) * HEAD_DIM ** (-0.5)).astype(BF16)


def half_rows(slot):
    return pl.ds(pl.multiple_of(slot * CHUNK, CHUNK), CHUNK)


def reach_bias(offsets, block, tile):
    return jnp.where(offsets[block * BLOCK] >= (REACH - tile) * BLOCK, 0.0, NEG)


def norm_step(place, r, sums, share, base, res):
    def finish(slot, carry):
        hat, inv_std = hat_of(res[half_rows(slot), :])
        grad_in, gain_sum, shift_sum = norm_back(sums.take(slot), hat, inv_std, r.gain[...])
        rows = base(slot) + grad_in
        r.grad.ref[half_rows(slot), :] = rows
        share.put(slot, rows.astype(BF16))
        return carry[0] + gain_sum, carry[1] + shift_sum

    zero = jnp.zeros((1, r.gain.shape[1]), F32)
    gain_sum, shift_sum = lax.fori_loop(0, place.chunks, finish, (zero, zero))
    r.norm[0:1, :] = gain_sum
    r.norm[1:2, :] = shift_sum


def open_body(chips, seqs, r):
    n1, half = r.n1.ref, (r.half.ref, r.prev.ref)
    tokens = n1.shape[0] // 2
    place = Place(chips, seqs, tokens)
    place.enter(seq="all")
    n, piece = place.per_piece, place.piece
    own_rows = pl.ds(pl.multiple_of(place.x * piece, CHUNK), piece)

    def half_part(chip, part):
        return pl.ds(pl.multiple_of(chip * piece + part * CHUNK, CHUNK), CHUNK)

    def far(which, ahead, part):
        dst = half[which].at[half_part(place.x, part)]
        src = dst if which else r.x.at[pl.ds(part * CHUNK, CHUNK)]
        at = (which, ahead - 1, part)
        return remote(src, dst, r.s2.at[at], r.r2.at[at], place.peer(ahead))

    def pass_on(part):
        src, dst = r.x.at[pl.ds(part * CHUNK, CHUNK)], half[1].at[half_part(place.x, part)]
        return remote(src, dst, r.ss.at[part], r.sr.at[part], {"seq": place.seq + 1})

    def parts(act):
        for part in range(n):
            act(part)

    pl.when(place.has_next)(lambda: parts(lambda part: pass_on(part).start()))
    for part in range(n):
        for ahead in range(1, chips):
            far(0, ahead, part).start()
    grads = Gather(place, r.og_own, r.og, n, [getattr(r, "og_" + str(i)) for i in range(5)])

    columns = pl.ds(pl.multiple_of(place.tp * r.mem.shape[3], 128), r.mem.shape[3])
    rows_apart = SeqSum.ROWS
    inner = seqs // rows_apart
    seq_row, seq_column = place.seq // inner, lax.rem(place.seq, inner)

    def mem_far(ahead):
        to = {"seq": lax.rem(seq_row + ahead, rows_apart) * inner + seq_column}
        sems = (r.fs.at[ahead - 1], r.fr.at[ahead - 1])
        return remote(r.memory.at[0, :, columns], r.mem.at[place.seq, 0], *sems, to)

    def mem_near(behind, ahead):
        row = lax.rem(seq_row + rows_apart - behind, rows_apart)
        to = {"seq": seq_row * inner + lax.rem(seq_column + ahead, inner)}
        dst = r.mem.at[row * inner + seq_column, 0]
        src = dst if behind else r.memory.at[0, :, columns]
        sems = (r.ns.at[behind, ahead - 1], r.nr.at[behind, ahead - 1])
        return remote(src, dst, *sems, to)

    def mem_pass(behind):
        mem_far(behind).wait_recv()
        for ahead in range(1, inner):
            mem_near(behind, ahead).start()

    def known_copies(ahead):
        to = {"seq": place.shard(ahead)}
        at = [(which, ahead - 1) for which in range(2)]
        return (
            remote(r.mask, r.masks.at[place.seq], r.ms.at[at[0]], r.mr.at[at[0]], to),
            remote(r.page_row, r.pages.at[place.seq], r.ms.at[at[1]], r.mr.at[at[1]], to),
        )

    def known_all(act):
        def step(index):
            for copy in known_copies(index + 1):
                act(copy)

        loop(seqs - 1, step)

    lane = lax.broadcasted_iota(jnp.int32, r.page_row.shape, 1)
    page_row = jnp.zeros(r.page_row.shape, jnp.int32)
    for block in range(tokens // BLOCK):
        page_row = jnp.where(lane == block, r.ids[block * BLOCK], page_row)
    r.page_row[...] = page_row
    own_copies = [
        pltpu.make_async_copy(r.memory.at[0, :, columns], r.mem.at[place.seq, 0], r.local.at[0]),
        pltpu.make_async_copy(r.mask, r.masks.at[place.seq], r.local.at[1]),
        pltpu.make_async_copy(r.page_row, r.pages.at[place.seq], r.local.at[2]),
    ]
    for copy in own_copies:
        copy.start()
    for ahead in (1, 3, 2):
        mem_far(ahead).start()
    for ahead in range(1, inner):
        mem_near(0, ahead).start()
    known_all(lambda copy: copy.start())
    half[0][own_rows, :] = r.x[...]

    def from_chip(ahead):
        return lax.rem(place.x + chips - ahead, chips)

    def near(which, ahead, part):
        row = pl.multiple_of((from_chip(ahead) * 2 + place.core) * piece + part * CHUNK, CHUNK)
        rows = n1.at[pl.ds((1 - which) * tokens + row, CHUNK)]
        at = (which, ahead, part)
        return remote(rows, rows, r.s1.at[at], r.r1.at[at], place.mate)

    def normed(which, ahead, part):
        chip = from_chip(ahead)
        hat, _ = hat_of(half[which][half_part(chip, part), :].astype(F32))
        row = pl.multiple_of((chip * 2 + place.core) * piece + part * CHUNK, CHUNK)
        n1[pl.ds((1 - which) * tokens + row, CHUNK), :] = (hat * r.gain[...] + r.shift[...]).astype(BF16)
        near(which, ahead, part).start()

    def project(which, ahead):
        for part in range(n):
            near(which, ahead, part).wait_recv()
        chip = from_chip(ahead)
        row = pl.multiple_of(chip * 2 * piece, CHUNK)
        rows = pl.ds((1 - which) * tokens + row, 2 * piece)
        rows_in = n1[rows, :]
        r.kext[rows, :] = dot(rows_in, r.wk[...]).astype(BF16)
        r.vext[rows, :] = dot(rows_in, r.wv[...]).astype(BF16)
        if not which:
            r.q[pl.ds(row, 2 * piece), :] = scaled(dot(rows_in, r.wq[...]))

    def step(which, ahead):
        for part in range(n):
            if ahead:
                far(which, ahead, part).wait_recv()
            normed(which, ahead, part)
        project(which, ahead)

    step(0, 0)
    mem_pass(1)
    for ahead in range(1, chips):
        step(0, ahead)
    r.half.start()
    mem_pass(3)

    @pl.when(jnp.logical_not(place.has_prev))
    def _():
        half[1][own_rows, :] = jnp.zeros((piece, n1.shape[1]), BF16)

    pl.when(place.has_prev)(lambda: parts(lambda part: pass_on(part).wait_recv()))
    for part in range(n):
        for ahead in range(1, chips):
            far(1, ahead, part).start()
    grads.start()
    step(1, 0)
    mem_pass(2)
    for ahead in range(1, chips):
        step(1, ahead)
    r.prev.start()
    r.n1.start()
    grads.relay()
    for part in range(n):
        for which in range(2):
            for ahead in range(1, chips):
                far(which, ahead, part).wait_send()
            for ahead in range(chips):
                near(which, ahead, part).wait_send()
    pl.when(place.has_next)(lambda: parts(lambda part: pass_on(part).wait_send()))
    grads.end()
    grads.drain()
    for copy in own_copies:
        copy.wait()
    for behind in range(1, rows_apart):
        mem_far(behind).wait_send()
    for behind in range(rows_apart):
        for ahead in range(1, inner):
            mem_near(behind, ahead).wait()
    known_all(lambda copy: copy.wait())


def opening(chips, seqs, ids, x, og, memory, mask, gain, shift, wq, wk, wv):
    width, dim = wq.shape[1], x.shape[1]
    tokens = ids.shape[0]
    n = tokens // (2 * chips) // CHUNK
    rows, inner = SeqSum.ROWS, seqs // SeqSum.ROWS
    dma = pltpu.SemaphoreType.DMA
    vmem = lambda array: (array, "vmem")
    return call(
        functools.partial(open_body, chips, seqs),
        "opening",
        dict(
            ids=(ids, "smem"),
            x=vmem(x),
            og_own=(og, "hbm"),
            memory=(memory, "hbm"),
            mask=vmem(mask),
            gain=vmem(gain),
            shift=vmem(shift),
            wq=vmem(wq),
            wk=vmem(wk),
            wv=vmem(wv),
        ),
        dict(
            n1=((2 * tokens, dim), BF16, "late"),
            half=((tokens // 2, dim), BF16, "late"),
            prev=((tokens // 2, dim), BF16, "late"),
            q=((tokens, width), BF16, "vmem"),
            kext=((2 * tokens, width), BF16, "vmem"),
            vext=((2 * tokens, width), BF16, "vmem"),
            mem=((seqs, 1, memory.shape[1], dim // (2 * chips)), BF16, "hbm"),
            masks=((seqs, 1, mask.shape[1]), jnp.int32, "vmem"),
            pages=((seqs, 8, 128), jnp.int32, "vmem"),
            og=((2 * chips, tokens // (2 * chips), dim), BF16, "hbm"),
        ),
        dict(
            s1=dma((2, chips, n)),
            r1=dma((2, chips, n)),
            s2=dma((2, chips - 1, n)),
            r2=dma((2, chips - 1, n)),
            ss=dma((n,)),
            sr=dma((n,)),
            ms=dma((2, seqs - 1)),
            mr=dma((2, seqs - 1)),
            fs=dma((rows - 1,)),
            fr=dma((rows - 1,)),
            ns=dma((rows, inner - 1)),
            nr=dma((rows, inner - 1)),
            local=dma((3,)),
            page_row=pltpu.VMEM((8, 128), jnp.int32),
            **Gather.scratch(chips, n, "og_"),
        ),
        0,
        10 * tokens * dim * width,
    )


def forward_body(chips, seqs, r):
    tokens = r.q.shape[0]
    place = Place(chips, seqs, tokens)
    place.enter()
    piece, blocks = place.piece, tokens // BLOCK
    per_block, chips_per_block = place.chunks // blocks, chips // blocks
    mem_true = r.mem8.shape[2]
    keys = r.mem_k.shape[0] // blocks
    stages = [Sums(place, r, stage=stage) for stage in range(3)]
    mem = r.mem.ref

    r.mem_own[...] = jnp.zeros_like(r.mem_own)
    r.bias[...] = jnp.full(r.bias.shape, NEG, F32)
    for block in range(blocks):
        rows = pl.ds(block * keys, mem_true)

        def choose(page):
            r.mem_own[rows, :] = jnp.where(r.ids[block * BLOCK] == page, r.mem8[page, 0], r.mem_own[rows, :])

        def mask_of(page, mask):
            return jnp.where(r.ids[block * BLOCK] == page, r.masks[page], mask)

        loop(seqs, choose)
        mask = lax.fori_loop(0, seqs, mask_of, jnp.zeros((1, mem_true), jnp.int32))
        r.bias[block, :, :mem_true] = jnp.broadcast_to(jnp.where(mask > 0, 0.0, NEG), (8, mem_true))
    memory = Gather(place, r.mem_own, mem, 4, [getattr(r, "mem_" + str(i)) for i in range(5)])
    memory.start()
    r.causal[...] = causal_tile(False)

    def self_block(block):
        biases = [functools.partial(reach_bias, r.offsets, block, tile) for tile in range(REACH)]
        attend(
            r.q,
            block,
            lambda tile, lanes: r.kext[block_rows(block + tile), lanes],
            lambda tile, lanes: r.vext[block_rows(block + tile), lanes],
            biases + [lambda: r.causal[...]],
            r.mixed1,
            r.lse1,
        )
        stages[0].all_pieces(
            block * chips_per_block, chips_per_block, lambda row: dot(r.mixed1[pl.ds(row, piece), :], r.wo[...])
        )

    loop(blocks, self_block)

    memory.relay()
    memory.end()
    wide = mem.shape[2]
    for weight, out in ((r.wck, r.mem_k), (r.wcv, r.mem_v)):
        rows = 0.0
        for device in range(2 * chips):
            rows = rows + dot(mem[device], weight[device * wide : (device + 1) * wide, :])
        out[...] = rows.astype(BF16)
    r.mem.start()

    half = r.half.wait()
    n2, res1, res2 = r.n2.ref, r.res1.ref, r.res2.ref
    share = Share(place, n2, r.ss, r.sr, 0)

    def finish_self(slot):
        rows = half[half_rows(slot), :].astype(F32) + stages[0].take(slot)
        res1[half_rows(slot), :] = rows
        hat, _ = hat_of(rows)
        share.put(slot, (hat * r.cross_gain[...] + r.cross_shift[...]).astype(BF16))

    cross_query, cross_output = r.wq.wait(), r.wco.wait()

    def cross_block(block):
        loop(per_block, lambda index: finish_self(block * per_block + index))
        share.end(block * per_block, per_block)
        rows = block_rows(block)
        page = pl.ds(pl.multiple_of(block * keys, 128), keys)
        r.q2[rows, :] = scaled(dot(n2[rows, :], cross_query[...]))
        attend(
            r.q2,
            block,
            lambda tile, lanes: r.mem_k[page, lanes],
            lambda tile, lanes: r.mem_v[page, lanes],
            [lambda: r.bias[block, 0:1, :]],
            r.mixed2,
            r.lse2,
        )
        stages[1].all_pieces(
            block * chips_per_block,
            chips_per_block,
            lambda row: dot(r.mixed2[pl.ds(row, piece), :], cross_output[...]),
        )

    loop(blocks, cross_block)
    r.n2.start()
    r.res1.start()

    share_ffn = Share(place, r.n3, r.ss, r.sr, 1)
    up, down, og = r.up.wait(), r.down.wait(), r.og.wait()
    act = r.act.ref

    def finish_cross(slot):
        rows = res1[half_rows(slot), :] + stages[1].take(slot)
        res2[half_rows(slot), :] = rows
        hat, _ = hat_of(rows)
        share_ffn.put(slot, (hat * r.gain[...] + r.shift[...]).astype(BF16))

    def term(row):
        rows = pl.ds(row, piece)
        pre = dot(r.n3[rows, :], up[...])
        half_erf = 0.5 * lax.erf(pre * (0.5**0.5)) + 0.5
        act[rows, :] = (pre * half_erf).astype(BF16)
        slope = half_erf + pre * jnp.exp(-0.5 * pre * pre) * (0.15915494309189535**0.5)
        grad_act = dot_nt(og[rows, :], down[...])
        low = (grad_act * slope).astype(BF16)
        r.gpre[rows, :] = low
        return dot_nt(low, up[...])

    def ffn_block(block):
        loop(per_block, lambda index: finish_cross(block * per_block + index))
        share_ffn.end(block * per_block, per_block)
        stages[2].all_pieces(block * chips_per_block, chips_per_block, term)

    loop(blocks, ffn_block)
    r.res2.start()
    r.act.start()
    grad_weight(r.g_down.ref, 0, og, act)
    r.g_down.start()
    grad_weight(r.g_up.ref, 0, r.n3, r.gpre)
    r.g_up.start()

    share_grad = Share(place, r.g.ref, r.ss, r.sr, 2)
    norm_step(
        place,
        r,
        stages[2],
        share_grad,
        lambda slot: og[pl.ds(place.row(slot, place.core), CHUNK), :].astype(F32),
        res2,
    )
    r.grad.start()
    share_grad.end(0, place.chunks)
    r.g.start()
    memory.drain()


def forward(chips, seqs, ids, offsets, a, w):
    tokens, width = a.q.shape
    dim, hidden = w.up.shape
    chunks = tokens // 2 // CHUNK
    blocks = tokens // BLOCK
    mem_true, wide = a.mem.shape[2:]
    keys = -(-mem_true // 128) * 128
    dma = pltpu.SemaphoreType.DMA
    vmem = lambda array: (array, "vmem")
    late = lambda array: (array, "late")
    return call(
        functools.partial(forward_body, chips, seqs),
        "forward",
        dict(
            ids=(ids, "smem"),
            offsets=(offsets, "smem"),
            q=vmem(a.q),
            kext=vmem(a.kext),
            vext=vmem(a.vext),
            mem8=vmem(a.mem),
            masks=vmem(a.masks),
            wo=vmem(w.attn_output),
            wck=vmem(w.cross_key),
            wcv=vmem(w.cross_value),
            cross_gain=vmem(w.cross_gain),
            cross_shift=vmem(w.cross_shift),
            gain=vmem(w.ffn_gain),
            shift=vmem(w.ffn_shift),
            half=late(a.half),
            wq=late(w.cross_query),
            wco=late(w.cross_output),
            up=late(w.up),
            og=late(a.og.reshape(tokens, dim)),
            down=late(w.down),
        ),
        dict(
            mixed1=((tokens, width), BF16, "vmem"),
            lse1=((width // PAIR, 8, tokens), F32, "vmem"),
            res1=((tokens // 2, dim), F32, "late"),
            n2=((tokens, dim), BF16, "late"),
            mem=((2 * chips, blocks * keys, wide), BF16, "late"),
            mem_k=((blocks * keys, width), BF16, "vmem"),
            mem_v=((blocks * keys, width), BF16, "vmem"),
            bias=((blocks, 8, keys), F32, "vmem"),
            q2=((tokens, width), BF16, "vmem"),
            mixed2=((tokens, width), BF16, "vmem"),
            lse2=((width // PAIR, 8, tokens), F32, "vmem"),
            res2=((tokens // 2, dim), F32, "late"),
            act=((tokens, hidden), BF16, "late"),
            grad=((tokens // 2, dim), F32, "late"),
            g=((tokens, dim), BF16, "late"),
            norm=((2, dim), F32, "vmem"),
            g_up=((dim, hidden), BF16, "late"),
            g_down=((dim, hidden), BF16, "late"),
        ),
        dict(
            **sum_scratch(chips, tokens, dim, stages=3),
            **Gather.scratch(chips, 4, "mem_"),
            mem_own=pltpu.VMEM((blocks * keys, wide), BF16),
            causal=pltpu.VMEM((BLOCK, BLOCK), F32),
            n3=pltpu.VMEM((tokens, dim), BF16),
            gpre=pltpu.VMEM((tokens, hidden), BF16),
            ss=dma((3, chunks)),
            sr=dma((3, chunks)),
        ),
        1,
        14 * tokens * dim * hidden,
    )


def cross_back_body(chips, seqs, r):
    tokens = r.g_in.shape[0]
    place = Place(chips, seqs, tokens)
    place.enter(seq="all")
    piece, n, blocks = place.piece, place.per_piece, tokens // BLOCK
    share_rows = r.sum_down.shape[0]
    keys = r.mem_k.shape[0] // blocks
    mine = lambda ref: (lambda shard: ref.at[pl.ds(pl.multiple_of(shard * share_rows, 8), share_rows)])
    seq_up = SeqSum(place, mine(r.g_up), r, "up_")
    seq_up.low = r.up_low
    seq_down = SeqSum(place, mine(r.g_down), r, "down_")
    seq_down.start()
    seq_up.start()
    fetches = [seq_sum.fetch(r.fetch.at[index]) for index, seq_sum in enumerate((seq_down, seq_up))]
    for copies in fetches:
        for copy in copies:
            copy.start()
    sums = Sums(place, r)

    def step(block):
        rows = block_rows(block)
        page = pl.ds(pl.multiple_of(block * keys, 128), keys)
        r.dout[rows, :] = dot_nt(r.g_in[rows, :], r.wo[...]).astype(BF16)
        dots_out(r.dout, r.mixed, block, r.dots)
        bias = jnp.transpose(r.bias[block])[:, 0:1]

        def pair_step(pair):
            lanes = pair_lanes(pair)
            dq, dk, dv = attend_back(
                r.q,
                r.dout,
                r.lse,
                r.dots,
                block,
                pair,
                r.mem_k[page, lanes],
                r.mem_v[page, lanes],
                lambda: bias,
            )
            r.gq[rows, lanes] = dq.astype(BF16)
            r.gk[page, lanes] = dk.astype(BF16)
            r.gv[page, lanes] = dv.astype(BF16)

        loop(r.q.shape[1] // PAIR, pair_step)
        sums.all_pieces(
            block * (chips // blocks),
            chips // blocks,
            lambda row: dot_nt(r.gq[pl.ds(row, piece), :], r.wq[...]),
        )

    loop(blocks, step)

    hidden = Sums(place, r, "hidden_")
    act, down = r.act.wait(), r.down.wait()
    hidden.own_pieces(lambda row: dot(act[pl.ds(row, piece), :], down[...]))

    width = r.q.shape[1]
    n2, mem = r.n2.wait(), r.mem.wait()
    g_w, mem_part = r.g_w.ref, r.mem_part.ref
    wide = mem.shape[2]

    def mem_step(device):
        rows = pl.ds(pl.multiple_of(device * wide, wide), wide)
        g_w[rows, width : 2 * width] = dot_tn(mem[device], r.gk[...]).astype(BF16)
        g_w[rows, 2 * width : 3 * width] = dot_tn(mem[device], r.gv[...]).astype(BF16)
        mem_part[device] = (dot_nt(r.gk[...], r.wck[rows, :]) + dot_nt(r.gv[...], r.wcv[rows, :])).astype(BF16)

    loop(2 * chips, mem_step)
    r.mem_part.start()
    grad_weight(g_w, 0, n2, r.gq)
    grad_weight(g_w, 3 * width, r.g_in, r.mixed)
    r.g_w.start()

    for copies in fetches:
        for copy in copies:
            copy.wait()
    seq_down.combine(r.sum_down, fetched=True)
    share = Share(place, r.g.ref, r.s1, r.r1)
    res, grad_in = r.res.wait(), r.grad_in.wait()
    norm_step(place, r, sums, share, lambda slot: grad_in[half_rows(slot), :], res)
    r.grad.start()
    share.end(0, place.chunks)
    r.g.start()
    for part in range(n):
        rows = pl.ds(part * CHUNK, CHUNK)
        mine_rows = pl.ds(pl.multiple_of(place.x * piece + part * CHUNK, CHUNK), CHUNK)
        base = pltpu.make_async_copy(r.res_out.at[mine_rows], r.base, r.fetch.at[2, 0])
        base.start()
        base.wait()
        r.out[rows, :] = (r.base[...] + hidden.own_total(part)).astype(BF16)
    seq_up.combine(r.up_own, far=False, fetched=True)
    seq_down.finish(r.sum_down)
    seq_down.end()
    seq_up.end(far=False)
    hidden.own_end()


def cross_back(chips, seqs, a, f, w):
    tokens, dim = f.g.shape
    width = f.q2.shape[1]
    hidden = f.act.shape[1]
    chunks = tokens // 2 // CHUNK
    mem_rows = f.mem_k.shape[0]
    rows = SeqSum.ROWS
    dma = pltpu.SemaphoreType.DMA
    vmem = lambda array: (array, "vmem")
    late = lambda array: (array, "late")
    hbm = lambda array: (array, "hbm")
    return call(
        functools.partial(cross_back_body, chips, seqs),
        "cross_back",
        dict(
            g_in=vmem(f.g),
            wo=vmem(w.cross_output),
            q=vmem(f.q2),
            mem_k=vmem(f.mem_k),
            mem_v=vmem(f.mem_v),
            bias=vmem(f.bias),
            mixed=vmem(f.mixed2),
            lse=vmem(f.lse2),
            wq=vmem(w.cross_query),
            gain=vmem(w.cross_gain),
            wck=vmem(w.cross_key),
            wcv=vmem(w.cross_value),
            act=late(f.act),
            down=late(w.down),
            mem=late(f.mem),
            n2=late(f.n2),
            res=late(f.res1),
            grad_in=late(f.grad),
            res_out=hbm(f.res2),
            g_up=hbm(f.g_up),
            g_down=hbm(f.g_down),
        ),
        dict(
            grad=((tokens // 2, dim), F32, "late"),
            g=((tokens, dim), BF16, "late"),
            norm=((2, dim), F32, "vmem"),
            g_w=((dim, 4 * width), BF16, "late"),
            mem_part=(f.mem.shape, BF16, "late"),
            up_own=((dim // seqs, hidden), F32, "vmem"),
            up_low=((rows, dim // seqs, hidden), BF16, "vmem"),
            sum_down=((dim // seqs, hidden), F32, "vmem"),
            out=((tokens // (2 * chips), dim), BF16, "vmem"),
        ),
        dict(
            **sum_scratch(chips, tokens, dim),
            **sum_scratch(chips, tokens, dim, "hidden_"),
            **SeqSum.scratch(seqs, (dim // seqs, hidden), BF16, "up_", far=False),
            **SeqSum.scratch(seqs, (dim // seqs, hidden), BF16, "down_"),
            gq=pltpu.VMEM((tokens, width), BF16),
            gk=pltpu.VMEM((mem_rows, width), BF16),
            gv=pltpu.VMEM((mem_rows, width), BF16),
            dout=pltpu.VMEM((tokens, width), BF16),
            dots=pltpu.VMEM((width // PAIR, 8, tokens), F32),
            base=pltpu.VMEM((CHUNK, dim), F32),
            s1=dma((1, chunks)),
            r1=dma((1, chunks)),
            fetch=dma((3, rows)),
        ),
        2,
        12 * tokens * dim * width,
    )


def close_body(chips, seqs, r):
    tokens, width = r.q.shape
    place = Place(chips, seqs, tokens)
    place.enter(seq="all", all_tp=True)
    piece, n, blocks = place.piece, place.per_piece, tokens // BLOCK
    pairs = width // PAIR
    share_rows = r.sum_w.shape[0]
    mine = lambda ref: (lambda shard: ref.at[pl.ds(pl.multiple_of(shard * share_rows, 8), share_rows)])

    seq_up = SeqSum(place, None, r, "up_")
    seq_up.low = r.up_low
    seq_up.each_far(lambda copy: copy.start())
    seq_cross = SeqSum(place, mine(r.g_w), r, "cross_")
    seq_cross.start()
    fetches = (
        [
            pltpu.make_async_copy(r.up_own, r.sum_up, r.fetch.at[0]),
            pltpu.make_async_copy(r.grad_in.at[pl.ds(place.x * piece, piece)], r.grad_own, r.fetch.at[1]),
        ]
        + [
            pltpu.make_async_copy(r.mem_part.at[chip * 2 + place.core], r.part.at[chip], r.fetch.at[2 + chip])
            for chip in range(chips)
        ]
        + seq_cross.fetch(r.fetch.at[pl.ds(2 + chips, SeqSum.ROWS)])
    )
    for fetch in fetches:
        fetch.start()

    mem_rows = r.mem_part.shape[1]

    def mem_near(chip):
        src = r.mem_part.at[chip * 2 + 1 - place.core]
        return remote(src, r.mem_mate.at[chip], r.mns.at[chip], r.mnr.at[chip], place.mate)

    def mem_far(ahead):
        sems = (r.mfs.at[ahead - 1], r.mfr.at[ahead - 1])
        return remote(r.mem_mate.at[place.chip(ahead)], r.mem_far.at[ahead - 1], *sems, place.peer(ahead))

    for chip in range(chips):
        mem_near(chip).start()

    r.causal[...] = causal_tile(True)

    def open_block(block):
        rows = block_rows(block)
        r.dout[rows, :] = dot_nt(r.g_in[rows, :], r.wo[...]).astype(BF16)
        dots_out(r.dout, r.mixed, block, r.dots)

    loop(blocks, open_block)
    r.dq[...] = jnp.zeros_like(r.dq)
    r.dk[...] = jnp.zeros_like(r.dk)
    r.dv[...] = jnp.zeros_like(r.dv)

    def tile_back(block, tile):
        rows, key_rows = block_rows(block), block_rows(block + tile)
        diagonal = jnp.where(tile == REACH, 1.0, 0.0)
        bias = jnp.where(tile == REACH, 0.0, reach_bias(r.offsets, block, tile))

        def step(pair):
            lanes = pair_lanes(pair)
            dq, dk, dv = attend_back(
                r.q,
                r.dout,
                r.lse,
                r.dots,
                block,
                pair,
                r.kext[key_rows, lanes],
                r.vext[key_rows, lanes],
                lambda: r.causal[...] * diagonal + bias,
            )
            r.dq[rows, lanes] = r.dq[rows, lanes] + dq
            r.dk[key_rows, lanes] = r.dk[key_rows, lanes] + dk
            r.dv[key_rows, lanes] = r.dv[key_rows, lanes] + dv

        loop(pairs, step)

    loop(3, lambda index: tile_back(index // 2, lax.rem(index, 2)))
    r.gkv[0, :tokens, :] = r.dk[:tokens, :].astype(BF16)
    r.gkv[1, :tokens, :] = r.dv[:tokens, :].astype(BF16)

    def kv_term(first):
        def term(row):
            rows = pl.ds(first + row, piece)
            return dot_nt(r.gkv[0, rows, :], r.wk[...]) + dot_nt(r.gkv[1, rows, :], r.wv[...])

        return term

    sums_prev = Sums(place, r, "prev_")
    sums_prev.own_pieces(kv_term(0))

    for fetch in fetches:
        fetch.wait()
    for chip in range(chips):
        mem_near(chip).wait_recv()
    for ahead in range(1, chips):
        chip = place.chip(ahead)
        both = r.part[chip].astype(F32) + r.mem_mate[chip].astype(F32)
        r.mem_mate[chip] = both.astype(BF16)
        mem_far(ahead).start()

    tile_back(0, REACH)

    def shift_copy(part):
        rows = pl.ds(part * CHUNK, CHUNK)
        sems = (r.ks.at[part], r.kr.at[part])
        return remote(r.shift_out.at[rows], r.shift_in.at[rows], *sems, {"seq": place.seq - 1})

    def shifts(act):
        for part in range(n):
            act(shift_copy(part))

    for part in range(n):
        r.shift_out[pl.ds(part * CHUNK, CHUNK), :] = sums_prev.own_total(part).astype(BF16)
    pl.when(place.has_prev)(lambda: shifts(lambda copy: copy.start()))
    seq_cross.combine(r.sum_w, fetched=True)

    @pl.when(jnp.logical_not(place.has_next))
    def _():
        r.shift_in[...] = jnp.zeros_like(r.shift_in)

    loop(2, lambda index: tile_back(1, 1 + index))
    r.gq[...] = r.dq[...].astype(BF16)
    r.gkv[0, tokens:, :] = r.dk[tokens:, :].astype(BF16)
    r.gkv[1, tokens:, :] = r.dv[tokens:, :].astype(BF16)

    n1 = r.n1.wait()
    grad_weight(r.g_self, 0, n1.at[pl.ds(tokens, tokens)], r.gq)
    for which in range(2):
        grad_weight(r.g_self, (1 + which) * width, n1, r.gkv.at[which])
    grad_weight(r.g_self, 3 * width, r.g_in, r.mixed)
    seq_self = SeqSum(place, mine(r.g_self), r, "self_")
    seq_self.start()

    own_kv = kv_term(tokens)
    sums = Sums(place, r)
    sums.own_pieces(lambda row: dot_nt(r.gq[pl.ds(row, piece), :], r.wq[...]) + own_kv(row))

    total = r.part[place.x].astype(F32) + r.mem_mate[place.x].astype(F32)
    for ahead in range(1, chips):
        mem_far(ahead).wait_recv()
        total = total + r.mem_far[ahead - 1].astype(F32)
    r.mem_sum[...] = total
    keys = mem_rows // blocks
    inner = seqs // SeqSum.ROWS
    seq_row, seq_column = place.seq // inner, lax.rem(place.seq, inner)

    def page_of(shard, block):
        return r.pages[shard, 0:1, block : block + 1]

    def page_near(ahead):
        to = {"seq": seq_row * inner + lax.rem(seq_column + ahead, inner)}
        return remote(r.page_out.at[ahead - 1], r.page_in.at[ahead - 1], r.pns.at[ahead - 1], r.pnr.at[ahead - 1], to)

    for ahead in range(1, inner):
        column = lax.rem(seq_column + ahead, inner)
        for block in range(blocks):
            page = r.ids[block * BLOCK]
            there = jnp.where(lax.rem(page, inner) == column, 1.0, 0.0)
            rows = r.mem_sum[block * keys : (block + 1) * keys, :]
            r.page_out[ahead - 1, block] = (rows * there).astype(BF16)
        page_near(ahead).start()

    half, prev = r.half.wait(), r.prev.wait()

    def norm_rows(slot, carry):
        ahead, part = slot // n, lax.rem(slot, n)
        mine_rows = pl.ds(pl.multiple_of(place.chip(ahead) * piece + part * CHUNK, CHUNK), CHUNK)
        gain_sum, shift_sum = carry
        for part_sums, ref in ((sums, half), (sums_prev, prev)):
            hat, _ = hat_of(ref[mine_rows, :].astype(F32))
            rows = part_sums.own[slot]
            gain_sum = gain_sum + jnp.sum(rows * hat, axis=0, keepdims=True)
            shift_sum = shift_sum + jnp.sum(rows, axis=0, keepdims=True)
        return gain_sum, shift_sum

    zero = jnp.zeros((1, r.gain.shape[1]), F32)
    norms = list(lax.fori_loop(0, place.chunks, norm_rows, (zero, zero)))
    norms += [ref[row : row + 1, :] * (1.0 / chips) for ref in (r.norm_cross, r.norm_ffn) for row in range(2)]
    columns = r.norm_out.shape[2]
    for shard in range(seqs):
        for row, values in enumerate(norms):
            r.norm_out[shard, row : row + 1, :] = values[:, shard * columns : (shard + 1) * columns]
        r.norm_out[shard, 6:8, :] = jnp.zeros((2, columns), F32)

    def norm_seq(ahead):
        shard = place.shard(ahead)
        sems = (r.nss.at[ahead - 1], r.nsr.at[ahead - 1])
        return remote(r.norm_out.at[shard], r.norm_seq.at[ahead - 1], *sems, {"seq": shard})

    for ahead in range(1, seqs):
        norm_seq(ahead).start()

    for ahead in range(1, inner):
        page_near(ahead).wait_recv()

    def page_rows(row):
        page = row * inner + seq_column
        rows = 0.0
        for block in range(blocks):
            same = (page_of(place.seq, block) == page).astype(F32)
            rows = rows + r.mem_sum[block * keys : (block + 1) * keys, :] * same
            for ahead in range(1, inner):
                shard = seq_row * inner + lax.rem(seq_column + inner - ahead, inner)
                same = (page_of(shard, block) == page).astype(F32)
                rows = rows + r.page_in[ahead - 1, block].astype(F32) * same
        return rows

    def page_far(ahead):
        to = {"seq": lax.rem(seq_row + ahead, SeqSum.ROWS) * inner + seq_column}
        sems = (r.pfs.at[ahead - 1], r.pfr.at[ahead - 1])
        return remote(r.page_low.at[ahead - 1], r.page_far.at[ahead - 1], *sems, to)

    def page_step(index):
        r.page_low[index] = page_rows(lax.rem(seq_row + index + 1, SeqSum.ROWS)).astype(BF16)
        page_far(index + 1).start()

    loop(SeqSum.ROWS - 1, page_step)
    r.page_sum[...] = page_rows(seq_row)

    seq_self.combine(r.sum_self)

    norm_rows_in = r.norm_out[place.seq]
    for ahead in range(1, seqs):
        norm_seq(ahead).wait_recv()
        norm_rows_in = norm_rows_in + r.norm_seq[ahead - 1]
    r.norm_sum[...] = norm_rows_in

    def norm_tp(ahead):
        to = {"tp": lax.rem(place.tp + ahead, 2 * chips)}
        return remote(r.norm_sum, r.norm_tp.at[ahead - 1], r.nts.at[ahead - 1], r.ntr.at[ahead - 1], to)

    for ahead in range(1, 2 * chips):
        norm_tp(ahead).start()

    pl.when(place.has_next)(lambda: shifts(lambda copy: copy.wait_recv()))
    for part in range(n):
        rows = pl.ds(part * CHUNK, CHUNK)
        mine_rows = pl.ds(pl.multiple_of(place.x * piece + part * CHUNK, CHUNK), CHUNK)
        hat, inv_std = hat_of(half[mine_rows, :].astype(F32))
        rows_in = sums.own_total(part) + r.shift_in[rows, :].astype(F32)
        rows_in, _, _ = norm_back(rows_in, hat, inv_std, r.gain[...])
        r.grad[rows, :] = r.grad_own[rows, :] + rows_in
    seq_up.finish(r.sum_up)
    seq_cross.finish(r.sum_w)
    for ahead in range(1, SeqSum.ROWS):
        page_far(ahead).wait_recv()
        r.page_sum[...] = r.page_sum[...] + r.page_far[ahead - 1].astype(F32)
    r.grad_mem[...] = r.page_sum[: r.grad_mem.shape[0], :]
    seq_self.finish(r.sum_self)
    rows = r.norm_sum[...]
    for ahead in range(1, 2 * chips):
        norm_tp(ahead).wait_recv()
        rows = rows + r.norm_tp[ahead - 1]
    r.norms[...] = rows

    for ahead in range(1, 2 * chips):
        norm_tp(ahead).wait_send()
    for chip in range(chips):
        mem_near(chip).wait_send()
    for ahead in range(1, chips):
        mem_far(ahead).wait_send()
    for seq_sum in (seq_cross, seq_self):
        seq_sum.end()
    seq_up.end(near=False)
    for ahead in range(1, seqs):
        norm_seq(ahead).wait_send()
    for ahead in range(1, inner):
        page_near(ahead).wait_send()
    for ahead in range(1, SeqSum.ROWS):
        page_far(ahead).wait_send()
    sums_prev.own_end()
    sums.own_end()
    pl.when(place.has_prev)(lambda: shifts(lambda copy: copy.wait_send()))


def closing(chips, seqs, ids, offsets, a, f, e, mem_true, w):
    tokens, width = a.q.shape
    dim = w.attn_output.shape[1]
    blocks = tokens // BLOCK
    own = tokens // (2 * chips)
    mem_rows, wide = e.mem_part.shape[1:]
    rows, inner = SeqSum.ROWS, seqs // SeqSum.ROWS
    keys = mem_rows // blocks
    dma = pltpu.SemaphoreType.DMA
    vmem = lambda array: (array, "vmem")
    late = lambda array: (array, "late")
    hbm = lambda array: (array, "hbm")
    return call(
        functools.partial(close_body, chips, seqs),
        "closing",
        dict(
            ids=(ids, "smem"),
            offsets=(offsets, "smem"),
            up_own=hbm(e.up_own),
            up_low=hbm(e.up_low),
            g_w=hbm(e.g_w),
            mem_part=hbm(e.mem_part),
            g_in=vmem(e.g),
            wo=vmem(w.attn_output),
            q=vmem(a.q),
            kext=vmem(a.kext),
            vext=vmem(a.vext),
            mixed=vmem(f.mixed1),
            lse=vmem(f.lse1),
            wq=vmem(w.attn_query),
            wk=vmem(w.attn_key),
            wv=vmem(w.attn_value),
            gain=vmem(w.self_gain),
            norm_cross=vmem(e.norm),
            norm_ffn=vmem(f.norm),
            pages=vmem(a.pages),
            n1=late(a.n1),
            half=late(a.half),
            prev=late(a.prev),
            grad_in=hbm(e.grad),
        ),
        dict(
            grad=((own, dim), F32, "vmem"),
            norms=((8, dim // seqs), F32, "vmem"),
            sum_up=((dim // seqs, e.up_own.shape[1]), F32, "vmem"),
            sum_w=((dim // seqs, 4 * width), F32, "vmem"),
            sum_self=((dim // seqs, 4 * width), F32, "vmem"),
            grad_mem=((mem_true, wide), F32, "vmem"),
        ),
        dict(
            **sum_scratch(chips, tokens, dim, "prev_"),
            **sum_scratch(chips, tokens, dim),
            **SeqSum.scratch(seqs, (dim // seqs, 4 * width), BF16, "cross_"),
            **SeqSum.scratch(seqs, (dim // seqs, 4 * width), BF16, "self_"),
            **SeqSum.scratch(seqs, (dim // seqs, e.up_own.shape[1]), BF16, "up_", near=False),
            norm_seq=pltpu.VMEM((seqs - 1, 8, dim // seqs), F32),
            nss=dma((seqs - 1,)),
            nsr=dma((seqs - 1,)),
            page_out=pltpu.VMEM((inner - 1, blocks, keys, wide), BF16),
            page_in=pltpu.VMEM((inner - 1, blocks, keys, wide), BF16),
            page_low=pltpu.VMEM((rows - 1, keys, wide), BF16),
            page_far=pltpu.VMEM((rows - 1, keys, wide), BF16),
            page_sum=pltpu.VMEM((keys, wide), F32),
            pns=dma((inner - 1,)),
            pnr=dma((inner - 1,)),
            pfs=dma((rows - 1,)),
            pfr=dma((rows - 1,)),
            causal=pltpu.VMEM((BLOCK, BLOCK), F32),
            dout=pltpu.VMEM((tokens, width), BF16),
            dots=pltpu.VMEM((width // PAIR, 8, tokens), F32),
            dq=pltpu.VMEM((tokens, width), F32),
            dk=pltpu.VMEM((2 * tokens, width), F32),
            dv=pltpu.VMEM((2 * tokens, width), F32),
            gq=pltpu.VMEM((tokens, width), BF16),
            gkv=pltpu.VMEM((2, 2 * tokens, width), BF16),
            g_self=pltpu.VMEM((dim, 4 * width), BF16),
            grad_own=pltpu.VMEM((own, dim), F32),
            part=pltpu.VMEM((chips, mem_rows, wide), BF16),
            fetch=dma((2 + chips + rows,)),
            shift_out=pltpu.VMEM((own, dim), BF16),
            shift_in=pltpu.VMEM((own, dim), BF16),
            ks=dma((own // CHUNK,)),
            kr=dma((own // CHUNK,)),
            mem_mate=pltpu.VMEM((chips, mem_rows, wide), BF16),
            mem_far=pltpu.VMEM((chips - 1, mem_rows, wide), BF16),
            mem_sum=pltpu.VMEM((mem_rows, wide), F32),
            mns=dma((chips,)),
            mnr=dma((chips,)),
            mfs=dma((chips - 1,)),
            mfr=dma((chips - 1,)),
            norm_out=pltpu.VMEM((seqs, 8, dim // seqs), F32),
            norm_sum=pltpu.VMEM((8, dim // seqs), F32),
            norm_tp=pltpu.VMEM((2 * chips - 1, 8, dim // seqs), F32),
            nts=dma((2 * chips - 1,)),
            ntr=dma((2 * chips - 1,)),
        ),
        3,
        20 * tokens * 3 * BLOCK * width,
    )


def layout_body(width, per_tp, sum_self, sum_w, sum_up, sum_down, grad, out, grad_mem, norms, *results):
    (out_out, grad_out, mem_out, *weights, up_out, down_out) = results[:-6]
    out_out[...] = out[...]
    grad_out[...] = grad[...]
    mem_out[0] = grad_mem[...]
    for index, ref in enumerate(weights):
        source, piece = (sum_self, sum_w)[index // 4], index % 4
        values = source[:, piece * width : (piece + 1) * width]
        ref[...] = jnp.transpose(values) if piece == 3 else values
    up_out[...] = sum_up[...]
    down_out[...] = jnp.transpose(sum_down[...])
    columns = norms.shape[1]
    first = lax.axis_index("tp") * per_tp
    from_column = lax.broadcasted_iota(jnp.int32, (columns, per_tp), 0)
    to_column = lax.broadcasted_iota(jnp.int32, (columns, per_tp), 1)
    pick = (from_column == to_column + first).astype(F32)
    mine = jnp.dot(norms[...], pick, precision=lax.Precision.HIGHEST, preferred_element_type=F32)
    for row, ref in enumerate(results[-6:]):
        ref[...] = mine[row : row + 1, :]


def layout(tps, width, c, e):
    share_rows, hidden = c.sum_up.shape
    own, dim = c.grad.shape
    per_tp = share_rows // tps
    weights = [(share_rows, width)] * 3 + [(width, share_rows)]
    dims = [(own, dim), (own, dim), (1, *c.grad_mem.shape), *weights, *weights, (share_rows, hidden), (hidden, share_rows)]
    types = [BF16] + [F32] * (len(dims) - 1)
    dims += [(1, per_tp)] * 6
    types += [F32] * 6
    return pl.pallas_call(
        functools.partial(layout_body, width, per_tp),
        name="layout",
        out_shape=[jax.ShapeDtypeStruct(d, t) for d, t in zip(dims, types)],
        in_specs=[VMEM] * 8,
        out_specs=[VMEM] * len(dims),
        compiler_params=pltpu.CompilerParams(vmem_limit_bytes=32 << 20),
    )(c.sum_self, c.sum_w, c.sum_up, e.sum_down, c.grad, e.out, c.grad_mem, c.norms)


def on_device(
    hidden_in,
    memory,
    page_ids,
    token_offsets,
    memory_mask,
    attn_query,
    attn_key,
    attn_value,
    attn_output,
    cross_query,
    cross_key,
    cross_value,
    cross_output,
    ffn_up,
    ffn_down,
    self_gain,
    self_shift,
    cross_gain,
    cross_shift,
    ffn_gain,
    ffn_shift,
    out_grad,
):
    tps, seqs = lax.axis_size("tp"), lax.axis_size("seq")
    chips = tps // 2
    width = attn_query.shape[1]
    w = Refs()
    w.attn_query, w.attn_key, w.attn_value, w.attn_output = attn_query, attn_key, attn_value, attn_output
    w.cross_query, w.cross_key, w.cross_value, w.cross_output = cross_query, cross_key, cross_value, cross_output
    w.up, w.down = ffn_up, ffn_down
    w.self_gain, w.self_shift = self_gain.reshape(1, -1), self_shift.reshape(1, -1)
    w.cross_gain, w.cross_shift = cross_gain.reshape(1, -1), cross_shift.reshape(1, -1)
    w.ffn_gain, w.ffn_shift = ffn_gain.reshape(1, -1), ffn_shift.reshape(1, -1)

    a = opening(
        chips,
        seqs,
        page_ids,
        hidden_in,
        out_grad,
        memory,
        memory_mask,
        w.self_gain,
        w.self_shift,
        attn_query,
        attn_key,
        attn_value,
    )
    f = forward(chips, seqs, page_ids, token_offsets, a, w)
    e = cross_back(chips, seqs, a, f, w)
    c = closing(chips, seqs, page_ids, token_offsets, a, f, e, memory.shape[1], w)
    results = layout(tps, width, c, e)
    return (
        results[0],
        results[1],
        results[2],
        *results[3:11],
        results[11],
        results[12],
        *[values.reshape(-1) for values in results[13:]],
    )


def solution(mesh):
    both = ("seq", "tp")
    in_specs = (
        P(both, None),
        P("seq", None, None),
        P("seq"),
        P("seq"),
        P("seq", None),
        P(None, "tp"),
        P(None, "tp"),
        P(None, "tp"),
        P("tp", None),
        P(None, "tp"),
        P(None, "tp"),
        P(None, "tp"),
        P("tp", None),
        P(None, "tp"),
        P("tp", None),
        P(),
        P(),
        P(),
        P(),
        P(),
        P(),
        P(both, None),
    )
    out_specs = (
        P(both, None),
        P(both, None),
        P("seq", None, "tp"),
        P("seq", "tp"),
        P("seq", "tp"),
        P("seq", "tp"),
        P("tp", "seq"),
        P("seq", "tp"),
        P("seq", "tp"),
        P("seq", "tp"),
        P("tp", "seq"),
        P("seq", "tp"),
        P("tp", "seq"),
        P(both),
        P(both),
        P(both),
        P(both),
        P(both),
        P(both),
    )
    return jax.shard_map(on_device, mesh=mesh, in_specs=in_specs, out_specs=out_specs, check_vma=False)
```

```python
import functools

import jax
import jax.numpy as jnp
from jax import lax
from jax.experimental import pallas as pl
from jax.experimental.pallas import tpu as pltpu
from jax.sharding import PartitionSpec as P

HEAD_DIM = 64
PAIR = 2 * HEAD_DIM
BLOCK = 512
REACH = 2
CHUNK = 128
EPS = 1e-05
NEG = -1e30
F32 = jnp.float32
BF16 = jnp.bfloat16
MESH = pl.DeviceIdType.MESH
VMEM = pl.BlockSpec(memory_space=pltpu.VMEM)
SMEM = pl.BlockSpec(memory_space=pltpu.SMEM)


def dot(left, right):
    return jnp.dot(left, right, preferred_element_type=F32)


def dot_nt(left, right):
    return lax.dot_general(left, right, (((1,), (1,)), ((), ())), preferred_element_type=F32)


def dot_tn(left, right):
    return lax.dot_general(left, right, (((0,), (0,)), ((), ())), preferred_element_type=F32)


def hat_of(rows):
    center = rows - jnp.mean(rows, axis=-1, keepdims=True)
    inv_std = lax.rsqrt(jnp.mean(center * center, axis=-1, keepdims=True) + EPS)
    return center * inv_std, inv_std


def norm_back(grad_rows, hat, inv_std, gain):
    grad_hat = grad_rows * gain
    inner = jnp.mean(grad_hat * hat, axis=-1, keepdims=True)
    grad_input = inv_std * (grad_hat - jnp.mean(grad_hat, axis=-1, keepdims=True) - hat * inner)
    gain_sum = jnp.sum(grad_rows * hat, axis=0, keepdims=True)
    shift_sum = jnp.sum(grad_rows, axis=0, keepdims=True)
    return grad_input, gain_sum, shift_sum


def remote(src, dst, send_sem, recv_sem, device):
    return pltpu.make_async_remote_copy(
        src_ref=src, dst_ref=dst, send_sem=send_sem, recv_sem=recv_sem, device_id=device, device_id_type=MESH
    )


class Late:
    def __init__(self, hbm, ref, sem, out):
        self.hbm, self.ref, self.sem, self.out, self.started, self.waited = hbm, ref, sem, out, False, False

    def copy(self):
        ends = (self.ref, self.hbm) if self.out else (self.hbm, self.ref)
        return pltpu.make_async_copy(*ends, self.sem)

    def start(self):
        self.copy().start()
        self.started = True

    def wait(self):
        if self.started and not self.waited:
            self.copy().wait()
            self.waited = True
        return self.ref


class Refs:
    pass


def call(body, name, ins, outs, scratch, collective_id, flops):
    dma = pltpu.SemaphoreType.DMA
    specs = {"vmem": VMEM, "smem": SMEM, "hbm": pl.BlockSpec(memory_space=pltpu.HBM)}
    specs["late"] = specs["hbm"]
    late_in = [key for key, (_, mode) in ins.items() if mode == "late"]
    late_out = [key for key, (_, _, mode) in outs.items() if mode == "late"]
    places = [pltpu.VMEM(ins[key][0].shape, ins[key][0].dtype) for key in late_in]
    places += [pltpu.VMEM(outs[key][0], outs[key][1]) for key in late_out]
    lates = len(places)

    def kernel(*refs):
        r = Refs()
        count = len(ins) + len(outs)
        for key, ref in zip([*ins, *outs], refs[:count]):
            setattr(r, key, ref)
        for key, ref in zip(scratch, refs[count : count + len(scratch)]):
            setattr(r, key, ref)
        rest = refs[count + len(scratch) :]
        all_late = []
        for index, key in enumerate(late_in + late_out):
            late = Late(getattr(r, key), rest[index], rest[-1].at[index], index >= len(late_in))
            setattr(r, key, late)
            all_late.append(late)
            if not late.out:
                late.start()
        body(r)
        for late in all_late:
            late.wait()

    result = pl.pallas_call(
        kernel,
        name=name,
        out_shape=[jax.ShapeDtypeStruct(dims, dtype) for dims, dtype, _ in outs.values()],
        in_specs=[specs[mode] for _, mode in ins.values()],
        out_specs=[specs[mode] for _, _, mode in outs.values()],
        scratch_shapes=[*scratch.values(), *places] + ([dma((lates,))] if lates else []),
        cost_estimate=pl.CostEstimate(flops=flops, bytes_accessed=16 << 20, transcendentals=0),
        compiler_params=pltpu.CompilerParams(
            collective_id=collective_id, has_side_effects=True, vmem_limit_bytes=62 << 20
        ),
    )(*[array for array, _ in ins.values()])
    out = Refs()
    for key, value in zip(outs, result):
        setattr(out, key, value)
    return out


def loop(count, step):
    lax.fori_loop(0, count, lambda index, carry: (step(index), carry)[1], 0)


class Place:
    def __init__(self, chips, seqs, rows):
        self.chips, self.seqs = chips, seqs
        self.piece = rows // (2 * chips)
        self.per_piece = self.piece // CHUNK
        self.chunks = chips * self.per_piece
        self.tp = lax.axis_index("tp")
        self.seq = lax.axis_index("seq")
        self.x = self.tp // 2
        self.core = lax.rem(self.tp, 2)
        self.mate = {"tp": self.x * 2 + 1 - self.core}
        self.has_prev, self.has_next = self.seq > 0, self.seq < seqs - 1

    def chip(self, ahead):
        return lax.rem(self.x + ahead, self.chips)

    def peer(self, ahead):
        return {"tp": self.chip(ahead) * 2 + self.core}

    def shard(self, ahead):
        return lax.rem(self.seq + ahead, self.seqs)

    def piece_row(self, chip, core):
        return pl.multiple_of((chip * 2 + core) * self.piece, CHUNK)

    def row(self, slot, core):
        chip, part = slot // self.per_piece, lax.rem(slot, self.per_piece)
        return pl.multiple_of((chip * 2 + core) * self.piece + part * CHUNK, CHUNK)

    def enter(self, seq="", all_tp=False):
        barrier = pltpu.get_barrier_semaphore()

        def greet(device):
            pl.semaphore_signal(barrier, inc=1, device_id=device, device_id_type=MESH)

        count = self.chips
        if all_tp:
            count = 2 * self.chips - 1
            for ahead in range(1, 2 * self.chips):
                greet({"tp": lax.rem(self.tp + ahead, 2 * self.chips)})
        else:
            greet(self.mate)
            for ahead in range(1, self.chips):
                greet(self.peer(ahead))
        if seq == "all":
            for ahead in range(1, self.seqs):
                greet({"seq": self.shard(ahead)})
            count = count + self.seqs - 1
        if seq == "row":
            inner = self.seqs // SeqSum.ROWS
            for ahead in range(1, inner):
                greet({"seq": self.seq // inner * inner + lax.rem(self.seq + ahead, inner)})
            count = count + inner - 1
        pl.semaphore_wait(barrier, count)


def sum_scratch(chips, rows, width, name="sums_", stages=1):
    chunks = rows // 2 // CHUNK
    dma = pltpu.SemaphoreType.DMA
    specs = [
        pltpu.VMEM((chunks, CHUNK, width), BF16),
        pltpu.VMEM((chunks, CHUNK, width), BF16),
        pltpu.VMEM((chunks, CHUNK, width), F32),
        dma((chunks,)),
        dma((chunks,)),
        pltpu.VMEM((stages, chips - 1, chunks, CHUNK, width), BF16),
        dma((stages, chips - 1, chunks)),
        dma((stages, chips - 1, chunks)),
    ]
    return {name + str(index): spec for index, spec in enumerate(specs)}


class Sums:
    def __init__(self, place, r, name="sums_", stage=0):
        self.place, self.stage = place, stage
        (self.out, self.mate, self.own, self.s1, self.r1, self.far, self.s2, self.r2) = [
            getattr(r, name + str(index)) for index in range(8)
        ]
        self.low = self.mate

    def core_copy(self, slot):
        return remote(self.out.at[slot], self.mate.at[slot], self.s1.at[slot], self.r1.at[slot], self.place.mate)

    def far_copy(self, ahead, slot):
        at = (self.stage, ahead - 1, slot)
        return remote(self.low.at[slot], self.far.at[at], self.s2.at[at], self.r2.at[at], self.place.peer(ahead))

    def near(self, slot, who, rows):
        n = self.place.per_piece

        @pl.when(who == 0)
        def _():
            for part in range(n):
                self.out[slot + part] = rows[part * CHUNK : (part + 1) * CHUNK].astype(BF16)
                self.core_copy(slot + part).start()

        @pl.when(who == 1)
        def _():
            for part in range(n):
                self.core_copy(slot + part).wait_recv()
                self.own[slot + part] = rows[part * CHUNK : (part + 1) * CHUNK] + self.mate[slot + part].astype(F32)

    def all_pieces(self, first, count, term):
        place = self.place
        n = place.per_piece

        def step(index):
            chip, who = first + index // 2, lax.rem(index, 2)
            core = jnp.where(who == 0, 1 - place.core, place.core)
            self.near(chip * n, who, term(place.piece_row(chip, core)))

            @pl.when(who == 1)
            def _():
                for part in range(n):
                    self.low[chip * n + part] = self.own[chip * n + part].astype(BF16)
                    for ahead in range(1, place.chips):
                        self.far_copy(ahead, chip * n + part).start()

        loop(2 * count, step)

    def take(self, slot):
        rows = self.own[slot]
        for ahead in range(1, self.place.chips):
            self.far_copy(ahead, slot).wait_recv()
            rows = rows + self.far[self.stage, ahead - 1, slot].astype(F32)
        self.core_copy(slot).wait_send()
        for ahead in range(1, self.place.chips):
            self.far_copy(ahead, slot).wait_send()
        return rows

    def own_pieces(self, term, go=True):
        place = self.place
        n = place.per_piece

        def step(index):
            ahead, who = lax.rem(index // 2 + 1, place.chips), lax.rem(index, 2)
            core = jnp.where(who == 0, 1 - place.core, place.core)
            self.near(ahead * n, who, term(place.piece_row(place.chip(ahead), core)))

            @pl.when(jnp.logical_and(who == 1, ahead > 0))
            def _():
                for part in range(n):
                    self.low[ahead * n + part] = self.own[ahead * n + part].astype(BF16)
                    if go:
                        self.far_copy(ahead, ahead * n + part).start()

        loop(2 * place.chips, step)

    def own_total(self, part):
        n = self.place.per_piece
        rows = self.own[part]
        for ahead in range(1, self.place.chips):
            slot = ahead * n + part
            self.far_copy(ahead, slot).wait_recv()
            rows = rows + self.far[self.stage, ahead - 1, slot].astype(F32)
        return rows

    def own_end(self, far=True):
        n = self.place.per_piece
        for slot in range(self.place.chunks):
            self.core_copy(slot).wait_send()
            if far and slot >= n:
                self.far_copy(slot // n, slot).wait_send()


class Share:
    def __init__(self, place, ref, send_sems, recv_sems, stage=0):
        self.place, self.ref, self.s, self.r, self.stage = place, ref, send_sems, recv_sems, stage

    def copy(self, slot):
        rows = pl.ds(self.place.row(slot, self.place.core), CHUNK)
        at = (self.stage, slot)
        return remote(self.ref.at[rows], self.ref.at[rows], self.s.at[at], self.r.at[at], self.place.mate)

    def put(self, slot, rows):
        self.ref[pl.ds(self.place.row(slot, self.place.core), CHUNK), :] = rows
        self.copy(slot).start()

    def end(self, first, count):
        loop(count, lambda index: self.copy(first + index).wait())


class Gather:
    def __init__(self, place, own, ref, parts, sems):
        self.place, self.own, self.ref, self.parts = place, own, ref, parts
        self.size = own.shape[0] // parts
        self.s1, self.r1, self.s2, self.r2, self.local = sems

    @staticmethod
    def scratch(chips, parts, name):
        dma = pltpu.SemaphoreType.DMA
        specs = [dma((chips, parts)), dma((chips, parts)), dma((chips - 1, parts)), dma((chips - 1, parts)), dma((1,))]
        return {name + str(index): spec for index, spec in enumerate(specs)}

    def far(self, ahead, part):
        rows = pl.ds(part * self.size, self.size)
        sems = (self.s2.at[ahead - 1, part], self.r2.at[ahead - 1, part])
        return remote(self.own.at[rows], self.ref.at[self.place.tp, rows], *sems, self.place.peer(ahead))

    def near(self, ahead, part):
        place = self.place
        rows = pl.ds(part * self.size, self.size)
        device = lax.rem(place.x + place.chips - ahead, place.chips) * 2 + place.core
        src = self.ref.at[device, rows] if ahead else self.own.at[rows]
        sems = (self.s1.at[ahead, part], self.r1.at[ahead, part])
        return remote(src, self.ref.at[device, rows], *sems, place.mate)

    def keep(self):
        return pltpu.make_async_copy(self.own, self.ref.at[self.place.tp], self.local.at[0])

    def start(self):
        self.keep().start()
        for part in range(self.parts):
            for ahead in range(1, self.place.chips):
                self.far(ahead, part).start()
            self.near(0, part).start()

    def relay(self):
        for ahead in range(1, self.place.chips):
            for part in range(self.parts):
                self.far(ahead, part).wait_recv()
                self.near(ahead, part).start()

    def end(self):
        self.keep().wait()
        for part in range(self.parts):
            for ahead in range(self.place.chips):
                self.near(ahead, part).wait_recv()

    def drain(self):
        for part in range(self.parts):
            for ahead in range(1, self.place.chips):
                self.far(ahead, part).wait_send()
            for ahead in range(self.place.chips):
                self.near(ahead, part).wait_send()


class SeqSum:
    ROWS = 4

    def __init__(self, place, slot, r, name):
        self.place, self.slot = place, slot
        self.near_recv, self.ns, self.nr, self.low, self.mid, self.first, self.second, self.fs, self.fr = [
            getattr(r, name + str(index), None) for index in range(9)
        ]
        self.inner = place.seqs // self.ROWS
        self.row, self.column = place.seq // self.inner, lax.rem(place.seq, self.inner)

    @staticmethod
    def scratch(seqs, dims, dtype, name, near=True, low=True, far=True):
        dma = pltpu.SemaphoreType.DMA
        rows, inner = SeqSum.ROWS, seqs // SeqSum.ROWS
        specs = [
            pltpu.VMEM((inner - 1, rows, *dims), dtype) if near else None,
            dma((inner - 1, rows)) if near else None,
            dma((inner - 1, rows)) if near else None,
            pltpu.VMEM((rows, *dims), dtype) if low else None,
            pltpu.VMEM(dims, dtype) if far else None,
            pltpu.VMEM((2, *dims), dtype) if far else None,
            pltpu.VMEM((1, *dims), dtype) if far else None,
            dma((3,)) if far else None,
            dma((3,)) if far else None,
        ]
        return {name + str(index): spec for index, spec in enumerate(specs) if spec is not None}

    def other_row(self, differs):
        bit, half = lax.rem(self.row, 2), self.row // 2
        return (self.row, self.row + 1 - 2 * bit, self.row + 2 - 4 * half, 3 - self.row)[differs]

    def shard(self, differs, column_ahead=0):
        return self.other_row(differs) * self.inner + lax.rem(self.column + column_ahead, self.inner)

    def near(self, ahead, differs):
        at = (ahead - 1, differs)
        to = {"seq": self.shard(0, ahead)}
        return remote(self.slot(self.shard(differs, ahead)), self.near_recv.at[at], self.ns.at[at], self.nr.at[at], to)

    def each_near(self, act):
        for ahead in range(1, self.inner):
            for differs in (1, 3, 2, 0):
                act(self.near(ahead, differs))

    def start(self):
        self.each_near(lambda copy: copy.start())

    def exchange(self, index):
        sems = (self.fs.at[index], self.fr.at[index])
        if index == 2:
            return remote(self.mid, self.second.at[0], *sems, {"seq": self.shard(2)})
        return remote(self.low.at[(1, 3)[index]], self.first.at[index], *sems, {"seq": self.shard(1)})

    def fetch(self, sems):
        return [
            pltpu.make_async_copy(self.slot(self.shard(differs)), self.low.at[differs], sems.at[differs])
            for differs in range(self.ROWS)
        ]

    def column_rows(self, differs, fetched):
        rows = (self.low.at[differs] if fetched else self.slot(self.shard(differs)))[...].astype(F32)
        for ahead in range(1, self.inner):
            self.near(ahead, differs).wait_recv()
            rows = rows + self.near_recv[ahead - 1, differs].astype(F32)
        return rows

    def combine(self, out, fetched=False, rows_of=None, go=True):
        rows_of = rows_of or (lambda differs: self.column_rows(differs, fetched))
        for differs in (1, 3):
            self.low[differs] = rows_of(differs).astype(self.low.dtype)
            if go:
                self.exchange(differs // 2).start()
        if go:
            self.mid[...] = rows_of(2).astype(self.mid.dtype)
        else:
            self.low[2] = rows_of(2).astype(self.low.dtype)
        out[...] = rows_of(0)

    def middle(self, out):
        self.exchange(1).wait_recv()
        self.mid[...] = (self.mid[...].astype(F32) + self.first[1].astype(F32)).astype(self.mid.dtype)
        self.exchange(2).start()
        self.exchange(0).wait_recv()
        out[...] = out[...] + self.first[0].astype(F32)

    def finish(self, out):
        self.exchange(2).wait_recv()
        out[...] = out[...] + self.second[0].astype(F32)

    def end(self, near=True, far=True):
        if near:
            self.each_near(lambda copy: copy.wait_send())
        if far:
            for index in range(3):
                self.exchange(index).wait_send()


def head_masks():
    lane = lax.broadcasted_iota(jnp.int32, (1, PAIR), 1)
    first = (lane < HEAD_DIM).astype(F32)
    return first, 1.0 - first


def pair_lanes(pair):
    return pl.ds(pl.multiple_of(pair * PAIR, PAIR), PAIR)


def block_rows(block):
    return pl.ds(pl.multiple_of(block * BLOCK, BLOCK), BLOCK)


def causal_tile(keys_first):
    rows = lax.broadcasted_iota(jnp.int32, (BLOCK, BLOCK), 0)
    columns = lax.broadcasted_iota(jnp.int32, (BLOCK, BLOCK), 1)
    allowed = rows <= columns if keys_first else columns <= rows
    return jnp.where(allowed, 0.0, NEG)


def attend(q_ref, block, keys, values, biases, mixed_ref, lse_ref):
    masks = head_masks()
    rows = block_rows(block)
    lane = lax.broadcasted_iota(jnp.int32, (BLOCK, 128), 1)

    def step(pair):
        lanes = pair_lanes(pair)
        queries = q_ref[rows, lanes]
        pair_out = jnp.zeros((BLOCK, PAIR), F32)
        lse_block = jnp.zeros((BLOCK, 128), F32)
        for head in range(2):
            head_queries = queries * masks[head].astype(BF16)
            scores = [dot_nt(head_queries, keys(tile, lanes)) + bias() for tile, bias in enumerate(biases)]
            top = functools.reduce(jnp.maximum, [jnp.max(s, axis=-1, keepdims=True) for s in scores])
            total, out = 0.0, 0.0
            for tile, s in enumerate(scores):
                weights = jnp.exp(s - top)
                total = total + jnp.sum(weights, axis=-1, keepdims=True)
                out = out + dot(weights.astype(BF16), values(tile, lanes))
            pair_out = pair_out + out * masks[head] / total
            lse_block = jnp.where(lane == head, top + jnp.log(total), lse_block)
        mixed_ref[rows, lanes] = pair_out.astype(BF16)
        lse_ref[pair, :, rows] = jnp.transpose(lse_block)[:8]

    loop(q_ref.shape[1] // PAIR, step)


def dots_out(grad_ref, mixed_ref, block, dots_ref):
    masks = head_masks()
    rows = block_rows(block)
    lane = lax.broadcasted_iota(jnp.int32, (BLOCK, 128), 1)
    for pair in range(grad_ref.shape[1] // PAIR):
        lanes = pair_lanes(pair)
        product = grad_ref[rows, lanes].astype(F32) * mixed_ref[rows, lanes].astype(F32)
        values = jnp.zeros((BLOCK, 128), F32)
        for head in range(2):
            value = jnp.sum(product * masks[head], axis=-1, keepdims=True)
            values = jnp.where(lane == head, value, values)
        dots_ref[pair, :, rows] = jnp.transpose(values)[:8]


def attend_back(q_ref, grad_ref, lse_ref, dots_ref, block, pair, keys, values, bias):
    masks = head_masks()
    lanes, rows = pair_lanes(pair), block_rows(block)
    queries, grads = q_ref[rows, lanes], grad_ref[rows, lanes]
    dq = dk = dv = 0.0
    for head in range(2):
        mask = masks[head].astype(BF16)
        head_queries, head_grads, head_keys = queries * mask, grads * mask, keys * mask
        scores = dot_nt(keys, head_queries) + bias()
        weights = jnp.exp(scores - lse_ref[pair, head : head + 1, rows])
        grad_weights = dot_nt(values, head_grads)
        grad_scores = (weights * (grad_weights - dots_ref[pair, head : head + 1, rows])).astype(BF16)
        dv = dv + dot(weights.astype(BF16), head_grads)
        dk = dk + dot(grad_scores, head_queries)
        dq = dq + dot_tn(grad_scores, head_keys)
    return dq * HEAD_DIM ** (-0.5), dk, dv


def grad_weight(out_ref, first, left_ref, *rights):
    count = left_ref.shape[1]
    step_size = min(256, count)
    width = sum(right.shape[1] for right in rights)

    def step(index):
        columns = pl.ds(pl.multiple_of(index * step_size, step_size), step_size)
        right = rights[0][...] if len(rights) == 1 else jnp.concatenate([right[...] for right in rights], axis=1)
        out_ref[columns, first : first + width] = dot_tn(left_ref[:, columns], right).astype(BF16)

    loop(count // step_size, step)


def scaled(queries):
    return (queries.astype(BF16).astype(F32) * HEAD_DIM ** (-0.5)).astype(BF16)


def half_rows(slot):
    return pl.ds(pl.multiple_of(slot * CHUNK, CHUNK), CHUNK)


def reach_bias(offsets, block, tile):
    return jnp.where(offsets[block * BLOCK] >= (REACH - tile) * BLOCK, 0.0, NEG)


def norm_step(place, r, sums, share, base, res):
    def finish(slot, carry):
        hat, inv_std = hat_of(res[half_rows(slot), :])
        grad_in, gain_sum, shift_sum = norm_back(sums.take(slot), hat, inv_std, r.gain[...])
        rows = base(slot) + grad_in
        r.grad.ref[half_rows(slot), :] = rows
        share.put(slot, rows.astype(BF16))
        return carry[0] + gain_sum, carry[1] + shift_sum

    zero = jnp.zeros((1, r.gain.shape[1]), F32)
    gain_sum, shift_sum = lax.fori_loop(0, place.chunks, finish, (zero, zero))
    r.norm[0:1, :] = gain_sum
    r.norm[1:2, :] = shift_sum


def open_body(chips, seqs, r):
    n1, half = r.n1.ref, (r.half.ref, r.prev.ref)
    tokens = n1.shape[0] // 2
    place = Place(chips, seqs, tokens)
    place.enter(seq="all")
    n, piece = place.per_piece, place.piece
    own_rows = pl.ds(pl.multiple_of(place.x * piece, CHUNK), piece)

    def half_part(chip, part):
        return pl.ds(pl.multiple_of(chip * piece + part * CHUNK, CHUNK), CHUNK)

    def far(which, ahead, part):
        dst = half[which].at[half_part(place.x, part)]
        src = dst if which else r.x.at[pl.ds(part * CHUNK, CHUNK)]
        at = (which, ahead - 1, part)
        return remote(src, dst, r.s2.at[at], r.r2.at[at], place.peer(ahead))

    def pass_on(part):
        src, dst = r.x.at[pl.ds(part * CHUNK, CHUNK)], half[1].at[half_part(place.x, part)]
        return remote(src, dst, r.ss.at[part], r.sr.at[part], {"seq": place.seq + 1})

    def parts(act):
        for part in range(n):
            act(part)

    pl.when(place.has_next)(lambda: parts(lambda part: pass_on(part).start()))
    for part in range(n):
        for ahead in range(1, chips):
            far(0, ahead, part).start()
    grads = Gather(place, r.og_own, r.og, n, [getattr(r, "og_" + str(i)) for i in range(5)])
    grads.start()

    columns = pl.ds(pl.multiple_of(place.tp * r.mem.shape[3], 128), r.mem.shape[3])
    rows_apart = SeqSum.ROWS
    inner = seqs // rows_apart
    seq_row, seq_column = place.seq // inner, lax.rem(place.seq, inner)

    def mem_far(ahead):
        to = {"seq": lax.rem(seq_row + ahead, rows_apart) * inner + seq_column}
        sems = (r.fs.at[ahead - 1], r.fr.at[ahead - 1])
        return remote(r.memory.at[0, :, columns], r.mem.at[place.seq, 0], *sems, to)

    def mem_near(behind, ahead):
        row = lax.rem(seq_row + rows_apart - behind, rows_apart)
        to = {"seq": seq_row * inner + lax.rem(seq_column + ahead, inner)}
        dst = r.mem.at[row * inner + seq_column, 0]
        src = dst if behind else r.memory.at[0, :, columns]
        sems = (r.ns.at[behind, ahead - 1], r.nr.at[behind, ahead - 1])
        return remote(src, dst, *sems, to)

    def mem_pass(behind):
        mem_far(behind).wait_recv()
        for ahead in range(1, inner):
            mem_near(behind, ahead).start()

    def known_copies(ahead):
        to = {"seq": place.shard(ahead)}
        at = [(which, ahead - 1) for which in range(2)]
        return (
            remote(r.mask, r.masks.at[place.seq], r.ms.at[at[0]], r.mr.at[at[0]], to),
            remote(r.page_row, r.pages.at[place.seq], r.ms.at[at[1]], r.mr.at[at[1]], to),
        )

    def known_all(act):
        def step(index):
            for copy in known_copies(index + 1):
                act(copy)

        loop(seqs - 1, step)

    lane = lax.broadcasted_iota(jnp.int32, r.page_row.shape, 1)
    page_row = jnp.zeros(r.page_row.shape, jnp.int32)
    for block in range(tokens // BLOCK):
        page_row = jnp.where(lane == block, r.ids[block * BLOCK], page_row)
    r.page_row[...] = page_row
    own_copies = [
        pltpu.make_async_copy(r.memory.at[0, :, columns], r.mem.at[place.seq, 0], r.local.at[0]),
        pltpu.make_async_copy(r.mask, r.masks.at[place.seq], r.local.at[1]),
        pltpu.make_async_copy(r.page_row, r.pages.at[place.seq], r.local.at[2]),
    ]
    for copy in own_copies:
        copy.start()
    for ahead in (1, 3, 2):
        mem_far(ahead).start()
    for ahead in range(1, inner):
        mem_near(0, ahead).start()
    known_all(lambda copy: copy.start())
    half[0][own_rows, :] = r.x[...]

    def from_chip(ahead):
        return lax.rem(place.x + chips - ahead, chips)

    def near(which, ahead, part):
        row = pl.multiple_of((from_chip(ahead) * 2 + place.core) * piece + part * CHUNK, CHUNK)
        rows = n1.at[pl.ds((1 - which) * tokens + row, CHUNK)]
        at = (which, ahead, part)
        return remote(rows, rows, r.s1.at[at], r.r1.at[at], place.mate)

    def normed(which, ahead, part):
        chip = from_chip(ahead)
        hat, _ = hat_of(half[which][half_part(chip, part), :].astype(F32))
        row = pl.multiple_of((chip * 2 + place.core) * piece + part * CHUNK, CHUNK)
        n1[pl.ds((1 - which) * tokens + row, CHUNK), :] = (hat * r.gain[...] + r.shift[...]).astype(BF16)
        near(which, ahead, part).start()

    def project(which, ahead):
        for part in range(n):
            near(which, ahead, part).wait_recv()
        chip = from_chip(ahead)
        row = pl.multiple_of(chip * 2 * piece, CHUNK)
        rows = pl.ds((1 - which) * tokens + row, 2 * piece)
        rows_in = n1[rows, :]
        r.kext[rows, :] = dot(rows_in, r.wk[...]).astype(BF16)
        r.vext[rows, :] = dot(rows_in, r.wv[...]).astype(BF16)
        if not which:
            r.q[pl.ds(row, 2 * piece), :] = scaled(dot(rows_in, r.wq[...]))

    def step(which, ahead):
        for part in range(n):
            if ahead:
                far(which, ahead, part).wait_recv()
            normed(which, ahead, part)
        project(which, ahead)

    step(0, 0)
    mem_pass(1)
    for ahead in range(1, chips):
        step(0, ahead)
    r.half.start()
    mem_pass(3)

    @pl.when(jnp.logical_not(place.has_prev))
    def _():
        half[1][own_rows, :] = jnp.zeros((piece, n1.shape[1]), BF16)

    pl.when(place.has_prev)(lambda: parts(lambda part: pass_on(part).wait_recv()))
    for part in range(n):
        for ahead in range(1, chips):
            far(1, ahead, part).start()
    grads.relay()
    step(1, 0)
    mem_pass(2)
    for ahead in range(1, chips):
        step(1, ahead)
    r.prev.start()
    r.n1.start()
    for part in range(n):
        for which in range(2):
            for ahead in range(1, chips):
                far(which, ahead, part).wait_send()
            for ahead in range(chips):
                near(which, ahead, part).wait_send()
    pl.when(place.has_next)(lambda: parts(lambda part: pass_on(part).wait_send()))
    grads.end()
    grads.drain()
    for copy in own_copies:
        copy.wait()
    for behind in range(1, rows_apart):
        mem_far(behind).wait_send()
    for behind in range(rows_apart):
        for ahead in range(1, inner):
            mem_near(behind, ahead).wait()
    known_all(lambda copy: copy.wait())


def opening(chips, seqs, ids, x, og, memory, mask, gain, shift, wq, wk, wv):
    width, dim = wq.shape[1], x.shape[1]
    tokens = ids.shape[0]
    n = tokens // (2 * chips) // CHUNK
    rows, inner = SeqSum.ROWS, seqs // SeqSum.ROWS
    dma = pltpu.SemaphoreType.DMA
    vmem = lambda array: (array, "vmem")
    return call(
        functools.partial(open_body, chips, seqs),
        "opening",
        dict(
            ids=(ids, "smem"),
            x=vmem(x),
            og_own=(og, "hbm"),
            memory=(memory, "hbm"),
            mask=vmem(mask),
            gain=vmem(gain),
            shift=vmem(shift),
            wq=vmem(wq),
            wk=vmem(wk),
            wv=vmem(wv),
        ),
        dict(
            n1=((2 * tokens, dim), BF16, "late"),
            half=((tokens // 2, dim), BF16, "late"),
            prev=((tokens // 2, dim), BF16, "late"),
            q=((tokens, width), BF16, "vmem"),
            kext=((2 * tokens, width), BF16, "vmem"),
            vext=((2 * tokens, width), BF16, "vmem"),
            mem=((seqs, 1, memory.shape[1], dim // (2 * chips)), BF16, "hbm"),
            masks=((seqs, 1, mask.shape[1]), jnp.int32, "vmem"),
            pages=((seqs, 8, 128), jnp.int32, "vmem"),
            og=((2 * chips, tokens // (2 * chips), dim), BF16, "hbm"),
        ),
        dict(
            s1=dma((2, chips, n)),
            r1=dma((2, chips, n)),
            s2=dma((2, chips - 1, n)),
            r2=dma((2, chips - 1, n)),
            ss=dma((n,)),
            sr=dma((n,)),
            ms=dma((2, seqs - 1)),
            mr=dma((2, seqs - 1)),
            fs=dma((rows - 1,)),
            fr=dma((rows - 1,)),
            ns=dma((rows, inner - 1)),
            nr=dma((rows, inner - 1)),
            local=dma((3,)),
            page_row=pltpu.VMEM((8, 128), jnp.int32),
            **Gather.scratch(chips, n, "og_"),
        ),
        0,
        10 * tokens * dim * width,
    )


def forward_body(chips, seqs, r):
    tokens = r.q.shape[0]
    place = Place(chips, seqs, tokens)
    place.enter(seq="row")
    piece, blocks = place.piece, tokens // BLOCK
    per_block, chips_per_block = place.chunks // blocks, chips // blocks
    mem_true = r.mem8.shape[2]
    keys = r.mem_k.shape[0] // blocks
    stages = [Sums(place, r, stage=stage) for stage in range(3)]
    mem = r.mem.ref

    r.mem_own[...] = jnp.zeros_like(r.mem_own)
    r.bias[...] = jnp.full(r.bias.shape, NEG, F32)
    for block in range(blocks):
        rows = pl.ds(block * keys, mem_true)

        def choose(page):
            r.mem_own[rows, :] = jnp.where(r.ids[block * BLOCK] == page, r.mem8[page, 0], r.mem_own[rows, :])

        def mask_of(page, mask):
            return jnp.where(r.ids[block * BLOCK] == page, r.masks[page], mask)

        loop(seqs, choose)
        mask = lax.fori_loop(0, seqs, mask_of, jnp.zeros((1, mem_true), jnp.int32))
        r.bias[block, :, :mem_true] = jnp.broadcast_to(jnp.where(mask > 0, 0.0, NEG), (8, mem_true))
    memory = Gather(place, r.mem_own, mem, 4, [getattr(r, "mem_" + str(i)) for i in range(5)])
    memory.start()
    r.causal[...] = causal_tile(False)

    def self_block(block):
        biases = [functools.partial(reach_bias, r.offsets, block, tile) for tile in range(REACH)]
        attend(
            r.q,
            block,
            lambda tile, lanes: r.kext[block_rows(block + tile), lanes],
            lambda tile, lanes: r.vext[block_rows(block + tile), lanes],
            biases + [lambda: r.causal[...]],
            r.mixed1,
            r.lse1,
        )
        stages[0].all_pieces(
            block * chips_per_block, chips_per_block, lambda row: dot(r.mixed1[pl.ds(row, piece), :], r.wo[...])
        )

    loop(blocks, self_block)

    memory.relay()
    memory.end()
    wide = mem.shape[2]
    for weight, out in ((r.wck, r.mem_k), (r.wcv, r.mem_v)):
        rows = 0.0
        for device in range(2 * chips):
            rows = rows + dot(mem[device], weight[device * wide : (device + 1) * wide, :])
        out[...] = rows.astype(BF16)
    r.mem.start()

    half = r.half.wait()
    n2, res1, res2 = r.n2.ref, r.res1.ref, r.res2.ref
    share = Share(place, n2, r.ss, r.sr, 0)

    def finish_self(slot):
        rows = half[half_rows(slot), :].astype(F32) + stages[0].take(slot)
        res1[half_rows(slot), :] = rows
        hat, _ = hat_of(rows)
        share.put(slot, (hat * r.cross_gain[...] + r.cross_shift[...]).astype(BF16))

    cross_query, cross_output = r.wq.wait(), r.wco.wait()

    def cross_block(block):
        loop(per_block, lambda index: finish_self(block * per_block + index))
        share.end(block * per_block, per_block)
        rows = block_rows(block)
        page = pl.ds(pl.multiple_of(block * keys, 128), keys)
        r.q2[rows, :] = scaled(dot(n2[rows, :], cross_query[...]))
        attend(
            r.q2,
            block,
            lambda tile, lanes: r.mem_k[page, lanes],
            lambda tile, lanes: r.mem_v[page, lanes],
            [lambda: r.bias[block, 0:1, :]],
            r.mixed2,
            r.lse2,
        )
        stages[1].all_pieces(
            block * chips_per_block,
            chips_per_block,
            lambda row: dot(r.mixed2[pl.ds(row, piece), :], cross_output[...]),
        )

    loop(blocks, cross_block)
    r.n2.start()
    r.res1.start()

    share_ffn = Share(place, r.n3, r.ss, r.sr, 1)
    up, down, og = r.up.wait(), r.down.wait(), r.og.wait()
    act = r.act.ref

    def finish_cross(slot):
        rows = res1[half_rows(slot), :] + stages[1].take(slot)
        res2[half_rows(slot), :] = rows
        hat, _ = hat_of(rows)
        share_ffn.put(slot, (hat * r.gain[...] + r.shift[...]).astype(BF16))

    def term(row):
        rows = pl.ds(row, piece)
        pre = dot(r.n3[rows, :], up[...])
        half_erf = 0.5 * lax.erf(pre * (0.5**0.5)) + 0.5
        act[rows, :] = (pre * half_erf).astype(BF16)
        slope = half_erf + pre * jnp.exp(-0.5 * pre * pre) * (0.15915494309189535**0.5)
        grad_act = dot_nt(og[rows, :], down[...])
        low = (grad_act * slope).astype(BF16)
        r.gpre[rows, :] = low
        return dot_nt(low, up[...])

    def ffn_block(block):
        loop(per_block, lambda index: finish_cross(block * per_block + index))
        share_ffn.end(block * per_block, per_block)
        stages[2].all_pieces(block * chips_per_block, chips_per_block, term)

    loop(blocks, ffn_block)
    r.res2.start()
    r.act.start()
    grad_weight(r.g_down, 0, og, act)
    share_rows = r.down_own.shape[0]
    seq_down = SeqSum(
        place, lambda shard: r.g_down.at[pl.ds(pl.multiple_of(shard * share_rows, 8), share_rows)], r, "down_"
    )
    seq_down.low = r.down_low
    seq_down.start()
    grad_weight(r.g_up.ref, 0, r.n3, r.gpre)
    r.g_up.start()

    share_grad = Share(place, r.g.ref, r.ss, r.sr, 2)
    norm_step(
        place,
        r,
        stages[2],
        share_grad,
        lambda slot: og[pl.ds(place.row(slot, place.core), CHUNK), :].astype(F32),
        res2,
    )
    r.grad.start()
    share_grad.end(0, place.chunks)
    r.g.start()
    seq_down.combine(r.down_own, go=False)
    seq_down.end(far=False)
    memory.drain()


def forward(chips, seqs, ids, offsets, a, w):
    tokens, width = a.q.shape
    dim, hidden = w.up.shape
    chunks = tokens // 2 // CHUNK
    blocks = tokens // BLOCK
    mem_true, wide = a.mem.shape[2:]
    keys = -(-mem_true // 128) * 128
    dma = pltpu.SemaphoreType.DMA
    vmem = lambda array: (array, "vmem")
    late = lambda array: (array, "late")
    return call(
        functools.partial(forward_body, chips, seqs),
        "forward",
        dict(
            ids=(ids, "smem"),
            offsets=(offsets, "smem"),
            q=vmem(a.q),
            kext=vmem(a.kext),
            vext=vmem(a.vext),
            mem8=vmem(a.mem),
            masks=vmem(a.masks),
            wo=vmem(w.attn_output),
            wck=vmem(w.cross_key),
            wcv=vmem(w.cross_value),
            cross_gain=vmem(w.cross_gain),
            cross_shift=vmem(w.cross_shift),
            gain=vmem(w.ffn_gain),
            shift=vmem(w.ffn_shift),
            half=late(a.half),
            wq=late(w.cross_query),
            wco=late(w.cross_output),
            up=late(w.up),
            og=late(a.og.reshape(tokens, dim)),
            down=late(w.down),
        ),
        dict(
            mixed1=((tokens, width), BF16, "vmem"),
            lse1=((width // PAIR, 8, tokens), F32, "vmem"),
            res1=((tokens // 2, dim), F32, "late"),
            n2=((tokens, dim), BF16, "late"),
            mem=((2 * chips, blocks * keys, wide), BF16, "late"),
            mem_k=((blocks * keys, width), BF16, "vmem"),
            mem_v=((blocks * keys, width), BF16, "vmem"),
            bias=((blocks, 8, keys), F32, "vmem"),
            q2=((tokens, width), BF16, "vmem"),
            mixed2=((tokens, width), BF16, "vmem"),
            lse2=((width // PAIR, 8, tokens), F32, "vmem"),
            res2=((tokens // 2, dim), F32, "late"),
            act=((tokens, hidden), BF16, "late"),
            grad=((tokens // 2, dim), F32, "late"),
            g=((tokens, dim), BF16, "late"),
            norm=((2, dim), F32, "vmem"),
            g_up=((dim, hidden), BF16, "late"),
            down_low=((SeqSum.ROWS, dim // seqs, hidden), BF16, "vmem"),
            down_own=((dim // seqs, hidden), F32, "vmem"),
        ),
        dict(
            **sum_scratch(chips, tokens, dim, stages=3),
            **Gather.scratch(chips, 4, "mem_"),
            mem_own=pltpu.VMEM((blocks * keys, wide), BF16),
            causal=pltpu.VMEM((BLOCK, BLOCK), F32),
            **SeqSum.scratch(seqs, (dim // seqs, hidden), BF16, "down_", low=False, far=False),
            g_down=pltpu.VMEM((dim, hidden), BF16),
            n3=pltpu.VMEM((tokens, dim), BF16),
            gpre=pltpu.VMEM((tokens, hidden), BF16),
            ss=dma((3, chunks)),
            sr=dma((3, chunks)),
        ),
        1,
        14 * tokens * dim * hidden,
    )


def cross_back_body(chips, seqs, r):
    tokens = r.g_in.shape[0]
    place = Place(chips, seqs, tokens)
    place.enter(seq="all")
    piece, n, blocks = place.piece, place.per_piece, tokens // BLOCK
    share_rows = r.sum_down.shape[0]
    keys = r.mem_k.shape[0] // blocks
    mine = lambda ref: (lambda shard: ref.at[pl.ds(pl.multiple_of(shard * share_rows, 8), share_rows)])
    seq_down = SeqSum(place, None, r, "down_")
    seq_down.low = r.down_low
    fetch_down = [
        pltpu.make_async_copy(r.down_low.at[2], seq_down.mid, r.fetch.at[0, 0]),
        pltpu.make_async_copy(r.down_own, r.sum_down, r.fetch.at[0, 1]),
    ]
    seq_up = SeqSum(place, mine(r.g_up), r, "up_")
    fetch_up = seq_up.fetch(r.fetch.at[1])
    base = pltpu.make_async_copy(r.res_out.at[pl.ds(place.x * piece, piece)], r.base, r.fetch.at[2, 0])
    base.start()
    for index in range(2):
        seq_down.exchange(index).start()
    seq_up.start()
    for copy in fetch_down + fetch_up:
        copy.start()
    sums = Sums(place, r)

    def step(block):
        rows = block_rows(block)
        page = pl.ds(pl.multiple_of(block * keys, 128), keys)
        r.dout[rows, :] = dot_nt(r.g_in[rows, :], r.wo[...]).astype(BF16)
        dots_out(r.dout, r.mixed, block, r.dots)
        bias = jnp.transpose(r.bias[block])[:, 0:1]

        def pair_step(pair):
            lanes = pair_lanes(pair)
            dq, dk, dv = attend_back(
                r.q,
                r.dout,
                r.lse,
                r.dots,
                block,
                pair,
                r.mem_k[page, lanes],
                r.mem_v[page, lanes],
                lambda: bias,
            )
            r.gq[rows, lanes] = dq.astype(BF16)
            r.gk[page, lanes] = dk.astype(BF16)
            r.gv[page, lanes] = dv.astype(BF16)

        loop(r.q.shape[1] // PAIR, pair_step)
        sums.all_pieces(
            block * (chips // blocks),
            chips // blocks,
            lambda row: dot_nt(r.gq[pl.ds(row, piece), :], r.wq[...]),
        )

    loop(blocks, step)

    width = r.q.shape[1]
    wide = r.mem_sum.shape[1]

    def mem_part(chip, core):
        rows = pl.ds(pl.multiple_of((chip * 2 + core) * wide, wide), wide)
        return dot_nt(r.gk[...], r.wck[rows, :]) + dot_nt(r.gv[...], r.wcv[rows, :])

    def mem_near(ahead):
        return remote(r.mem_out.at[ahead], r.mem_mate.at[ahead], r.mns.at[ahead], r.mnr.at[ahead], place.mate)

    def mem_far(ahead):
        sems = (r.mfs.at[ahead - 1], r.mfr.at[ahead - 1])
        return remote(r.mem_mate.at[ahead], r.mem_far.at[ahead - 1], *sems, place.peer(ahead))

    for ahead in range(chips):
        r.mem_out[ahead] = mem_part(place.chip(ahead), 1 - place.core).astype(BF16)
        mem_near(ahead).start()
    for ahead in range(1, chips):
        rows = mem_part(place.chip(ahead), place.core)
        mem_near(ahead).wait_recv()
        r.mem_mate[ahead] = (rows + r.mem_mate[ahead].astype(F32)).astype(BF16)
        mem_far(ahead).start()
    rows = mem_part(place.x, place.core)
    mem_near(0).wait_recv()
    r.mem_sum[...] = rows + r.mem_mate[0].astype(F32)
    for copy in fetch_down:
        copy.wait()
    seq_down.middle(r.sum_down)

    hidden = Sums(place, r, "hidden_")
    act, down = r.act.wait(), r.down.wait()
    hidden.own_pieces(lambda row: dot(act[pl.ds(row, piece), :], down[...]), go=False)
    base.wait()
    for part in range(n):
        rows = pl.ds(part * CHUNK, CHUNK)
        r.out_own[rows, :] = r.base[rows, :] + hidden.own[part]
        for ahead in range(1, chips):
            r.out_low[ahead - 1, part] = hidden.low[ahead * n + part]

    n2, mem = r.n2.wait(), r.mem.wait()
    g_w = r.g_w

    def mem_step(device):
        rows = pl.ds(pl.multiple_of(device * wide, wide), wide)
        both = jnp.concatenate([r.gk[...], r.gv[...]], axis=1)
        g_w[rows, width : 3 * width] = dot_tn(mem[device], both).astype(BF16)

    loop(2 * chips, mem_step)
    grad_weight(g_w, 0, n2, r.gq)
    grad_weight(g_w, 3 * width, r.g_in, r.mixed)
    seq_cross = SeqSum(place, mine(g_w), r, "cross_")
    seq_cross.low = r.cross_low
    seq_cross.start()

    for copy in fetch_up:
        copy.wait()
    seq_up.combine(r.sum_up, fetched=True)
    share = Share(place, r.g.ref, r.s1, r.r1)
    res, grad_in = r.res.wait(), r.grad_in.wait()
    norm_step(place, r, sums, share, lambda slot: grad_in[half_rows(slot), :], res)
    r.grad.start()
    share.end(0, place.chunks)
    r.g.start()
    seq_up.middle(r.sum_up)
    for ahead in range(1, chips):
        mem_far(ahead).wait_recv()
        r.mem_sum[...] = r.mem_sum[...] + r.mem_far[ahead - 1].astype(F32)
    seq_down.finish(r.sum_down)
    seq_up.finish(r.sum_up)
    seq_cross.combine(r.cross_own, go=False)
    seq_down.end(near=False)
    seq_up.end()
    seq_cross.end(far=False)
    hidden.own_end(far=False)
    for ahead in range(chips):
        mem_near(ahead).wait_send()
    for ahead in range(1, chips):
        mem_far(ahead).wait_send()


def cross_back(chips, seqs, a, f, w):
    tokens, dim = f.g.shape
    width = f.q2.shape[1]
    hidden = f.act.shape[1]
    chunks = tokens // 2 // CHUNK
    mem_rows = f.mem_k.shape[0]
    rows = SeqSum.ROWS
    dma = pltpu.SemaphoreType.DMA
    vmem = lambda array: (array, "vmem")
    late = lambda array: (array, "late")
    hbm = lambda array: (array, "hbm")
    return call(
        functools.partial(cross_back_body, chips, seqs),
        "cross_back",
        dict(
            g_in=vmem(f.g),
            wo=vmem(w.cross_output),
            q=vmem(f.q2),
            mem_k=vmem(f.mem_k),
            mem_v=vmem(f.mem_v),
            bias=vmem(f.bias),
            mixed=vmem(f.mixed2),
            lse=vmem(f.lse2),
            wq=vmem(w.cross_query),
            gain=vmem(w.cross_gain),
            wck=vmem(w.cross_key),
            wcv=vmem(w.cross_value),
            act=late(f.act),
            down=late(w.down),
            mem=late(f.mem),
            n2=late(f.n2),
            res=late(f.res1),
            grad_in=late(f.grad),
            res_out=hbm(f.res2),
            g_up=hbm(f.g_up),
            down_low=hbm(f.down_low),
            down_own=hbm(f.down_own),
        ),
        dict(
            grad=((tokens // 2, dim), F32, "late"),
            g=((tokens, dim), BF16, "late"),
            norm=((2, dim), F32, "vmem"),
            cross_low=((rows, dim // seqs, 4 * width), BF16, "vmem"),
            cross_own=((dim // seqs, 4 * width), F32, "vmem"),
            mem_sum=((mem_rows, f.mem.shape[2]), F32, "vmem"),
            sum_up=((dim // seqs, hidden), F32, "vmem"),
            sum_down=((dim // seqs, hidden), F32, "vmem"),
            out_own=((tokens // (2 * chips), dim), F32, "vmem"),
            out_low=((chips - 1, tokens // (2 * chips) // CHUNK, CHUNK, dim), BF16, "vmem"),
        ),
        dict(
            **sum_scratch(chips, tokens, dim),
            **sum_scratch(chips, tokens, dim, "hidden_"),
            **SeqSum.scratch(seqs, (dim // seqs, 4 * width), BF16, "cross_", low=False, far=False),
            g_w=pltpu.VMEM((dim, 4 * width), BF16),
            **SeqSum.scratch(seqs, (dim // seqs, hidden), BF16, "up_"),
            **SeqSum.scratch(seqs, (dim // seqs, hidden), BF16, "down_", near=False, low=False),
            mem_out=pltpu.VMEM((chips, mem_rows, f.mem.shape[2]), BF16),
            mem_mate=pltpu.VMEM((chips, mem_rows, f.mem.shape[2]), BF16),
            mem_far=pltpu.VMEM((chips - 1, mem_rows, f.mem.shape[2]), BF16),
            mns=dma((chips,)),
            mnr=dma((chips,)),
            mfs=dma((chips - 1,)),
            mfr=dma((chips - 1,)),
            gq=pltpu.VMEM((tokens, width), BF16),
            gk=pltpu.VMEM((mem_rows, width), BF16),
            gv=pltpu.VMEM((mem_rows, width), BF16),
            dout=pltpu.VMEM((tokens, width), BF16),
            dots=pltpu.VMEM((width // PAIR, 8, tokens), F32),
            base=pltpu.VMEM((tokens // (2 * chips), dim), F32),
            s1=dma((1, chunks)),
            r1=dma((1, chunks)),
            fetch=dma((3, rows)),
        ),
        2,
        12 * tokens * dim * width,
    )


def close_body(chips, seqs, r):
    tokens, width = r.q.shape
    place = Place(chips, seqs, tokens)
    place.enter(seq="all", all_tp=True)
    piece, n, blocks = place.piece, place.per_piece, tokens // BLOCK
    pairs = width // PAIR
    share_rows = r.sum_w.shape[0]
    mine = lambda ref: (lambda shard: ref.at[pl.ds(pl.multiple_of(shard * share_rows, 8), share_rows)])

    mem_rows = r.mem_sum.shape[0]
    keys = mem_rows // blocks
    inner = seqs // SeqSum.ROWS
    seq_row, seq_column = place.seq // inner, lax.rem(place.seq, inner)

    def page_of(shard, block):
        return r.pages[shard, 0:1, block : block + 1]

    def page_near(ahead):
        to = {"seq": seq_row * inner + lax.rem(seq_column + ahead, inner)}
        return remote(r.page_out.at[ahead - 1], r.page_in.at[ahead - 1], r.pns.at[ahead - 1], r.pnr.at[ahead - 1], to)

    for ahead in range(1, inner):
        column = lax.rem(seq_column + ahead, inner)
        for block in range(blocks):
            page = r.ids[block * BLOCK]
            there = jnp.where(lax.rem(page, inner) == column, 1.0, 0.0)
            rows = r.mem_sum[block * keys : (block + 1) * keys, :]
            r.page_out[ahead - 1, block] = (rows * there).astype(BF16)
        page_near(ahead).start()
    seq_page = SeqSum(place, None, r, "page_")

    seq_cross = SeqSum(place, None, r, "cross_")
    seq_cross.low = r.cross_low
    for index in range(2):
        seq_cross.exchange(index).start()

    def out_copy(ahead, part):
        at = (ahead - 1, part)
        return remote(r.out_low.at[at], r.out_far.at[at], r.hs.at[at], r.hr.at[at], place.peer(ahead))

    for part in range(n):
        for ahead in range(1, chips):
            out_copy(ahead, part).start()
    fetches = [
        pltpu.make_async_copy(r.grad_in.at[pl.ds(place.x * piece, piece)], r.grad_own, r.fetch.at[0]),
        pltpu.make_async_copy(r.cross_low.at[2], seq_cross.mid, r.fetch.at[1]),
        pltpu.make_async_copy(r.cross_own, r.sum_w, r.fetch.at[2]),
        pltpu.make_async_copy(r.out_own, r.out_sum, r.fetch.at[3]),
    ]
    for fetch in fetches:
        fetch.start()

    def open_block(block):
        rows = block_rows(block)
        r.dout[rows, :] = dot_nt(r.g_in[rows, :], r.wo[...]).astype(BF16)
        dots_out(r.dout, r.mixed, block, r.dots)

    loop(blocks, open_block)
    r.causal[...] = causal_tile(True)
    r.dq[...] = jnp.zeros_like(r.dq)
    r.dk[...] = jnp.zeros_like(r.dk)
    r.dv[...] = jnp.zeros_like(r.dv)

    def tile_back(block, tile):
        rows, key_rows = block_rows(block), block_rows(block + tile)
        diagonal = jnp.where(tile == REACH, 1.0, 0.0)
        bias = jnp.where(tile == REACH, 0.0, reach_bias(r.offsets, block, tile))

        def step(pair):
            lanes = pair_lanes(pair)
            dq, dk, dv = attend_back(
                r.q,
                r.dout,
                r.lse,
                r.dots,
                block,
                pair,
                r.kext[key_rows, lanes],
                r.vext[key_rows, lanes],
                lambda: r.causal[...] * diagonal + bias,
            )
            r.dq[rows, lanes] = r.dq[rows, lanes] + dq
            r.dk[key_rows, lanes] = r.dk[key_rows, lanes] + dk
            r.dv[key_rows, lanes] = r.dv[key_rows, lanes] + dv

        loop(pairs, step)

    loop(3, lambda index: tile_back(index // 2, lax.rem(index, 2)))
    r.gkv[0, :tokens, :] = r.dk[:tokens, :].astype(BF16)
    r.gkv[1, :tokens, :] = r.dv[:tokens, :].astype(BF16)

    def kv_term(first):
        def term(row):
            rows = pl.ds(first + row, piece)
            return dot_nt(r.gkv[0, rows, :], r.wk[...]) + dot_nt(r.gkv[1, rows, :], r.wv[...])

        return term

    sums_prev = Sums(place, r, "prev_")
    sums_prev.own_pieces(kv_term(0))

    for ahead in range(1, inner):
        page_near(ahead).wait_recv()

    def page_rows(differs):
        page = seq_page.other_row(differs) * inner + seq_column
        rows = 0.0
        for block in range(blocks):
            same = (page_of(place.seq, block) == page).astype(F32)
            rows = rows + r.mem_sum[block * keys : (block + 1) * keys, :] * same
            for ahead in range(1, inner):
                shard = seq_row * inner + lax.rem(seq_column + inner - ahead, inner)
                same = (page_of(shard, block) == page).astype(F32)
                rows = rows + r.page_in[ahead - 1, block].astype(F32) * same
        return rows

    seq_page.combine(r.page_sum, rows_of=page_rows)
    for fetch in fetches:
        fetch.wait()
    seq_cross.middle(r.sum_w)

    loop(3, lambda index: tile_back((index + 1) // 2, REACH - lax.rem(index, 2)))
    r.gkv[0, tokens:, :] = r.dk[tokens:, :].astype(BF16)
    r.gkv[1, tokens:, :] = r.dv[tokens:, :].astype(BF16)

    n1 = r.n1.wait()
    grad_weight(r.g_kv, 0, n1, r.gkv.at[0], r.gkv.at[1])
    seq_kv = SeqSum(place, mine(r.g_kv), r, "kv_")
    seq_kv.start()

    def shift_copy(part):
        rows = pl.ds(part * CHUNK, CHUNK)
        sems = (r.ks.at[part], r.kr.at[part])
        return remote(r.shift_out.at[rows], r.shift_in.at[rows], *sems, {"seq": place.seq - 1})

    def shifts(act):
        for part in range(n):
            act(shift_copy(part))

    for part in range(n):
        r.shift_out[pl.ds(part * CHUNK, CHUNK), :] = sums_prev.own_total(part).astype(BF16)
        pl.when(place.has_prev)(lambda: shift_copy(part).start())

    @pl.when(jnp.logical_not(place.has_next))
    def _():
        r.shift_in[...] = jnp.zeros_like(r.shift_in)

    r.gq[...] = r.dq[...].astype(BF16)
    grad_weight(r.g_q, 0, n1.at[pl.ds(tokens, tokens)], r.gq)
    seq_q = SeqSum(place, mine(r.g_q), r, "q_")
    seq_q.start()
    own_kv = kv_term(tokens)
    sums = Sums(place, r)
    sums.own_pieces(lambda row: dot_nt(r.gq[pl.ds(row, piece), :], r.wq[...]) + own_kv(row))
    grad_weight(r.g_out, 0, r.g_in, r.mixed)
    seq_out = SeqSum(place, mine(r.g_out), r, "out_")
    seq_out.start()
    seq_page.middle(r.page_sum)

    half, prev = r.half.wait(), r.prev.wait()

    def norm_rows(slot, carry):
        ahead, part = slot // n, lax.rem(slot, n)
        mine_rows = pl.ds(pl.multiple_of(place.chip(ahead) * piece + part * CHUNK, CHUNK), CHUNK)
        gain_sum, shift_sum = carry
        for part_sums, ref in ((sums, half), (sums_prev, prev)):
            hat, _ = hat_of(ref[mine_rows, :].astype(F32))
            rows = part_sums.own[slot]
            gain_sum = gain_sum + jnp.sum(rows * hat, axis=0, keepdims=True)
            shift_sum = shift_sum + jnp.sum(rows, axis=0, keepdims=True)
        return gain_sum, shift_sum

    zero = jnp.zeros((1, r.gain.shape[1]), F32)
    norms = list(lax.fori_loop(0, place.chunks, norm_rows, (zero, zero)))
    norms += [ref[row : row + 1, :] * (1.0 / chips) for ref in (r.norm_cross, r.norm_ffn) for row in range(2)]
    columns = r.norm_out.shape[2]
    for shard in range(seqs):
        for row, values in enumerate(norms):
            r.norm_out[shard, row : row + 1, :] = values[:, shard * columns : (shard + 1) * columns]
        r.norm_out[shard, 6:8, :] = jnp.zeros((2, columns), F32)

    def norm_seq(ahead):
        shard = place.shard(ahead)
        sems = (r.nss.at[ahead - 1], r.nsr.at[ahead - 1])
        return remote(r.norm_out.at[shard], r.norm_seq.at[ahead - 1], *sems, {"seq": shard})

    for ahead in range(1, seqs):
        norm_seq(ahead).start()
    seq_kv.combine(r.sum_kv)
    seq_q.combine(r.sum_q)
    norm_rows_in = r.norm_out[place.seq]
    for ahead in range(1, seqs):
        norm_seq(ahead).wait_recv()
        norm_rows_in = norm_rows_in + r.norm_seq[ahead - 1]
    r.norm_sum[...] = norm_rows_in

    def norm_tp(ahead):
        to = {"tp": lax.rem(place.tp + ahead, 2 * chips)}
        return remote(r.norm_sum, r.norm_tp.at[ahead - 1], r.nts.at[ahead - 1], r.ntr.at[ahead - 1], to)

    for ahead in range(1, 2 * chips):
        norm_tp(ahead).start()
    seq_out.combine(r.sum_out)
    seq_kv.middle(r.sum_kv)
    seq_q.middle(r.sum_q)
    seq_out.middle(r.sum_out)

    pl.when(place.has_next)(lambda: shifts(lambda copy: copy.wait_recv()))
    for part in range(n):
        rows = pl.ds(part * CHUNK, CHUNK)
        mine_rows = pl.ds(pl.multiple_of(place.x * piece + part * CHUNK, CHUNK), CHUNK)
        hat, inv_std = hat_of(half[mine_rows, :].astype(F32))
        rows_in = sums.own_total(part) + r.shift_in[rows, :].astype(F32)
        rows_in, _, _ = norm_back(rows_in, hat, inv_std, r.gain[...])
        r.grad[rows, :] = r.grad_own[rows, :] + rows_in
    for part in range(n):
        rows = pl.ds(part * CHUNK, CHUNK)
        out_rows = r.out_sum[rows, :]
        for ahead in range(1, chips):
            out_copy(ahead, part).wait_recv()
            out_rows = out_rows + r.out_far[ahead - 1, part].astype(F32)
        r.out[rows, :] = out_rows.astype(BF16)
    seq_cross.finish(r.sum_w)
    seq_page.finish(r.page_sum)
    r.grad_mem[...] = r.page_sum[: r.grad_mem.shape[0], :]
    seq_out.finish(r.sum_out)
    seq_kv.finish(r.sum_kv)
    seq_q.finish(r.sum_q)
    rows = r.norm_sum[...]
    for ahead in range(1, 2 * chips):
        norm_tp(ahead).wait_recv()
        rows = rows + r.norm_tp[ahead - 1]
    r.norms[...] = rows

    for ahead in range(1, 2 * chips):
        norm_tp(ahead).wait_send()
    for seq_sum in (seq_out, seq_kv, seq_q):
        seq_sum.end()
    seq_cross.end(near=False)
    for part in range(n):
        for ahead in range(1, chips):
            out_copy(ahead, part).wait_send()
    seq_page.end(near=False)
    for ahead in range(1, seqs):
        norm_seq(ahead).wait_send()
    for ahead in range(1, inner):
        page_near(ahead).wait_send()
    sums_prev.own_end()
    sums.own_end()
    pl.when(place.has_prev)(lambda: shifts(lambda copy: copy.wait_send()))


def closing(chips, seqs, ids, offsets, a, f, e, mem_true, w):
    tokens, width = a.q.shape
    dim = w.attn_output.shape[1]
    blocks = tokens // BLOCK
    own = tokens // (2 * chips)
    mem_rows, wide = e.mem_sum.shape
    rows, inner = SeqSum.ROWS, seqs // SeqSum.ROWS
    keys = mem_rows // blocks
    dma = pltpu.SemaphoreType.DMA
    vmem = lambda array: (array, "vmem")
    late = lambda array: (array, "late")
    hbm = lambda array: (array, "hbm")
    return call(
        functools.partial(close_body, chips, seqs),
        "closing",
        dict(
            ids=(ids, "smem"),
            offsets=(offsets, "smem"),
            cross_low=hbm(e.cross_low),
            cross_own=hbm(e.cross_own),
            out_low=hbm(e.out_low),
            out_own=hbm(e.out_own),
            mem_sum=vmem(e.mem_sum),
            g_in=vmem(e.g),
            wo=vmem(w.attn_output),
            q=vmem(a.q),
            kext=vmem(a.kext),
            vext=vmem(a.vext),
            mixed=vmem(f.mixed1),
            lse=vmem(f.lse1),
            wq=vmem(w.attn_query),
            wk=vmem(w.attn_key),
            wv=vmem(w.attn_value),
            gain=vmem(w.self_gain),
            norm_cross=vmem(e.norm),
            norm_ffn=vmem(f.norm),
            pages=vmem(a.pages),
            n1=late(a.n1),
            half=late(a.half),
            prev=late(a.prev),
            grad_in=hbm(e.grad),
        ),
        dict(
            grad=((own, dim), F32, "vmem"),
            out=((own, dim), BF16, "vmem"),
            norms=((8, dim // seqs), F32, "vmem"),
            sum_w=((dim // seqs, 4 * width), F32, "vmem"),
            sum_q=((dim // seqs, width), F32, "vmem"),
            sum_kv=((dim // seqs, 2 * width), F32, "vmem"),
            sum_out=((dim // seqs, width), F32, "vmem"),
            grad_mem=((mem_true, wide), F32, "vmem"),
        ),
        dict(
            **sum_scratch(chips, tokens, dim, "prev_"),
            **sum_scratch(chips, tokens, dim),
            **SeqSum.scratch(seqs, (dim // seqs, 4 * width), BF16, "cross_", near=False, low=False),
            out_sum=pltpu.VMEM((own, dim), F32),
            out_far=pltpu.VMEM((chips - 1, own // CHUNK, CHUNK, dim), BF16),
            hs=dma((chips - 1, own // CHUNK)),
            hr=dma((chips - 1, own // CHUNK)),
            **SeqSum.scratch(seqs, (dim // seqs, width), BF16, "q_"),
            **SeqSum.scratch(seqs, (dim // seqs, 2 * width), BF16, "kv_"),
            **SeqSum.scratch(seqs, (dim // seqs, width), BF16, "out_"),
            **SeqSum.scratch(seqs, (keys, wide), BF16, "page_", near=False),
            norm_seq=pltpu.VMEM((seqs - 1, 8, dim // seqs), F32),
            nss=dma((seqs - 1,)),
            nsr=dma((seqs - 1,)),
            page_out=pltpu.VMEM((inner - 1, blocks, keys, wide), BF16),
            page_in=pltpu.VMEM((inner - 1, blocks, keys, wide), BF16),
            page_sum=pltpu.VMEM((keys, wide), F32),
            pns=dma((inner - 1,)),
            pnr=dma((inner - 1,)),
            causal=pltpu.VMEM((BLOCK, BLOCK), F32),
            dout=pltpu.VMEM((tokens, width), BF16),
            dots=pltpu.VMEM((width // PAIR, 8, tokens), F32),
            dq=pltpu.VMEM((tokens, width), F32),
            dk=pltpu.VMEM((2 * tokens, width), F32),
            dv=pltpu.VMEM((2 * tokens, width), F32),
            gq=pltpu.VMEM((tokens, width), BF16),
            gkv=pltpu.VMEM((2, 2 * tokens, width), BF16),
            g_q=pltpu.VMEM((dim, width), BF16),
            g_kv=pltpu.VMEM((dim, 2 * width), BF16),
            g_out=pltpu.VMEM((dim, width), BF16),
            grad_own=pltpu.VMEM((own, dim), F32),
            fetch=dma((4,)),
            shift_out=pltpu.VMEM((own, dim), BF16),
            shift_in=pltpu.VMEM((own, dim), BF16),
            ks=dma((own // CHUNK,)),
            kr=dma((own // CHUNK,)),
            norm_out=pltpu.VMEM((seqs, 8, dim // seqs), F32),
            norm_sum=pltpu.VMEM((8, dim // seqs), F32),
            norm_tp=pltpu.VMEM((2 * chips - 1, 8, dim // seqs), F32),
            nts=dma((2 * chips - 1,)),
            ntr=dma((2 * chips - 1,)),
        ),
        3,
        20 * tokens * 3 * BLOCK * width,
    )


def layout_body(width, per_tp, *refs):
    sources, results, places, sems = refs[:10], refs[10:-11], refs[-11:-1], refs[-1]
    copies = [pltpu.make_async_copy(src, dst, sems.at[i]) for i, (src, dst) in enumerate(zip(sources, places))]
    for copy in copies:
        copy.start()
    for copy in copies:
        copy.wait()
    sum_q, sum_kv, sum_out, sum_w, sum_up, sum_down, grad, out, grad_mem, norms = places
    (out_out, grad_out, mem_out, q_out, k_out, v_out, o_out, cq_out, ck_out, cv_out, co_out, up_out, down_out) = results[:-6]
    out_out[...] = out[...]
    grad_out[...] = grad[...]
    mem_out[0] = grad_mem[...]
    q_out[...] = sum_q[...]
    k_out[...] = sum_kv[:, :width]
    v_out[...] = sum_kv[:, width:]
    o_out[...] = jnp.transpose(sum_out[...])
    for piece, ref in enumerate((cq_out, ck_out, cv_out)):
        ref[...] = sum_w[:, piece * width : (piece + 1) * width]
    co_out[...] = jnp.transpose(sum_w[:, 3 * width :])
    up_out[...] = sum_up[...]
    down_out[...] = jnp.transpose(sum_down[...])
    columns = norms.shape[1]
    first = lax.axis_index("tp") * per_tp
    from_column = lax.broadcasted_iota(jnp.int32, (columns, per_tp), 0)
    to_column = lax.broadcasted_iota(jnp.int32, (columns, per_tp), 1)
    pick = (from_column == to_column + first).astype(F32)
    mine = jnp.dot(norms[...], pick, precision=lax.Precision.HIGHEST, preferred_element_type=F32)
    for row, ref in enumerate(results[-6:]):
        ref[...] = mine[row : row + 1, :]


def layout(tps, width, c, e):
    share_rows, hidden = e.sum_up.shape
    own, dim = c.grad.shape
    per_tp = share_rows // tps
    weights = [(share_rows, width)] * 3 + [(width, share_rows)]
    dims = [(own, dim), (own, dim), (1, *c.grad_mem.shape), *weights, *weights, (share_rows, hidden), (hidden, share_rows)]
    types = [BF16] + [F32] * (len(dims) - 1)
    dims += [(1, per_tp)] * 6
    types += [F32] * 6
    sources = (c.sum_q, c.sum_kv, c.sum_out, c.sum_w, e.sum_up, e.sum_down, c.grad, c.out, c.grad_mem, c.norms)
    return pl.pallas_call(
        functools.partial(layout_body, width, per_tp),
        name="layout",
        out_shape=[jax.ShapeDtypeStruct(d, t) for d, t in zip(dims, types)],
        in_specs=[pl.BlockSpec(memory_space=pltpu.HBM)] * len(sources),
        out_specs=[VMEM] * len(dims),
        scratch_shapes=[pltpu.VMEM(source.shape, source.dtype) for source in sources]
        + [pltpu.SemaphoreType.DMA((len(sources),))],
        compiler_params=pltpu.CompilerParams(vmem_limit_bytes=62 << 20),
    )(*sources)


def on_device(
    hidden_in,
    memory,
    page_ids,
    token_offsets,
    memory_mask,
    attn_query,
    attn_key,
    attn_value,
    attn_output,
    cross_query,
    cross_key,
    cross_value,
    cross_output,
    ffn_up,
    ffn_down,
    self_gain,
    self_shift,
    cross_gain,
    cross_shift,
    ffn_gain,
    ffn_shift,
    out_grad,
):
    tps, seqs = lax.axis_size("tp"), lax.axis_size("seq")
    chips = tps // 2
    width = attn_query.shape[1]
    w = Refs()
    w.attn_query, w.attn_key, w.attn_value, w.attn_output = attn_query, attn_key, attn_value, attn_output
    w.cross_query, w.cross_key, w.cross_value, w.cross_output = cross_query, cross_key, cross_value, cross_output
    w.up, w.down = ffn_up, ffn_down
    w.self_gain, w.self_shift = self_gain.reshape(1, -1), self_shift.reshape(1, -1)
    w.cross_gain, w.cross_shift = cross_gain.reshape(1, -1), cross_shift.reshape(1, -1)
    w.ffn_gain, w.ffn_shift = ffn_gain.reshape(1, -1), ffn_shift.reshape(1, -1)

    a = opening(
        chips,
        seqs,
        page_ids,
        hidden_in,
        out_grad,
        memory,
        memory_mask,
        w.self_gain,
        w.self_shift,
        attn_query,
        attn_key,
        attn_value,
    )
    f = forward(chips, seqs, page_ids, token_offsets, a, w)
    e = cross_back(chips, seqs, a, f, w)
    c = closing(chips, seqs, page_ids, token_offsets, a, f, e, memory.shape[1], w)
    results = layout(tps, width, c, e)
    return (
        results[0],
        results[1],
        results[2],
        *results[3:11],
        results[11],
        results[12],
        *[values.reshape(-1) for values in results[13:]],
    )


def solution(mesh):
    both = ("seq", "tp")
    in_specs = (
        P(both, None),
        P("seq", None, None),
        P("seq"),
        P("seq"),
        P("seq", None),
        P(None, "tp"),
        P(None, "tp"),
        P(None, "tp"),
        P("tp", None),
        P(None, "tp"),
        P(None, "tp"),
        P(None, "tp"),
        P("tp", None),
        P(None, "tp"),
        P("tp", None),
        P(),
        P(),
        P(),
        P(),
        P(),
        P(),
        P(both, None),
    )
    out_specs = (
        P(both, None),
        P(both, None),
        P("seq", None, "tp"),
        P("seq", "tp"),
        P("seq", "tp"),
        P("seq", "tp"),
        P("tp", "seq"),
        P("seq", "tp"),
        P("seq", "tp"),
        P("seq", "tp"),
        P("tp", "seq"),
        P("seq", "tp"),
        P("tp", "seq"),
        P(both),
        P(both),
        P(both),
        P(both),
        P(both),
        P(both),
    )
    return jax.shard_map(on_device, mesh=mesh, in_specs=in_specs, out_specs=out_specs, check_vma=False)
```

```python
import functools

import jax
import jax.numpy as jnp
from jax import lax
from jax.experimental import pallas as pl
from jax.experimental.pallas import tpu as pltpu
from jax.sharding import PartitionSpec as P

HEAD_DIM = 64
PAIR = 2 * HEAD_DIM
BLOCK = 512
REACH = 2
CHUNK = 128
EPS = 1e-05
NEG = -1e30
F32 = jnp.float32
BF16 = jnp.bfloat16
MESH = pl.DeviceIdType.MESH
VMEM = pl.BlockSpec(memory_space=pltpu.VMEM)
SMEM = pl.BlockSpec(memory_space=pltpu.SMEM)


def dot(left, right):
    return jnp.dot(left, right, preferred_element_type=F32)


def dot_nt(left, right):
    return lax.dot_general(left, right, (((1,), (1,)), ((), ())), preferred_element_type=F32)


def dot_tn(left, right):
    return lax.dot_general(left, right, (((0,), (0,)), ((), ())), preferred_element_type=F32)


def hat_of(rows):
    center = rows - jnp.mean(rows, axis=-1, keepdims=True)
    inv_std = lax.rsqrt(jnp.mean(center * center, axis=-1, keepdims=True) + EPS)
    return center * inv_std, inv_std


def norm_back(grad_rows, hat, inv_std, gain):
    grad_hat = grad_rows * gain
    inner = jnp.mean(grad_hat * hat, axis=-1, keepdims=True)
    grad_input = inv_std * (grad_hat - jnp.mean(grad_hat, axis=-1, keepdims=True) - hat * inner)
    gain_sum = jnp.sum(grad_rows * hat, axis=0, keepdims=True)
    shift_sum = jnp.sum(grad_rows, axis=0, keepdims=True)
    return grad_input, gain_sum, shift_sum


def remote(src, dst, send_sem, recv_sem, device):
    return pltpu.make_async_remote_copy(
        src_ref=src, dst_ref=dst, send_sem=send_sem, recv_sem=recv_sem, device_id=device, device_id_type=MESH
    )


class Late:
    def __init__(self, hbm, ref, sem, out):
        self.hbm, self.ref, self.sem, self.out, self.started, self.waited = hbm, ref, sem, out, False, False

    def copy(self):
        ends = (self.ref, self.hbm) if self.out else (self.hbm, self.ref)
        return pltpu.make_async_copy(*ends, self.sem)

    def start(self):
        self.copy().start()
        self.started = True

    def wait(self):
        if self.started and not self.waited:
            self.copy().wait()
            self.waited = True
        return self.ref


class Refs:
    pass


def call(body, name, ins, outs, scratch, collective_id, flops):
    dma = pltpu.SemaphoreType.DMA
    specs = {"vmem": VMEM, "smem": SMEM, "hbm": pl.BlockSpec(memory_space=pltpu.HBM)}
    specs["late"] = specs["hbm"]
    late_in = [key for key, (_, mode) in ins.items() if mode == "late"]
    late_out = [key for key, (_, _, mode) in outs.items() if mode == "late"]
    places = [pltpu.VMEM(ins[key][0].shape, ins[key][0].dtype) for key in late_in]
    places += [pltpu.VMEM(outs[key][0], outs[key][1]) for key in late_out]
    lates = len(places)

    def kernel(*refs):
        r = Refs()
        count = len(ins) + len(outs)
        for key, ref in zip([*ins, *outs], refs[:count]):
            setattr(r, key, ref)
        for key, ref in zip(scratch, refs[count : count + len(scratch)]):
            setattr(r, key, ref)
        rest = refs[count + len(scratch) :]
        all_late = []
        for index, key in enumerate(late_in + late_out):
            late = Late(getattr(r, key), rest[index], rest[-1].at[index], index >= len(late_in))
            setattr(r, key, late)
            all_late.append(late)
            if not late.out:
                late.start()
        body(r)
        for late in all_late:
            late.wait()

    result = pl.pallas_call(
        kernel,
        name=name,
        out_shape=[jax.ShapeDtypeStruct(dims, dtype) for dims, dtype, _ in outs.values()],
        in_specs=[specs[mode] for _, mode in ins.values()],
        out_specs=[specs[mode] for _, _, mode in outs.values()],
        scratch_shapes=[*scratch.values(), *places] + ([dma((lates,))] if lates else []),
        cost_estimate=pl.CostEstimate(flops=flops, bytes_accessed=16 << 20, transcendentals=0),
        compiler_params=pltpu.CompilerParams(
            collective_id=collective_id, has_side_effects=True, vmem_limit_bytes=62 << 20
        ),
    )(*[array for array, _ in ins.values()])
    out = Refs()
    for key, value in zip(outs, result):
        setattr(out, key, value)
    return out


def loop(count, step):
    lax.fori_loop(0, count, lambda index, carry: (step(index), carry)[1], 0)


class Place:
    def __init__(self, chips, seqs, rows):
        self.chips, self.seqs = chips, seqs
        self.piece = rows // (2 * chips)
        self.per_piece = self.piece // CHUNK
        self.chunks = chips * self.per_piece
        self.tp = lax.axis_index("tp")
        self.seq = lax.axis_index("seq")
        self.x = self.tp // 2
        self.core = lax.rem(self.tp, 2)
        self.mate = {"tp": self.x * 2 + 1 - self.core}
        self.has_prev, self.has_next = self.seq > 0, self.seq < seqs - 1

    def chip(self, ahead):
        return lax.rem(self.x + ahead, self.chips)

    def peer(self, ahead):
        return {"tp": self.chip(ahead) * 2 + self.core}

    def shard(self, ahead):
        return lax.rem(self.seq + ahead, self.seqs)

    def piece_row(self, chip, core):
        return pl.multiple_of((chip * 2 + core) * self.piece, CHUNK)

    def row(self, slot, core):
        chip, part = slot // self.per_piece, lax.rem(slot, self.per_piece)
        return pl.multiple_of((chip * 2 + core) * self.piece + part * CHUNK, CHUNK)

    def enter(self, seq="", all_tp=False):
        barrier = pltpu.get_barrier_semaphore()

        def greet(device):
            pl.semaphore_signal(barrier, inc=1, device_id=device, device_id_type=MESH)

        count = self.chips
        if all_tp:
            count = 2 * self.chips - 1
            for ahead in range(1, 2 * self.chips):
                greet({"tp": lax.rem(self.tp + ahead, 2 * self.chips)})
        else:
            greet(self.mate)
            for ahead in range(1, self.chips):
                greet(self.peer(ahead))
        if seq == "all":
            for ahead in range(1, self.seqs):
                greet({"seq": self.shard(ahead)})
            count = count + self.seqs - 1
        if seq == "row":
            inner = self.seqs // SeqSum.ROWS
            for ahead in range(1, inner):
                greet({"seq": self.seq // inner * inner + lax.rem(self.seq + ahead, inner)})
            count = count + inner - 1
        pl.semaphore_wait(barrier, count)


def sum_scratch(chips, rows, width, name="sums_", stages=1):
    chunks = rows // 2 // CHUNK
    dma = pltpu.SemaphoreType.DMA
    specs = [
        pltpu.VMEM((chunks, CHUNK, width), BF16),
        pltpu.VMEM((chunks, CHUNK, width), BF16),
        pltpu.VMEM((chunks, CHUNK, width), F32),
        dma((chunks,)),
        dma((chunks,)),
        pltpu.VMEM((stages, chips - 1, chunks, CHUNK, width), BF16),
        dma((stages, chips - 1, chunks)),
        dma((stages, chips - 1, chunks)),
    ]
    return {name + str(index): spec for index, spec in enumerate(specs)}


class Sums:
    def __init__(self, place, r, name="sums_", stage=0):
        self.place, self.stage = place, stage
        (self.out, self.mate, self.own, self.s1, self.r1, self.far, self.s2, self.r2) = [
            getattr(r, name + str(index)) for index in range(8)
        ]
        self.low = self.mate

    def core_copy(self, slot):
        return remote(self.out.at[slot], self.mate.at[slot], self.s1.at[slot], self.r1.at[slot], self.place.mate)

    def far_copy(self, ahead, slot):
        at = (self.stage, ahead - 1, slot)
        return remote(self.low.at[slot], self.far.at[at], self.s2.at[at], self.r2.at[at], self.place.peer(ahead))

    def near(self, slot, who, rows):
        n = self.place.per_piece

        @pl.when(who == 0)
        def _():
            for part in range(n):
                self.out[slot + part] = rows[part * CHUNK : (part + 1) * CHUNK].astype(BF16)
                self.core_copy(slot + part).start()

        @pl.when(who == 1)
        def _():
            for part in range(n):
                self.core_copy(slot + part).wait_recv()
                self.own[slot + part] = rows[part * CHUNK : (part + 1) * CHUNK] + self.mate[slot + part].astype(F32)

    def all_pieces(self, first, count, term):
        place = self.place
        n = place.per_piece

        def step(index):
            chip, who = first + index // 2, lax.rem(index, 2)
            core = jnp.where(who == 0, 1 - place.core, place.core)
            self.near(chip * n, who, term(place.piece_row(chip, core)))

            @pl.when(who == 1)
            def _():
                for part in range(n):
                    self.low[chip * n + part] = self.own[chip * n + part].astype(BF16)
                    for ahead in range(1, place.chips):
                        self.far_copy(ahead, chip * n + part).start()

        loop(2 * count, step)

    def take(self, slot):
        rows = self.own[slot]
        for ahead in range(1, self.place.chips):
            self.far_copy(ahead, slot).wait_recv()
            rows = rows + self.far[self.stage, ahead - 1, slot].astype(F32)
        self.core_copy(slot).wait_send()
        for ahead in range(1, self.place.chips):
            self.far_copy(ahead, slot).wait_send()
        return rows

    def own_pieces(self, term, go=True):
        place = self.place
        n = place.per_piece

        def step(index):
            ahead, who = lax.rem(index // 2 + 1, place.chips), lax.rem(index, 2)
            core = jnp.where(who == 0, 1 - place.core, place.core)
            self.near(ahead * n, who, term(place.piece_row(place.chip(ahead), core)))

            @pl.when(jnp.logical_and(who == 1, ahead > 0))
            def _():
                for part in range(n):
                    self.low[ahead * n + part] = self.own[ahead * n + part].astype(BF16)
                    if go:
                        self.far_copy(ahead, ahead * n + part).start()

        loop(2 * place.chips, step)

    def own_total(self, part):
        n = self.place.per_piece
        rows = self.own[part]
        for ahead in range(1, self.place.chips):
            slot = ahead * n + part
            self.far_copy(ahead, slot).wait_recv()
            rows = rows + self.far[self.stage, ahead - 1, slot].astype(F32)
        return rows

    def own_end(self, far=True):
        n = self.place.per_piece
        for slot in range(self.place.chunks):
            self.core_copy(slot).wait_send()
            if far and slot >= n:
                self.far_copy(slot // n, slot).wait_send()


class Share:
    def __init__(self, place, ref, send_sems, recv_sems, stage=0):
        self.place, self.ref, self.s, self.r, self.stage = place, ref, send_sems, recv_sems, stage

    def copy(self, slot):
        rows = pl.ds(self.place.row(slot, self.place.core), CHUNK)
        at = (self.stage, slot)
        return remote(self.ref.at[rows], self.ref.at[rows], self.s.at[at], self.r.at[at], self.place.mate)

    def put(self, slot, rows):
        self.ref[pl.ds(self.place.row(slot, self.place.core), CHUNK), :] = rows
        self.copy(slot).start()

    def end(self, first, count):
        loop(count, lambda index: self.copy(first + index).wait())


class Gather:
    def __init__(self, place, own, ref, parts, sems):
        self.place, self.own, self.ref, self.parts = place, own, ref, parts
        self.size = own.shape[0] // parts
        self.s1, self.r1, self.s2, self.r2, self.local = sems

    @staticmethod
    def scratch(chips, parts, name):
        dma = pltpu.SemaphoreType.DMA
        specs = [dma((chips, parts)), dma((chips, parts)), dma((chips - 1, parts)), dma((chips - 1, parts)), dma((1,))]
        return {name + str(index): spec for index, spec in enumerate(specs)}

    def far(self, ahead, part):
        rows = pl.ds(part * self.size, self.size)
        sems = (self.s2.at[ahead - 1, part], self.r2.at[ahead - 1, part])
        return remote(self.own.at[rows], self.ref.at[self.place.tp, rows], *sems, self.place.peer(ahead))

    def near(self, ahead, part):
        place = self.place
        rows = pl.ds(part * self.size, self.size)
        device = lax.rem(place.x + place.chips - ahead, place.chips) * 2 + place.core
        src = self.ref.at[device, rows] if ahead else self.own.at[rows]
        sems = (self.s1.at[ahead, part], self.r1.at[ahead, part])
        return remote(src, self.ref.at[device, rows], *sems, place.mate)

    def keep(self):
        return pltpu.make_async_copy(self.own, self.ref.at[self.place.tp], self.local.at[0])

    def start(self):
        self.keep().start()
        for part in range(self.parts):
            for ahead in range(1, self.place.chips):
                self.far(ahead, part).start()
            self.near(0, part).start()

    def relay(self):
        for ahead in range(1, self.place.chips):
            for part in range(self.parts):
                self.far(ahead, part).wait_recv()
                self.near(ahead, part).start()

    def end(self):
        self.keep().wait()
        for part in range(self.parts):
            for ahead in range(self.place.chips):
                self.near(ahead, part).wait_recv()

    def drain(self):
        for part in range(self.parts):
            for ahead in range(1, self.place.chips):
                self.far(ahead, part).wait_send()
            for ahead in range(self.place.chips):
                self.near(ahead, part).wait_send()


class SeqSum:
    ROWS = 4

    def __init__(self, place, slot, r, name):
        self.place, self.slot = place, slot
        self.near_recv, self.ns, self.nr, self.low, self.mid, self.first, self.second, self.fs, self.fr = [
            getattr(r, name + str(index), None) for index in range(9)
        ]
        self.inner = place.seqs // self.ROWS
        self.row, self.column = place.seq // self.inner, lax.rem(place.seq, self.inner)

    @staticmethod
    def scratch(seqs, dims, dtype, name, near=True, low=True, far=True):
        dma = pltpu.SemaphoreType.DMA
        rows, inner = SeqSum.ROWS, seqs // SeqSum.ROWS
        specs = [
            pltpu.VMEM((inner - 1, rows, *dims), dtype) if near else None,
            dma((inner - 1, rows)) if near else None,
            dma((inner - 1, rows)) if near else None,
            pltpu.VMEM((rows, *dims), dtype) if low else None,
            pltpu.VMEM(dims, dtype) if far else None,
            pltpu.VMEM((2, *dims), dtype) if far else None,
            pltpu.VMEM((1, *dims), dtype) if far else None,
            dma((3,)) if far else None,
            dma((3,)) if far else None,
        ]
        return {name + str(index): spec for index, spec in enumerate(specs) if spec is not None}

    def other_row(self, differs):
        bit, half = lax.rem(self.row, 2), self.row // 2
        return (self.row, self.row + 1 - 2 * bit, self.row + 2 - 4 * half, 3 - self.row)[differs]

    def shard(self, differs, column_ahead=0):
        return self.other_row(differs) * self.inner + lax.rem(self.column + column_ahead, self.inner)

    def near(self, ahead, differs):
        at = (ahead - 1, differs)
        to = {"seq": self.shard(0, ahead)}
        return remote(self.slot(self.shard(differs, ahead)), self.near_recv.at[at], self.ns.at[at], self.nr.at[at], to)

    def each_near(self, act):
        for ahead in range(1, self.inner):
            for differs in (1, 3, 2, 0):
                act(self.near(ahead, differs))

    def start(self):
        self.each_near(lambda copy: copy.start())

    def exchange(self, index):
        sems = (self.fs.at[index], self.fr.at[index])
        if index == 2:
            return remote(self.mid, self.second.at[0], *sems, {"seq": self.shard(2)})
        return remote(self.low.at[(1, 3)[index]], self.first.at[index], *sems, {"seq": self.shard(1)})

    def fetch(self, sems):
        return [
            pltpu.make_async_copy(self.slot(self.shard(differs)), self.low.at[differs], sems.at[differs])
            for differs in range(self.ROWS)
        ]

    def column_rows(self, differs, fetched):
        rows = (self.low.at[differs] if fetched else self.slot(self.shard(differs)))[...].astype(F32)
        for ahead in range(1, self.inner):
            self.near(ahead, differs).wait_recv()
            rows = rows + self.near_recv[ahead - 1, differs].astype(F32)
        return rows

    def combine(self, out, fetched=False, rows_of=None, go=True):
        rows_of = rows_of or (lambda differs: self.column_rows(differs, fetched))
        for differs in (1, 3):
            self.low[differs] = rows_of(differs).astype(self.low.dtype)
            if go:
                self.exchange(differs // 2).start()
        if go:
            self.mid[...] = rows_of(2).astype(self.mid.dtype)
        else:
            self.low[2] = rows_of(2).astype(self.low.dtype)
        out[...] = rows_of(0)

    def middle(self, out):
        self.exchange(1).wait_recv()
        self.mid[...] = (self.mid[...].astype(F32) + self.first[1].astype(F32)).astype(self.mid.dtype)
        self.exchange(2).start()
        self.exchange(0).wait_recv()
        out[...] = out[...] + self.first[0].astype(F32)

    def finish(self, out):
        self.exchange(2).wait_recv()
        out[...] = out[...] + self.second[0].astype(F32)

    def end(self, near=True, far=True):
        if near:
            self.each_near(lambda copy: copy.wait_send())
        if far:
            for index in range(3):
                self.exchange(index).wait_send()


def head_masks():
    lane = lax.broadcasted_iota(jnp.int32, (1, PAIR), 1)
    first = (lane < HEAD_DIM).astype(F32)
    return first, 1.0 - first


def pair_lanes(pair):
    return pl.ds(pl.multiple_of(pair * PAIR, PAIR), PAIR)


def block_rows(block):
    return pl.ds(pl.multiple_of(block * BLOCK, BLOCK), BLOCK)


def causal_tile(keys_first):
    rows = lax.broadcasted_iota(jnp.int32, (BLOCK, BLOCK), 0)
    columns = lax.broadcasted_iota(jnp.int32, (BLOCK, BLOCK), 1)
    allowed = rows <= columns if keys_first else columns <= rows
    return jnp.where(allowed, 0.0, NEG)


def attend(q_ref, block, keys, values, biases, mixed_ref, lse_ref):
    masks = head_masks()
    rows = block_rows(block)
    lane = lax.broadcasted_iota(jnp.int32, (BLOCK, 128), 1)

    def step(pair):
        lanes = pair_lanes(pair)
        queries = q_ref[rows, lanes]
        pair_out = jnp.zeros((BLOCK, PAIR), F32)
        lse_block = jnp.zeros((BLOCK, 128), F32)
        for head in range(2):
            head_queries = queries * masks[head].astype(BF16)
            scores = [dot_nt(head_queries, keys(tile, lanes)) + bias() for tile, bias in enumerate(biases)]
            top = functools.reduce(jnp.maximum, [jnp.max(s, axis=-1, keepdims=True) for s in scores])
            total, out = 0.0, 0.0
            for tile, s in enumerate(scores):
                weights = jnp.exp(s - top)
                total = total + jnp.sum(weights, axis=-1, keepdims=True)
                out = out + dot(weights.astype(BF16), values(tile, lanes))
            pair_out = pair_out + out * masks[head] / total
            lse_block = jnp.where(lane == head, top + jnp.log(total), lse_block)
        mixed_ref[rows, lanes] = pair_out.astype(BF16)
        lse_ref[pair, :, rows] = jnp.transpose(lse_block)[:8]

    loop(q_ref.shape[1] // PAIR, step)


def dots_out(grad_ref, mixed_ref, block, dots_ref):
    masks = head_masks()
    rows = block_rows(block)
    lane = lax.broadcasted_iota(jnp.int32, (BLOCK, 128), 1)
    for pair in range(grad_ref.shape[1] // PAIR):
        lanes = pair_lanes(pair)
        product = grad_ref[rows, lanes].astype(F32) * mixed_ref[rows, lanes].astype(F32)
        values = jnp.zeros((BLOCK, 128), F32)
        for head in range(2):
            value = jnp.sum(product * masks[head], axis=-1, keepdims=True)
            values = jnp.where(lane == head, value, values)
        dots_ref[pair, :, rows] = jnp.transpose(values)[:8]


def attend_back(q_ref, grad_ref, lse_ref, dots_ref, block, pair, keys, values, bias):
    masks = head_masks()
    lanes, rows = pair_lanes(pair), block_rows(block)
    queries, grads = q_ref[rows, lanes], grad_ref[rows, lanes]
    dq = dk = dv = 0.0
    for head in range(2):
        mask = masks[head].astype(BF16)
        head_queries, head_grads, head_keys = queries * mask, grads * mask, keys * mask
        scores = dot_nt(keys, head_queries) + bias()
        weights = jnp.exp(scores - lse_ref[pair, head : head + 1, rows])
        grad_weights = dot_nt(values, head_grads)
        grad_scores = (weights * (grad_weights - dots_ref[pair, head : head + 1, rows])).astype(BF16)
        dv = dv + dot(weights.astype(BF16), head_grads)
        dk = dk + dot(grad_scores, head_queries)
        dq = dq + dot_tn(grad_scores, head_keys)
    return dq * HEAD_DIM ** (-0.5), dk, dv


def grad_weight(out_ref, first, left_ref, *rights):
    count = left_ref.shape[1]
    step_size = min(256, count)
    width = sum(right.shape[1] for right in rights)

    def step(index):
        columns = pl.ds(pl.multiple_of(index * step_size, step_size), step_size)
        right = rights[0][...] if len(rights) == 1 else jnp.concatenate([right[...] for right in rights], axis=1)
        out_ref[columns, first : first + width] = dot_tn(left_ref[:, columns], right).astype(BF16)

    loop(count // step_size, step)


def scaled(queries):
    return (queries.astype(BF16).astype(F32) * HEAD_DIM ** (-0.5)).astype(BF16)


def half_rows(slot):
    return pl.ds(pl.multiple_of(slot * CHUNK, CHUNK), CHUNK)


def reach_bias(offsets, block, tile):
    return jnp.where(offsets[block * BLOCK] >= (REACH - tile) * BLOCK, 0.0, NEG)


def norm_step(place, r, sums, share, base, res):
    def finish(slot, carry):
        hat, inv_std = hat_of(res[half_rows(slot), :])
        grad_in, gain_sum, shift_sum = norm_back(sums.take(slot), hat, inv_std, r.gain[...])
        rows = base(slot) + grad_in
        r.grad.ref[half_rows(slot), :] = rows
        share.put(slot, rows.astype(BF16))
        return carry[0] + gain_sum, carry[1] + shift_sum

    zero = jnp.zeros((1, r.gain.shape[1]), F32)
    gain_sum, shift_sum = lax.fori_loop(0, place.chunks, finish, (zero, zero))
    r.norm[0:1, :] = gain_sum
    r.norm[1:2, :] = shift_sum


def open_body(chips, seqs, r):
    n1, half = r.n1.ref, (r.half.ref, r.prev.ref)
    tokens = n1.shape[0] // 2
    place = Place(chips, seqs, tokens)
    place.enter(seq="all")
    n, piece = place.per_piece, place.piece
    own_rows = pl.ds(pl.multiple_of(place.x * piece, CHUNK), piece)

    def half_part(chip, part):
        return pl.ds(pl.multiple_of(chip * piece + part * CHUNK, CHUNK), CHUNK)

    def far(which, ahead, part):
        dst = half[which].at[half_part(place.x, part)]
        src = dst if which else r.x.at[pl.ds(part * CHUNK, CHUNK)]
        at = (which, ahead - 1, part)
        return remote(src, dst, r.s2.at[at], r.r2.at[at], place.peer(ahead))

    def pass_on(part):
        src, dst = r.x.at[pl.ds(part * CHUNK, CHUNK)], half[1].at[half_part(place.x, part)]
        return remote(src, dst, r.ss.at[part], r.sr.at[part], {"seq": place.seq + 1})

    def parts(act):
        for part in range(n):
            act(part)

    pl.when(place.has_next)(lambda: parts(lambda part: pass_on(part).start()))
    for part in range(n):
        for ahead in range(1, chips):
            far(0, ahead, part).start()
    grads = Gather(place, r.og_own, r.og, n, [getattr(r, "og_" + str(i)) for i in range(5)])
    grads.start()

    columns = pl.ds(pl.multiple_of(place.tp * r.mem.shape[3], 128), r.mem.shape[3])
    rows_apart = SeqSum.ROWS
    inner = seqs // rows_apart
    seq_row, seq_column = place.seq // inner, lax.rem(place.seq, inner)

    def mem_far(ahead):
        to = {"seq": lax.rem(seq_row + ahead, rows_apart) * inner + seq_column}
        sems = (r.fs.at[ahead - 1], r.fr.at[ahead - 1])
        return remote(r.memory.at[0, :, columns], r.mem.at[place.seq, 0], *sems, to)

    def mem_near(behind, ahead):
        row = lax.rem(seq_row + rows_apart - behind, rows_apart)
        to = {"seq": seq_row * inner + lax.rem(seq_column + ahead, inner)}
        dst = r.mem.at[row * inner + seq_column, 0]
        src = dst if behind else r.memory.at[0, :, columns]
        sems = (r.ns.at[behind, ahead - 1], r.nr.at[behind, ahead - 1])
        return remote(src, dst, *sems, to)

    def mem_pass(behind):
        mem_far(behind).wait_recv()
        for ahead in range(1, inner):
            mem_near(behind, ahead).start()

    def known_copies(ahead):
        to = {"seq": place.shard(ahead)}
        at = [(which, ahead - 1) for which in range(2)]
        return (
            remote(r.mask, r.masks.at[place.seq], r.ms.at[at[0]], r.mr.at[at[0]], to),
            remote(r.page_row, r.pages.at[place.seq], r.ms.at[at[1]], r.mr.at[at[1]], to),
        )

    def known_all(act):
        def step(index):
            for copy in known_copies(index + 1):
                act(copy)

        loop(seqs - 1, step)

    lane = lax.broadcasted_iota(jnp.int32, r.page_row.shape, 1)
    page_row = jnp.zeros(r.page_row.shape, jnp.int32)
    for block in range(tokens // BLOCK):
        page_row = jnp.where(lane == block, r.ids[block * BLOCK], page_row)
    r.page_row[...] = page_row
    own_copies = [
        pltpu.make_async_copy(r.memory.at[0, :, columns], r.mem.at[place.seq, 0], r.local.at[0]),
        pltpu.make_async_copy(r.mask, r.masks.at[place.seq], r.local.at[1]),
        pltpu.make_async_copy(r.page_row, r.pages.at[place.seq], r.local.at[2]),
    ]
    for copy in own_copies:
        copy.start()
    for ahead in (1, 3, 2):
        mem_far(ahead).start()
    for ahead in range(1, inner):
        mem_near(0, ahead).start()
    known_all(lambda copy: copy.start())
    half[0][own_rows, :] = r.x[...]

    def from_chip(ahead):
        return lax.rem(place.x + chips - ahead, chips)

    def near(which, ahead, part):
        row = pl.multiple_of((from_chip(ahead) * 2 + place.core) * piece + part * CHUNK, CHUNK)
        rows = n1.at[pl.ds((1 - which) * tokens + row, CHUNK)]
        at = (which, ahead, part)
        return remote(rows, rows, r.s1.at[at], r.r1.at[at], place.mate)

    def normed(which, ahead, part):
        chip = from_chip(ahead)
        hat, _ = hat_of(half[which][half_part(chip, part), :].astype(F32))
        row = pl.multiple_of((chip * 2 + place.core) * piece + part * CHUNK, CHUNK)
        n1[pl.ds((1 - which) * tokens + row, CHUNK), :] = (hat * r.gain[...] + r.shift[...]).astype(BF16)
        near(which, ahead, part).start()

    def project(which, ahead):
        for part in range(n):
            near(which, ahead, part).wait_recv()
        chip = from_chip(ahead)
        row = pl.multiple_of(chip * 2 * piece, CHUNK)
        rows = pl.ds((1 - which) * tokens + row, 2 * piece)
        rows_in = n1[rows, :]
        r.kext[rows, :] = dot(rows_in, r.wk[...]).astype(BF16)
        r.vext[rows, :] = dot(rows_in, r.wv[...]).astype(BF16)
        if not which:
            r.q[pl.ds(row, 2 * piece), :] = scaled(dot(rows_in, r.wq[...]))

    def step(which, ahead):
        for part in range(n):
            if ahead:
                far(which, ahead, part).wait_recv()
            normed(which, ahead, part)
        project(which, ahead)

    step(0, 0)
    mem_pass(1)
    for ahead in range(1, chips):
        step(0, ahead)
    r.half.start()
    mem_pass(3)

    @pl.when(jnp.logical_not(place.has_prev))
    def _():
        half[1][own_rows, :] = jnp.zeros((piece, n1.shape[1]), BF16)

    pl.when(place.has_prev)(lambda: parts(lambda part: pass_on(part).wait_recv()))
    for part in range(n):
        for ahead in range(1, chips):
            far(1, ahead, part).start()
    grads.relay()
    step(1, 0)
    mem_pass(2)
    for ahead in range(1, chips):
        step(1, ahead)
    r.prev.start()
    r.n1.start()
    for part in range(n):
        for which in range(2):
            for ahead in range(1, chips):
                far(which, ahead, part).wait_send()
            for ahead in range(chips):
                near(which, ahead, part).wait_send()
    pl.when(place.has_next)(lambda: parts(lambda part: pass_on(part).wait_send()))
    grads.end()
    grads.drain()
    for copy in own_copies:
        copy.wait()
    for behind in range(1, rows_apart):
        mem_far(behind).wait_send()
    for behind in range(rows_apart):
        for ahead in range(1, inner):
            mem_near(behind, ahead).wait()
    known_all(lambda copy: copy.wait())


def opening(chips, seqs, ids, x, og, memory, mask, gain, shift, wq, wk, wv):
    width, dim = wq.shape[1], x.shape[1]
    tokens = ids.shape[0]
    n = tokens // (2 * chips) // CHUNK
    rows, inner = SeqSum.ROWS, seqs // SeqSum.ROWS
    dma = pltpu.SemaphoreType.DMA
    vmem = lambda array: (array, "vmem")
    return call(
        functools.partial(open_body, chips, seqs),
        "opening",
        dict(
            ids=(ids, "smem"),
            x=vmem(x),
            og_own=(og, "hbm"),
            memory=(memory, "hbm"),
            mask=vmem(mask),
            gain=vmem(gain),
            shift=vmem(shift),
            wq=vmem(wq),
            wk=vmem(wk),
            wv=vmem(wv),
        ),
        dict(
            n1=((2 * tokens, dim), BF16, "late"),
            half=((tokens // 2, dim), BF16, "late"),
            prev=((tokens // 2, dim), BF16, "late"),
            q=((tokens, width), BF16, "vmem"),
            kext=((2 * tokens, width), BF16, "vmem"),
            vext=((2 * tokens, width), BF16, "vmem"),
            mem=((seqs, 1, memory.shape[1], dim // (2 * chips)), BF16, "hbm"),
            masks=((seqs, 1, mask.shape[1]), jnp.int32, "vmem"),
            pages=((seqs, 8, 128), jnp.int32, "vmem"),
            og=((2 * chips, tokens // (2 * chips), dim), BF16, "hbm"),
        ),
        dict(
            s1=dma((2, chips, n)),
            r1=dma((2, chips, n)),
            s2=dma((2, chips - 1, n)),
            r2=dma((2, chips - 1, n)),
            ss=dma((n,)),
            sr=dma((n,)),
            ms=dma((2, seqs - 1)),
            mr=dma((2, seqs - 1)),
            fs=dma((rows - 1,)),
            fr=dma((rows - 1,)),
            ns=dma((rows, inner - 1)),
            nr=dma((rows, inner - 1)),
            local=dma((3,)),
            page_row=pltpu.VMEM((8, 128), jnp.int32),
            **Gather.scratch(chips, n, "og_"),
        ),
        0,
        10 * tokens * dim * width,
    )


def forward_body(chips, seqs, r):
    tokens = r.q.shape[0]
    place = Place(chips, seqs, tokens)
    place.enter(seq="row")
    piece, blocks = place.piece, tokens // BLOCK
    per_block, chips_per_block = place.chunks // blocks, chips // blocks
    mem_true = r.mem8.shape[2]
    keys = r.mem_k.shape[0] // blocks
    stages = [Sums(place, r, stage=stage) for stage in range(3)]
    mem = r.mem.ref

    r.mem_own[...] = jnp.zeros_like(r.mem_own)
    r.bias[...] = jnp.full(r.bias.shape, NEG, F32)
    for block in range(blocks):
        rows = pl.ds(block * keys, mem_true)

        def choose(page):
            r.mem_own[rows, :] = jnp.where(r.ids[block * BLOCK] == page, r.mem8[page, 0], r.mem_own[rows, :])

        def mask_of(page, mask):
            return jnp.where(r.ids[block * BLOCK] == page, r.masks[page], mask)

        loop(seqs, choose)
        mask = lax.fori_loop(0, seqs, mask_of, jnp.zeros((1, mem_true), jnp.int32))
        r.bias[block, :, :mem_true] = jnp.broadcast_to(jnp.where(mask > 0, 0.0, NEG), (8, mem_true))
    memory = Gather(place, r.mem_own, mem, 4, [getattr(r, "mem_" + str(i)) for i in range(5)])
    memory.start()
    r.causal[...] = causal_tile(False)

    def self_block(block):
        biases = [functools.partial(reach_bias, r.offsets, block, tile) for tile in range(REACH)]
        attend(
            r.q,
            block,
            lambda tile, lanes: r.kext[block_rows(block + tile), lanes],
            lambda tile, lanes: r.vext[block_rows(block + tile), lanes],
            biases + [lambda: r.causal[...]],
            r.mixed1,
            r.lse1,
        )
        stages[0].all_pieces(
            block * chips_per_block, chips_per_block, lambda row: dot(r.mixed1[pl.ds(row, piece), :], r.wo[...])
        )

    loop(blocks, self_block)

    memory.relay()
    memory.end()
    wide = mem.shape[2]
    for weight, out in ((r.wck, r.mem_k), (r.wcv, r.mem_v)):
        rows = 0.0
        for device in range(2 * chips):
            rows = rows + dot(mem[device], weight[device * wide : (device + 1) * wide, :])
        out[...] = rows.astype(BF16)
    r.mem.start()

    half = r.half.wait()
    n2, res1, res2 = r.n2.ref, r.res1.ref, r.res2.ref
    share = Share(place, n2, r.ss, r.sr, 0)

    def finish_self(slot):
        rows = half[half_rows(slot), :].astype(F32) + stages[0].take(slot)
        res1[half_rows(slot), :] = rows
        hat, _ = hat_of(rows)
        share.put(slot, (hat * r.cross_gain[...] + r.cross_shift[...]).astype(BF16))

    cross_query, cross_output = r.wq.wait(), r.wco.wait()

    def cross_block(block):
        loop(per_block, lambda index: finish_self(block * per_block + index))
        share.end(block * per_block, per_block)
        rows = block_rows(block)
        page = pl.ds(pl.multiple_of(block * keys, 128), keys)
        r.q2[rows, :] = scaled(dot(n2[rows, :], cross_query[...]))
        attend(
            r.q2,
            block,
            lambda tile, lanes: r.mem_k[page, lanes],
            lambda tile, lanes: r.mem_v[page, lanes],
            [lambda: r.bias[block, 0:1, :]],
            r.mixed2,
            r.lse2,
        )
        stages[1].all_pieces(
            block * chips_per_block,
            chips_per_block,
            lambda row: dot(r.mixed2[pl.ds(row, piece), :], cross_output[...]),
        )

    loop(blocks, cross_block)
    r.n2.start()
    r.res1.start()

    share_ffn = Share(place, r.n3, r.ss, r.sr, 1)
    up, down, og = r.up.wait(), r.down.wait(), r.og.wait()
    act = r.act.ref

    def finish_cross(slot):
        rows = res1[half_rows(slot), :] + stages[1].take(slot)
        res2[half_rows(slot), :] = rows
        hat, _ = hat_of(rows)
        share_ffn.put(slot, (hat * r.gain[...] + r.shift[...]).astype(BF16))

    def term(row):
        rows = pl.ds(row, piece)
        pre = dot(r.n3[rows, :], up[...])
        half_erf = 0.5 * lax.erf(pre * (0.5**0.5)) + 0.5
        act[rows, :] = (pre * half_erf).astype(BF16)
        slope = half_erf + pre * jnp.exp(-0.5 * pre * pre) * (0.15915494309189535**0.5)
        grad_act = dot_nt(og[rows, :], down[...])
        low = (grad_act * slope).astype(BF16)
        r.gpre[rows, :] = low
        return dot_nt(low, up[...])

    def ffn_block(block):
        loop(per_block, lambda index: finish_cross(block * per_block + index))
        share_ffn.end(block * per_block, per_block)
        stages[2].all_pieces(block * chips_per_block, chips_per_block, term)

    loop(blocks, ffn_block)
    r.res2.start()
    r.act.start()
    grad_weight(r.g_down, 0, og, act)
    share_rows = r.down_own.shape[0]
    seq_down = SeqSum(
        place, lambda shard: r.g_down.at[pl.ds(pl.multiple_of(shard * share_rows, 8), share_rows)], r, "down_"
    )
    seq_down.low = r.down_low
    seq_down.start()
    grad_weight(r.g_up.ref, 0, r.n3, r.gpre)
    r.g_up.start()

    share_grad = Share(place, r.g.ref, r.ss, r.sr, 2)
    norm_step(
        place,
        r,
        stages[2],
        share_grad,
        lambda slot: og[pl.ds(place.row(slot, place.core), CHUNK), :].astype(F32),
        res2,
    )
    r.grad.start()
    share_grad.end(0, place.chunks)
    r.g.start()
    seq_down.combine(r.down_own, go=False)
    seq_down.end(far=False)
    memory.drain()


def forward(chips, seqs, ids, offsets, a, w):
    tokens, width = a.q.shape
    dim, hidden = w.up.shape
    chunks = tokens // 2 // CHUNK
    blocks = tokens // BLOCK
    mem_true, wide = a.mem.shape[2:]
    keys = -(-mem_true // 128) * 128
    dma = pltpu.SemaphoreType.DMA
    vmem = lambda array: (array, "vmem")
    late = lambda array: (array, "late")
    return call(
        functools.partial(forward_body, chips, seqs),
        "forward",
        dict(
            ids=(ids, "smem"),
            offsets=(offsets, "smem"),
            q=vmem(a.q),
            kext=vmem(a.kext),
            vext=vmem(a.vext),
            mem8=vmem(a.mem),
            masks=vmem(a.masks),
            wo=vmem(w.attn_output),
            wck=vmem(w.cross_key),
            wcv=vmem(w.cross_value),
            cross_gain=vmem(w.cross_gain),
            cross_shift=vmem(w.cross_shift),
            gain=vmem(w.ffn_gain),
            shift=vmem(w.ffn_shift),
            half=late(a.half),
            wq=late(w.cross_query),
            wco=late(w.cross_output),
            up=late(w.up),
            og=late(a.og.reshape(tokens, dim)),
            down=late(w.down),
        ),
        dict(
            mixed1=((tokens, width), BF16, "vmem"),
            lse1=((width // PAIR, 8, tokens), F32, "vmem"),
            res1=((tokens // 2, dim), F32, "late"),
            n2=((tokens, dim), BF16, "late"),
            mem=((2 * chips, blocks * keys, wide), BF16, "late"),
            mem_k=((blocks * keys, width), BF16, "vmem"),
            mem_v=((blocks * keys, width), BF16, "vmem"),
            bias=((blocks, 8, keys), F32, "vmem"),
            q2=((tokens, width), BF16, "vmem"),
            mixed2=((tokens, width), BF16, "vmem"),
            lse2=((width // PAIR, 8, tokens), F32, "vmem"),
            res2=((tokens // 2, dim), F32, "late"),
            act=((tokens, hidden), BF16, "late"),
            grad=((tokens // 2, dim), F32, "late"),
            g=((tokens, dim), BF16, "late"),
            norm=((2, dim), F32, "vmem"),
            g_up=((dim, hidden), BF16, "late"),
            down_low=((SeqSum.ROWS, dim // seqs, hidden), BF16, "vmem"),
            down_own=((dim // seqs, hidden), F32, "vmem"),
        ),
        dict(
            **sum_scratch(chips, tokens, dim, stages=3),
            **Gather.scratch(chips, 4, "mem_"),
            mem_own=pltpu.VMEM((blocks * keys, wide), BF16),
            causal=pltpu.VMEM((BLOCK, BLOCK), F32),
            **SeqSum.scratch(seqs, (dim // seqs, hidden), BF16, "down_", low=False, far=False),
            g_down=pltpu.VMEM((dim, hidden), BF16),
            n3=pltpu.VMEM((tokens, dim), BF16),
            gpre=pltpu.VMEM((tokens, hidden), BF16),
            ss=dma((3, chunks)),
            sr=dma((3, chunks)),
        ),
        1,
        14 * tokens * dim * hidden,
    )


def cross_back_body(chips, seqs, r):
    tokens = r.g_in.shape[0]
    place = Place(chips, seqs, tokens)
    place.enter(seq="all")
    piece, n, blocks = place.piece, place.per_piece, tokens // BLOCK
    share_rows = r.sum_down.shape[0]
    keys = r.mem_k.shape[0] // blocks
    mine = lambda ref: (lambda shard: ref.at[pl.ds(pl.multiple_of(shard * share_rows, 8), share_rows)])
    seq_down = SeqSum(place, None, r, "down_")
    seq_down.low = r.down_low
    fetch_down = [
        pltpu.make_async_copy(r.down_low.at[2], seq_down.mid, r.fetch.at[0, 0]),
        pltpu.make_async_copy(r.down_own, r.sum_down, r.fetch.at[0, 1]),
    ]
    seq_up = SeqSum(place, mine(r.g_up), r, "up_")
    fetch_up = seq_up.fetch(r.fetch.at[1])
    base = pltpu.make_async_copy(r.res_out.at[pl.ds(place.x * piece, piece)], r.base, r.fetch.at[2, 0])
    base.start()
    for index in range(2):
        seq_down.exchange(index).start()
    seq_up.start()
    for copy in fetch_down + fetch_up:
        copy.start()
    sums = Sums(place, r)

    def step(block):
        rows = block_rows(block)
        page = pl.ds(pl.multiple_of(block * keys, 128), keys)
        r.dout[rows, :] = dot_nt(r.g_in[rows, :], r.wo[...]).astype(BF16)
        dots_out(r.dout, r.mixed, block, r.dots)
        bias = jnp.transpose(r.bias[block])[:, 0:1]

        def pair_step(pair):
            lanes = pair_lanes(pair)
            dq, dk, dv = attend_back(
                r.q,
                r.dout,
                r.lse,
                r.dots,
                block,
                pair,
                r.mem_k[page, lanes],
                r.mem_v[page, lanes],
                lambda: bias,
            )
            r.gq[rows, lanes] = dq.astype(BF16)
            r.gk[page, lanes] = dk.astype(BF16)
            r.gv[page, lanes] = dv.astype(BF16)

        loop(r.q.shape[1] // PAIR, pair_step)
        sums.all_pieces(
            block * (chips // blocks),
            chips // blocks,
            lambda row: dot_nt(r.gq[pl.ds(row, piece), :], r.wq[...]),
        )

    loop(blocks, step)

    width = r.q.shape[1]
    wide = r.mem_sum.shape[1]

    def mem_part(chip, core):
        rows = pl.ds(pl.multiple_of((chip * 2 + core) * wide, wide), wide)
        return dot_nt(r.gk[...], r.wck[rows, :]) + dot_nt(r.gv[...], r.wcv[rows, :])

    def mem_near(ahead):
        return remote(r.mem_out.at[ahead], r.mem_mate.at[ahead], r.mns.at[ahead], r.mnr.at[ahead], place.mate)

    def mem_far(ahead):
        sems = (r.mfs.at[ahead - 1], r.mfr.at[ahead - 1])
        return remote(r.mem_mate.at[ahead], r.mem_far.at[ahead - 1], *sems, place.peer(ahead))

    for ahead in range(chips):
        r.mem_out[ahead] = mem_part(place.chip(ahead), 1 - place.core).astype(BF16)
        mem_near(ahead).start()
    for ahead in range(1, chips):
        rows = mem_part(place.chip(ahead), place.core)
        mem_near(ahead).wait_recv()
        r.mem_mate[ahead] = (rows + r.mem_mate[ahead].astype(F32)).astype(BF16)
        mem_far(ahead).start()
    rows = mem_part(place.x, place.core)
    mem_near(0).wait_recv()
    r.mem_sum[...] = rows + r.mem_mate[0].astype(F32)
    for copy in fetch_down:
        copy.wait()
    seq_down.middle(r.sum_down)

    hidden = Sums(place, r, "hidden_")
    act, down = r.act.wait(), r.down.wait()
    hidden.own_pieces(lambda row: dot(act[pl.ds(row, piece), :], down[...]), go=False)
    base.wait()
    for part in range(n):
        rows = pl.ds(part * CHUNK, CHUNK)
        r.out_own[rows, :] = r.base[rows, :] + hidden.own[part]
        for ahead in range(1, chips):
            r.out_low[ahead - 1, part] = hidden.low[ahead * n + part]

    n2, mem = r.n2.wait(), r.mem.wait()
    g_w = r.g_w

    def mem_step(device):
        rows = pl.ds(pl.multiple_of(device * wide, wide), wide)
        both = jnp.concatenate([r.gk[...], r.gv[...]], axis=1)
        g_w[rows, width : 3 * width] = dot_tn(mem[device], both).astype(BF16)

    loop(2 * chips, mem_step)
    grad_weight(g_w, 0, n2, r.gq)
    grad_weight(g_w, 3 * width, r.g_in, r.mixed)
    seq_cross = SeqSum(place, mine(g_w), r, "cross_")
    seq_cross.low = r.cross_low
    seq_cross.start()

    for copy in fetch_up:
        copy.wait()
    seq_up.combine(r.sum_up, fetched=True)
    share = Share(place, r.g.ref, r.s1, r.r1)
    res, grad_in = r.res.wait(), r.grad_in.wait()
    norm_step(place, r, sums, share, lambda slot: grad_in[half_rows(slot), :], res)
    r.grad.start()
    share.end(0, place.chunks)
    r.g.start()
    seq_up.middle(r.sum_up)
    for ahead in range(1, chips):
        mem_far(ahead).wait_recv()
        r.mem_sum[...] = r.mem_sum[...] + r.mem_far[ahead - 1].astype(F32)
    seq_down.finish(r.sum_down)
    seq_up.finish(r.sum_up)
    seq_cross.combine(r.cross_own, go=False)
    seq_down.end(near=False)
    seq_up.end()
    seq_cross.end(far=False)
    hidden.own_end(far=False)
    for ahead in range(chips):
        mem_near(ahead).wait_send()
    for ahead in range(1, chips):
        mem_far(ahead).wait_send()


def cross_back(chips, seqs, a, f, w):
    tokens, dim = f.g.shape
    width = f.q2.shape[1]
    hidden = f.act.shape[1]
    chunks = tokens // 2 // CHUNK
    mem_rows = f.mem_k.shape[0]
    rows = SeqSum.ROWS
    dma = pltpu.SemaphoreType.DMA
    vmem = lambda array: (array, "vmem")
    late = lambda array: (array, "late")
    hbm = lambda array: (array, "hbm")
    return call(
        functools.partial(cross_back_body, chips, seqs),
        "cross_back",
        dict(
            g_in=vmem(f.g),
            wo=vmem(w.cross_output),
            q=vmem(f.q2),
            mem_k=vmem(f.mem_k),
            mem_v=vmem(f.mem_v),
            bias=vmem(f.bias),
            mixed=vmem(f.mixed2),
            lse=vmem(f.lse2),
            wq=vmem(w.cross_query),
            gain=vmem(w.cross_gain),
            wck=vmem(w.cross_key),
            wcv=vmem(w.cross_value),
            act=late(f.act),
            down=late(w.down),
            mem=late(f.mem),
            n2=late(f.n2),
            res=late(f.res1),
            grad_in=late(f.grad),
            res_out=hbm(f.res2),
            g_up=hbm(f.g_up),
            down_low=hbm(f.down_low),
            down_own=hbm(f.down_own),
        ),
        dict(
            grad=((tokens // 2, dim), F32, "late"),
            g=((tokens, dim), BF16, "late"),
            norm=((2, dim), F32, "vmem"),
            cross_low=((rows, dim // seqs, 4 * width), BF16, "vmem"),
            cross_own=((dim // seqs, 4 * width), F32, "vmem"),
            mem_sum=((mem_rows, f.mem.shape[2]), F32, "vmem"),
            sum_up=((dim // seqs, hidden), F32, "vmem"),
            sum_down=((dim // seqs, hidden), F32, "vmem"),
            out_own=((tokens // (2 * chips), dim), F32, "vmem"),
            out_low=((chips - 1, tokens // (2 * chips) // CHUNK, CHUNK, dim), BF16, "vmem"),
        ),
        dict(
            **sum_scratch(chips, tokens, dim),
            **sum_scratch(chips, tokens, dim, "hidden_"),
            **SeqSum.scratch(seqs, (dim // seqs, 4 * width), BF16, "cross_", low=False, far=False),
            g_w=pltpu.VMEM((dim, 4 * width), BF16),
            **SeqSum.scratch(seqs, (dim // seqs, hidden), BF16, "up_"),
            **SeqSum.scratch(seqs, (dim // seqs, hidden), BF16, "down_", near=False, low=False),
            mem_out=pltpu.VMEM((chips, mem_rows, f.mem.shape[2]), BF16),
            mem_mate=pltpu.VMEM((chips, mem_rows, f.mem.shape[2]), BF16),
            mem_far=pltpu.VMEM((chips - 1, mem_rows, f.mem.shape[2]), BF16),
            mns=dma((chips,)),
            mnr=dma((chips,)),
            mfs=dma((chips - 1,)),
            mfr=dma((chips - 1,)),
            gq=pltpu.VMEM((tokens, width), BF16),
            gk=pltpu.VMEM((mem_rows, width), BF16),
            gv=pltpu.VMEM((mem_rows, width), BF16),
            dout=pltpu.VMEM((tokens, width), BF16),
            dots=pltpu.VMEM((width // PAIR, 8, tokens), F32),
            base=pltpu.VMEM((tokens // (2 * chips), dim), F32),
            s1=dma((1, chunks)),
            r1=dma((1, chunks)),
            fetch=dma((3, rows)),
        ),
        2,
        12 * tokens * dim * width,
    )


def close_body(chips, seqs, r):
    tokens, width = r.q.shape
    place = Place(chips, seqs, tokens)
    place.enter(seq="all", all_tp=True)
    piece, n, blocks = place.piece, place.per_piece, tokens // BLOCK
    pairs = width // PAIR
    share_rows = r.sum_w.shape[0]
    mine = lambda ref: (lambda shard: ref.at[pl.ds(pl.multiple_of(shard * share_rows, 8), share_rows)])

    mem_rows = r.mem_sum.shape[0]
    keys = mem_rows // blocks
    inner = seqs // SeqSum.ROWS
    seq_row, seq_column = place.seq // inner, lax.rem(place.seq, inner)

    def page_of(shard, block):
        return r.pages[shard, 0:1, block : block + 1]

    def page_near(ahead):
        to = {"seq": seq_row * inner + lax.rem(seq_column + ahead, inner)}
        return remote(r.page_out.at[ahead - 1], r.page_in.at[ahead - 1], r.pns.at[ahead - 1], r.pnr.at[ahead - 1], to)

    for ahead in range(1, inner):
        column = lax.rem(seq_column + ahead, inner)
        for block in range(blocks):
            page = r.ids[block * BLOCK]
            there = jnp.where(lax.rem(page, inner) == column, 1.0, 0.0)
            rows = r.mem_sum[block * keys : (block + 1) * keys, :]
            r.page_out[ahead - 1, block] = (rows * there).astype(BF16)
        page_near(ahead).start()
    seq_page = SeqSum(place, None, r, "page_")

    seq_cross = SeqSum(place, None, r, "cross_")
    seq_cross.low = r.cross_low
    for index in range(2):
        seq_cross.exchange(index).start()

    def out_copy(ahead, part):
        at = (ahead - 1, part)
        return remote(r.out_low.at[at], r.out_far.at[at], r.hs.at[at], r.hr.at[at], place.peer(ahead))

    for part in range(n):
        for ahead in range(1, chips):
            out_copy(ahead, part).start()
    fetches = [
        pltpu.make_async_copy(r.grad_in.at[pl.ds(place.x * piece, piece)], r.grad_own, r.fetch.at[0]),
        pltpu.make_async_copy(r.cross_low.at[2], seq_cross.mid, r.fetch.at[1]),
        pltpu.make_async_copy(r.cross_own, r.sum_w, r.fetch.at[2]),
        pltpu.make_async_copy(r.out_own, r.out_sum, r.fetch.at[3]),
    ]
    for fetch in fetches:
        fetch.start()

    def open_block(block):
        rows = block_rows(block)
        r.dout[rows, :] = dot_nt(r.g_in[rows, :], r.wo[...]).astype(BF16)
        dots_out(r.dout, r.mixed, block, r.dots)

    loop(blocks, open_block)
    n1 = r.n1.wait()
    grad_weight(r.g_out, 0, r.g_in, r.mixed)
    seq_out = SeqSum(place, mine(r.g_out), r, "out_")
    seq_out.start()
    r.causal[...] = causal_tile(True)
    r.dq[...] = jnp.zeros_like(r.dq)
    r.dk[...] = jnp.zeros_like(r.dk)
    r.dv[...] = jnp.zeros_like(r.dv)
    sums_prev = Sums(place, r, "prev_")
    weights = [getattr(r, "g_p" + str(pair)) for pair in range(pairs)]
    weight_sums = [getattr(r, "sum_p" + str(pair)) for pair in range(pairs)]
    seq_pairs = [SeqSum(place, mine(ref), r, "p" + str(pair) + "_") for pair, ref in enumerate(weights)]

    def low_keys(pair, first):
        lanes, rows = pl.ds(pair * PAIR, PAIR), pl.ds(first, tokens)
        r.gkv[0, rows, lanes] = r.dk[rows, lanes].astype(BF16)
        r.gkv[1, rows, lanes] = r.dv[rows, lanes].astype(BF16)

    def pair_weights(pair):
        lanes = pl.ds(pair * PAIR, PAIR)
        r.gq[:, lanes] = r.dq[:, lanes].astype(BF16)
        grad_weight(weights[pair], 0, n1.at[pl.ds(tokens, tokens)], r.gq.at[:, lanes])
        grad_weight(weights[pair], PAIR, n1, r.gkv.at[0, :, lanes], r.gkv.at[1, :, lanes])
        seq_pairs[pair].start()

    def kv_term(first):
        def term(row):
            rows = pl.ds(first + row, piece)
            return dot_nt(r.gkv[0, rows, :], r.wk[...]) + dot_nt(r.gkv[1, rows, :], r.wv[...])

        return term

    def page_rows(differs):
        page = seq_page.other_row(differs) * inner + seq_column
        rows = 0.0
        for block in range(blocks):
            same = (page_of(place.seq, block) == page).astype(F32)
            rows = rows + r.mem_sum[block * keys : (block + 1) * keys, :] * same
            for ahead in range(1, inner):
                shard = seq_row * inner + lax.rem(seq_column + inner - ahead, inner)
                same = (page_of(shard, block) == page).astype(F32)
                rows = rows + r.page_in[ahead - 1, block].astype(F32) * same
        return rows

    def early():
        for fetch in fetches:
            fetch.wait()
        seq_cross.middle(r.sum_w)

    def pair_done(pair):
        low_keys(pair, 0)
        low_keys(pair, tokens)
        pair_weights(pair)

    def pages_on():
        for ahead in range(1, inner):
            page_near(ahead).wait_recv()
        seq_page.combine(r.page_sum, rows_of=page_rows)
        seq_out.combine(r.sum_out)

    def prev_done():
        low_keys(pairs - 1, 0)
        sums_prev.own_pieces(kv_term(0))
        seq_page.middle(r.page_sum)

    def late_sums():
        for pair in range(pairs - 1):
            seq_pairs[pair].combine(weight_sums[pair])
        seq_out.middle(r.sum_out)

    tiles = 6
    last = tiles * (pairs - 1)

    def tile_back(index):
        pair, at = index // tiles, lax.rem(index, tiles)
        block = jnp.where(at < 3, at // 2, (at - 2) // 2)
        tile = jnp.where(at < 3, lax.rem(at, 2), REACH - lax.rem(at - 3, 2))
        rows, key_rows, lanes = block_rows(block), block_rows(block + tile), pair_lanes(pair)
        diagonal = jnp.where(tile == REACH, 1.0, 0.0)
        bias = jnp.where(tile == REACH, 0.0, reach_bias(r.offsets, block, tile))
        dq, dk, dv = attend_back(
            r.q,
            r.dout,
            r.lse,
            r.dots,
            block,
            pair,
            r.kext[key_rows, lanes],
            r.vext[key_rows, lanes],
            lambda: r.causal[...] * diagonal + bias,
        )
        r.dq[rows, lanes] = r.dq[rows, lanes] + dq
        r.dk[key_rows, lanes] = r.dk[key_rows, lanes] + dk
        r.dv[key_rows, lanes] = r.dv[key_rows, lanes] + dv
        pl.when(index == 3)(early)
        for done in range(pairs - 1):
            pl.when(index == tiles * done + tiles - 1)(functools.partial(pair_done, done))
        pl.when(index == last - 1)(pages_on)
        pl.when(index == last + 2)(prev_done)
        pl.when(index == last + 4)(late_sums)

    loop(tiles * pairs, tile_back)
    low_keys(pairs - 1, tokens)
    pair_weights(pairs - 1)

    def shift_copy(part):
        rows = pl.ds(part * CHUNK, CHUNK)
        sems = (r.ks.at[part], r.kr.at[part])
        return remote(r.shift_out.at[rows], r.shift_in.at[rows], *sems, {"seq": place.seq - 1})

    def shifts(act):
        for part in range(n):
            act(shift_copy(part))

    own_kv = kv_term(tokens)
    sums = Sums(place, r)
    sums.own_pieces(lambda row: dot_nt(r.gq[pl.ds(row, piece), :], r.wq[...]) + own_kv(row))
    for part in range(n):
        r.shift_out[pl.ds(part * CHUNK, CHUNK), :] = sums_prev.own_total(part).astype(BF16)
        pl.when(place.has_prev)(lambda: shift_copy(part).start())

    @pl.when(jnp.logical_not(place.has_next))
    def _():
        r.shift_in[...] = jnp.zeros_like(r.shift_in)

    half, prev = r.half.wait(), r.prev.wait()

    def norm_rows(slot, carry):
        ahead, part = slot // n, lax.rem(slot, n)
        mine_rows = pl.ds(pl.multiple_of(place.chip(ahead) * piece + part * CHUNK, CHUNK), CHUNK)
        gain_sum, shift_sum = carry
        for part_sums, ref in ((sums, half), (sums_prev, prev)):
            hat, _ = hat_of(ref[mine_rows, :].astype(F32))
            rows = part_sums.own[slot]
            gain_sum = gain_sum + jnp.sum(rows * hat, axis=0, keepdims=True)
            shift_sum = shift_sum + jnp.sum(rows, axis=0, keepdims=True)
        return gain_sum, shift_sum

    zero = jnp.zeros((1, r.gain.shape[1]), F32)
    norms = list(lax.fori_loop(0, place.chunks, norm_rows, (zero, zero)))
    norms += [ref[row : row + 1, :] * (1.0 / chips) for ref in (r.norm_cross, r.norm_ffn) for row in range(2)]
    columns = r.norm_out.shape[2]
    for shard in range(seqs):
        for row, values in enumerate(norms):
            r.norm_out[shard, row : row + 1, :] = values[:, shard * columns : (shard + 1) * columns]
        r.norm_out[shard, 6:8, :] = jnp.zeros((2, columns), F32)

    def norm_seq(ahead):
        shard = place.shard(ahead)
        sems = (r.nss.at[ahead - 1], r.nsr.at[ahead - 1])
        return remote(r.norm_out.at[shard], r.norm_seq.at[ahead - 1], *sems, {"seq": shard})

    for ahead in range(1, seqs):
        norm_seq(ahead).start()
    for pair in range(pairs - 1):
        seq_pairs[pair].middle(weight_sums[pair])
    seq_pairs[-1].combine(weight_sums[-1])
    norm_rows_in = r.norm_out[place.seq]
    for ahead in range(1, seqs):
        norm_seq(ahead).wait_recv()
        norm_rows_in = norm_rows_in + r.norm_seq[ahead - 1]
    r.norm_sum[...] = norm_rows_in

    def norm_tp(ahead):
        to = {"tp": lax.rem(place.tp + ahead, 2 * chips)}
        return remote(r.norm_sum, r.norm_tp.at[ahead - 1], r.nts.at[ahead - 1], r.ntr.at[ahead - 1], to)

    for ahead in range(1, 2 * chips):
        norm_tp(ahead).start()
    seq_pairs[-1].middle(weight_sums[-1])

    pl.when(place.has_next)(lambda: shifts(lambda copy: copy.wait_recv()))
    for part in range(n):
        rows = pl.ds(part * CHUNK, CHUNK)
        mine_rows = pl.ds(pl.multiple_of(place.x * piece + part * CHUNK, CHUNK), CHUNK)
        hat, inv_std = hat_of(half[mine_rows, :].astype(F32))
        rows_in = sums.own_total(part) + r.shift_in[rows, :].astype(F32)
        rows_in, _, _ = norm_back(rows_in, hat, inv_std, r.gain[...])
        r.grad[rows, :] = r.grad_own[rows, :] + rows_in
    for part in range(n):
        rows = pl.ds(part * CHUNK, CHUNK)
        out_rows = r.out_sum[rows, :]
        for ahead in range(1, chips):
            out_copy(ahead, part).wait_recv()
            out_rows = out_rows + r.out_far[ahead - 1, part].astype(F32)
        r.out[rows, :] = out_rows.astype(BF16)
    seq_cross.finish(r.sum_w)
    seq_page.finish(r.page_sum)
    r.grad_mem[...] = r.page_sum[: r.grad_mem.shape[0], :]
    seq_out.finish(r.sum_out)
    for seq_sum, ref in zip(seq_pairs, weight_sums):
        seq_sum.finish(ref)
    rows = r.norm_sum[...]
    for ahead in range(1, 2 * chips):
        norm_tp(ahead).wait_recv()
        rows = rows + r.norm_tp[ahead - 1]
    r.norms[...] = rows

    for ahead in range(1, 2 * chips):
        norm_tp(ahead).wait_send()
    for seq_sum in (seq_out, *seq_pairs):
        seq_sum.end()
    seq_cross.end(near=False)
    for part in range(n):
        for ahead in range(1, chips):
            out_copy(ahead, part).wait_send()
    seq_page.end(near=False)
    for ahead in range(1, seqs):
        norm_seq(ahead).wait_send()
    for ahead in range(1, inner):
        page_near(ahead).wait_send()
    sums_prev.own_end()
    sums.own_end()
    pl.when(place.has_prev)(lambda: shifts(lambda copy: copy.wait_send()))


def closing(chips, seqs, ids, offsets, a, f, e, mem_true, w):
    tokens, width = a.q.shape
    dim = w.attn_output.shape[1]
    blocks = tokens // BLOCK
    own = tokens // (2 * chips)
    pairs = width // PAIR
    pair_scratch = {}
    for pair in range(pairs):
        pair_scratch.update(SeqSum.scratch(seqs, (dim // seqs, 3 * PAIR), BF16, "p" + str(pair) + "_"))
    mem_rows, wide = e.mem_sum.shape
    rows, inner = SeqSum.ROWS, seqs // SeqSum.ROWS
    keys = mem_rows // blocks
    dma = pltpu.SemaphoreType.DMA
    vmem = lambda array: (array, "vmem")
    late = lambda array: (array, "late")
    hbm = lambda array: (array, "hbm")
    return call(
        functools.partial(close_body, chips, seqs),
        "closing",
        dict(
            ids=(ids, "smem"),
            offsets=(offsets, "smem"),
            cross_low=hbm(e.cross_low),
            cross_own=hbm(e.cross_own),
            out_low=hbm(e.out_low),
            out_own=hbm(e.out_own),
            mem_sum=vmem(e.mem_sum),
            g_in=vmem(e.g),
            wo=vmem(w.attn_output),
            q=vmem(a.q),
            kext=vmem(a.kext),
            vext=vmem(a.vext),
            mixed=vmem(f.mixed1),
            lse=vmem(f.lse1),
            wq=vmem(w.attn_query),
            wk=vmem(w.attn_key),
            wv=vmem(w.attn_value),
            gain=vmem(w.self_gain),
            norm_cross=vmem(e.norm),
            norm_ffn=vmem(f.norm),
            pages=vmem(a.pages),
            n1=late(a.n1),
            half=late(a.half),
            prev=late(a.prev),
            grad_in=hbm(e.grad),
        ),
        dict(
            grad=((own, dim), F32, "vmem"),
            out=((own, dim), BF16, "vmem"),
            norms=((8, dim // seqs), F32, "vmem"),
            sum_w=((dim // seqs, 4 * width), F32, "vmem"),
            **{"sum_p" + str(pair): ((dim // seqs, 3 * PAIR), F32, "vmem") for pair in range(pairs)},
            sum_out=((dim // seqs, width), F32, "vmem"),
            grad_mem=((mem_true, wide), F32, "vmem"),
        ),
        dict(
            **sum_scratch(chips, tokens, dim, "prev_"),
            **sum_scratch(chips, tokens, dim),
            **SeqSum.scratch(seqs, (dim // seqs, 4 * width), BF16, "cross_", near=False, low=False),
            out_sum=pltpu.VMEM((own, dim), F32),
            out_far=pltpu.VMEM((chips - 1, own // CHUNK, CHUNK, dim), BF16),
            hs=dma((chips - 1, own // CHUNK)),
            hr=dma((chips - 1, own // CHUNK)),
            **pair_scratch,
            **SeqSum.scratch(seqs, (dim // seqs, width), BF16, "out_"),
            **SeqSum.scratch(seqs, (keys, wide), BF16, "page_", near=False),
            norm_seq=pltpu.VMEM((seqs - 1, 8, dim // seqs), F32),
            nss=dma((seqs - 1,)),
            nsr=dma((seqs - 1,)),
            page_out=pltpu.VMEM((inner - 1, blocks, keys, wide), BF16),
            page_in=pltpu.VMEM((inner - 1, blocks, keys, wide), BF16),
            page_sum=pltpu.VMEM((keys, wide), F32),
            pns=dma((inner - 1,)),
            pnr=dma((inner - 1,)),
            causal=pltpu.VMEM((BLOCK, BLOCK), F32),
            dout=pltpu.VMEM((tokens, width), BF16),
            dots=pltpu.VMEM((width // PAIR, 8, tokens), F32),
            dq=pltpu.VMEM((tokens, width), F32),
            dk=pltpu.VMEM((2 * tokens, width), F32),
            dv=pltpu.VMEM((2 * tokens, width), F32),
            gq=pltpu.VMEM((tokens, width), BF16),
            gkv=pltpu.VMEM((2, 2 * tokens, width), BF16),
            **{"g_p" + str(pair): pltpu.VMEM((dim, 3 * PAIR), BF16) for pair in range(pairs)},
            g_out=pltpu.VMEM((dim, width), BF16),
            grad_own=pltpu.VMEM((own, dim), F32),
            fetch=dma((4,)),
            shift_out=pltpu.VMEM((own, dim), BF16),
            shift_in=pltpu.VMEM((own, dim), BF16),
            ks=dma((own // CHUNK,)),
            kr=dma((own // CHUNK,)),
            norm_out=pltpu.VMEM((seqs, 8, dim // seqs), F32),
            norm_sum=pltpu.VMEM((8, dim // seqs), F32),
            norm_tp=pltpu.VMEM((2 * chips - 1, 8, dim // seqs), F32),
            nts=dma((2 * chips - 1,)),
            ntr=dma((2 * chips - 1,)),
        ),
        3,
        20 * tokens * 3 * BLOCK * width,
    )


def layout_body(width, per_tp, *refs):
    pairs = width // PAIR
    count = pairs + 8
    sources, results, places, sems = refs[:count], refs[count : -1 - count], refs[-1 - count : -1], refs[-1]
    copies = [pltpu.make_async_copy(src, dst, sems.at[i]) for i, (src, dst) in enumerate(zip(sources, places))]
    for copy in copies:
        copy.start()
    for copy in copies:
        copy.wait()
    sum_out, sum_w, sum_up, sum_down, grad, out, grad_mem, norms = places[pairs:]
    (out_out, grad_out, mem_out, q_out, k_out, v_out, o_out, cq_out, ck_out, cv_out, co_out, up_out, down_out) = results[:-6]
    out_out[...] = out[...]
    grad_out[...] = grad[...]
    mem_out[0] = grad_mem[...]
    for pair, sums in enumerate(places[:pairs]):
        for piece, ref in enumerate((q_out, k_out, v_out)):
            ref[:, pair * PAIR : (pair + 1) * PAIR] = sums[:, piece * PAIR : (piece + 1) * PAIR]
    o_out[...] = jnp.transpose(sum_out[...])
    for piece, ref in enumerate((cq_out, ck_out, cv_out)):
        ref[...] = sum_w[:, piece * width : (piece + 1) * width]
    co_out[...] = jnp.transpose(sum_w[:, 3 * width :])
    up_out[...] = sum_up[...]
    down_out[...] = jnp.transpose(sum_down[...])
    columns = norms.shape[1]
    first = lax.axis_index("tp") * per_tp
    from_column = lax.broadcasted_iota(jnp.int32, (columns, per_tp), 0)
    to_column = lax.broadcasted_iota(jnp.int32, (columns, per_tp), 1)
    pick = (from_column == to_column + first).astype(F32)
    mine = jnp.dot(norms[...], pick, precision=lax.Precision.HIGHEST, preferred_element_type=F32)
    for row, ref in enumerate(results[-6:]):
        ref[...] = mine[row : row + 1, :]


def layout(tps, width, c, e):
    share_rows, hidden = e.sum_up.shape
    own, dim = c.grad.shape
    per_tp = share_rows // tps
    weights = [(share_rows, width)] * 3 + [(width, share_rows)]
    dims = [(own, dim), (own, dim), (1, *c.grad_mem.shape), *weights, *weights, (share_rows, hidden), (hidden, share_rows)]
    types = [BF16] + [F32] * (len(dims) - 1)
    dims += [(1, per_tp)] * 6
    types += [F32] * 6
    sources = [getattr(c, "sum_p" + str(pair)) for pair in range(width // PAIR)]
    sources += [c.sum_out, c.sum_w, e.sum_up, e.sum_down, c.grad, c.out, c.grad_mem, c.norms]
    return pl.pallas_call(
        functools.partial(layout_body, width, per_tp),
        name="layout",
        out_shape=[jax.ShapeDtypeStruct(d, t) for d, t in zip(dims, types)],
        in_specs=[pl.BlockSpec(memory_space=pltpu.HBM)] * len(sources),
        out_specs=[VMEM] * len(dims),
        scratch_shapes=[pltpu.VMEM(source.shape, source.dtype) for source in sources]
        + [pltpu.SemaphoreType.DMA((len(sources),))],
        compiler_params=pltpu.CompilerParams(vmem_limit_bytes=62 << 20),
    )(*sources)


def on_device(
    hidden_in,
    memory,
    page_ids,
    token_offsets,
    memory_mask,
    attn_query,
    attn_key,
    attn_value,
    attn_output,
    cross_query,
    cross_key,
    cross_value,
    cross_output,
    ffn_up,
    ffn_down,
    self_gain,
    self_shift,
    cross_gain,
    cross_shift,
    ffn_gain,
    ffn_shift,
    out_grad,
):
    tps, seqs = lax.axis_size("tp"), lax.axis_size("seq")
    chips = tps // 2
    width = attn_query.shape[1]
    w = Refs()
    w.attn_query, w.attn_key, w.attn_value, w.attn_output = attn_query, attn_key, attn_value, attn_output
    w.cross_query, w.cross_key, w.cross_value, w.cross_output = cross_query, cross_key, cross_value, cross_output
    w.up, w.down = ffn_up, ffn_down
    w.self_gain, w.self_shift = self_gain.reshape(1, -1), self_shift.reshape(1, -1)
    w.cross_gain, w.cross_shift = cross_gain.reshape(1, -1), cross_shift.reshape(1, -1)
    w.ffn_gain, w.ffn_shift = ffn_gain.reshape(1, -1), ffn_shift.reshape(1, -1)

    a = opening(
        chips,
        seqs,
        page_ids,
        hidden_in,
        out_grad,
        memory,
        memory_mask,
        w.self_gain,
        w.self_shift,
        attn_query,
        attn_key,
        attn_value,
    )
    f = forward(chips, seqs, page_ids, token_offsets, a, w)
    e = cross_back(chips, seqs, a, f, w)
    c = closing(chips, seqs, page_ids, token_offsets, a, f, e, memory.shape[1], w)
    results = layout(tps, width, c, e)
    return (
        results[0],
        results[1],
        results[2],
        *results[3:11],
        results[11],
        results[12],
        *[values.reshape(-1) for values in results[13:]],
    )


def solution(mesh):
    both = ("seq", "tp")
    in_specs = (
        P(both, None),
        P("seq", None, None),
        P("seq"),
        P("seq"),
        P("seq", None),
        P(None, "tp"),
        P(None, "tp"),
        P(None, "tp"),
        P("tp", None),
        P(None, "tp"),
        P(None, "tp"),
        P(None, "tp"),
        P("tp", None),
        P(None, "tp"),
        P("tp", None),
        P(),
        P(),
        P(),
        P(),
        P(),
        P(),
        P(both, None),
    )
    out_specs = (
        P(both, None),
        P(both, None),
        P("seq", None, "tp"),
        P("seq", "tp"),
        P("seq", "tp"),
        P("seq", "tp"),
        P("tp", "seq"),
        P("seq", "tp"),
        P("seq", "tp"),
        P("seq", "tp"),
        P("tp", "seq"),
        P("seq", "tp"),
        P("tp", "seq"),
        P(both),
        P(both),
        P(both),
        P(both),
        P(both),
        P(both),
    )
    return jax.shard_map(on_device, mesh=mesh, in_specs=in_specs, out_specs=out_specs, check_vma=False)
```

```python
import functools

import jax
import jax.numpy as jnp
from jax import lax
from jax.experimental import pallas as pl
from jax.experimental.pallas import tpu as pltpu
from jax.sharding import PartitionSpec as P

HEAD_DIM = 64
PAIR = 2 * HEAD_DIM
BLOCK = 512
REACH = 2
CHUNK = 128
EPS = 1e-05
NEG = -1e30
F32 = jnp.float32
BF16 = jnp.bfloat16
MESH = pl.DeviceIdType.MESH
VMEM = pl.BlockSpec(memory_space=pltpu.VMEM)
SMEM = pl.BlockSpec(memory_space=pltpu.SMEM)


def dot(left, right):
    return jnp.dot(left, right, preferred_element_type=F32)


def dot_nt(left, right):
    return lax.dot_general(left, right, (((1,), (1,)), ((), ())), preferred_element_type=F32)


def dot_tn(left, right):
    return lax.dot_general(left, right, (((0,), (0,)), ((), ())), preferred_element_type=F32)


def hat_of(rows):
    center = rows - jnp.mean(rows, axis=-1, keepdims=True)
    inv_std = lax.rsqrt(jnp.mean(center * center, axis=-1, keepdims=True) + EPS)
    return center * inv_std, inv_std


def norm_back(grad_rows, hat, inv_std, gain):
    grad_hat = grad_rows * gain
    inner = jnp.mean(grad_hat * hat, axis=-1, keepdims=True)
    grad_input = inv_std * (grad_hat - jnp.mean(grad_hat, axis=-1, keepdims=True) - hat * inner)
    gain_sum = jnp.sum(grad_rows * hat, axis=0, keepdims=True)
    shift_sum = jnp.sum(grad_rows, axis=0, keepdims=True)
    return grad_input, gain_sum, shift_sum


def remote(src, dst, send_sem, recv_sem, device):
    return pltpu.make_async_remote_copy(
        src_ref=src, dst_ref=dst, send_sem=send_sem, recv_sem=recv_sem, device_id=device, device_id_type=MESH
    )


class Late:
    def __init__(self, hbm, ref, sem, out):
        self.hbm, self.ref, self.sem, self.out, self.started, self.waited = hbm, ref, sem, out, False, False

    def copy(self):
        ends = (self.ref, self.hbm) if self.out else (self.hbm, self.ref)
        return pltpu.make_async_copy(*ends, self.sem)

    def start(self):
        self.copy().start()
        self.started = True

    def wait(self):
        if self.started and not self.waited:
            self.copy().wait()
            self.waited = True
        return self.ref


class Refs:
    pass


def call(body, name, ins, outs, scratch, collective_id, flops):
    dma = pltpu.SemaphoreType.DMA
    specs = {"vmem": VMEM, "smem": SMEM, "hbm": pl.BlockSpec(memory_space=pltpu.HBM)}
    specs["late"] = specs["hbm"]
    late_in = [key for key, (_, mode) in ins.items() if mode == "late"]
    late_out = [key for key, (_, _, mode) in outs.items() if mode == "late"]
    places = [pltpu.VMEM(ins[key][0].shape, ins[key][0].dtype) for key in late_in]
    places += [pltpu.VMEM(outs[key][0], outs[key][1]) for key in late_out]
    lates = len(places)

    def kernel(*refs):
        r = Refs()
        count = len(ins) + len(outs)
        for key, ref in zip([*ins, *outs], refs[:count]):
            setattr(r, key, ref)
        for key, ref in zip(scratch, refs[count : count + len(scratch)]):
            setattr(r, key, ref)
        rest = refs[count + len(scratch) :]
        all_late = []
        for index, key in enumerate(late_in + late_out):
            late = Late(getattr(r, key), rest[index], rest[-1].at[index], index >= len(late_in))
            setattr(r, key, late)
            all_late.append(late)
            if not late.out:
                late.start()
        body(r)
        for late in all_late:
            late.wait()

    result = pl.pallas_call(
        kernel,
        name=name,
        out_shape=[jax.ShapeDtypeStruct(dims, dtype) for dims, dtype, _ in outs.values()],
        in_specs=[specs[mode] for _, mode in ins.values()],
        out_specs=[specs[mode] for _, _, mode in outs.values()],
        scratch_shapes=[*scratch.values(), *places] + ([dma((lates,))] if lates else []),
        cost_estimate=pl.CostEstimate(flops=flops, bytes_accessed=16 << 20, transcendentals=0),
        compiler_params=pltpu.CompilerParams(
            collective_id=collective_id, has_side_effects=True, vmem_limit_bytes=62 << 20
        ),
    )(*[array for array, _ in ins.values()])
    out = Refs()
    for key, value in zip(outs, result):
        setattr(out, key, value)
    return out


def loop(count, step):
    lax.fori_loop(0, count, lambda index, carry: (step(index), carry)[1], 0)


class Place:
    def __init__(self, chips, seqs, rows):
        self.chips, self.seqs = chips, seqs
        self.piece = rows // (2 * chips)
        self.per_piece = self.piece // CHUNK
        self.chunks = chips * self.per_piece
        self.tp = lax.axis_index("tp")
        self.seq = lax.axis_index("seq")
        self.x = self.tp // 2
        self.core = lax.rem(self.tp, 2)
        self.mate = {"tp": self.x * 2 + 1 - self.core}
        self.has_prev, self.has_next = self.seq > 0, self.seq < seqs - 1

    def chip(self, ahead):
        return lax.rem(self.x + ahead, self.chips)

    def peer(self, ahead):
        return {"tp": self.chip(ahead) * 2 + self.core}

    def shard(self, ahead):
        return lax.rem(self.seq + ahead, self.seqs)

    def piece_row(self, chip, core):
        return pl.multiple_of((chip * 2 + core) * self.piece, CHUNK)

    def row(self, slot, core):
        chip, part = slot // self.per_piece, lax.rem(slot, self.per_piece)
        return pl.multiple_of((chip * 2 + core) * self.piece + part * CHUNK, CHUNK)

    def enter(self, seq="", all_tp=False):
        barrier = pltpu.get_barrier_semaphore()

        def greet(device):
            pl.semaphore_signal(barrier, inc=1, device_id=device, device_id_type=MESH)

        count = self.chips
        if all_tp:
            count = 2 * self.chips - 1
            for ahead in range(1, 2 * self.chips):
                greet({"tp": lax.rem(self.tp + ahead, 2 * self.chips)})
        else:
            greet(self.mate)
            for ahead in range(1, self.chips):
                greet(self.peer(ahead))
        if seq == "all":
            for ahead in range(1, self.seqs):
                greet({"seq": self.shard(ahead)})
            count = count + self.seqs - 1
        if seq == "row":
            inner = self.seqs // SeqSum.ROWS
            for ahead in range(1, inner):
                greet({"seq": self.seq // inner * inner + lax.rem(self.seq + ahead, inner)})
            count = count + inner - 1
        pl.semaphore_wait(barrier, count)


def sum_scratch(chips, rows, width, name="sums_", stages=1):
    chunks = rows // 2 // CHUNK
    dma = pltpu.SemaphoreType.DMA
    specs = [
        pltpu.VMEM((chunks, CHUNK, width), BF16),
        pltpu.VMEM((chunks, CHUNK, width), BF16),
        pltpu.VMEM((chunks, CHUNK, width), F32),
        dma((chunks,)),
        dma((chunks,)),
        pltpu.VMEM((stages, chips - 1, chunks, CHUNK, width), BF16),
        dma((stages, chips - 1, chunks)),
        dma((stages, chips - 1, chunks)),
    ]
    return {name + str(index): spec for index, spec in enumerate(specs)}


class Sums:
    def __init__(self, place, r, name="sums_", stage=0):
        self.place, self.stage = place, stage
        (self.out, self.mate, self.own, self.s1, self.r1, self.far, self.s2, self.r2) = [
            getattr(r, name + str(index)) for index in range(8)
        ]
        self.low = self.mate

    def core_copy(self, slot):
        return remote(self.out.at[slot], self.mate.at[slot], self.s1.at[slot], self.r1.at[slot], self.place.mate)

    def far_copy(self, ahead, slot):
        at = (self.stage, ahead - 1, slot)
        return remote(self.low.at[slot], self.far.at[at], self.s2.at[at], self.r2.at[at], self.place.peer(ahead))

    def near(self, slot, who, rows):
        n = self.place.per_piece

        @pl.when(who == 0)
        def _():
            for part in range(n):
                self.out[slot + part] = rows[part * CHUNK : (part + 1) * CHUNK].astype(BF16)
                self.core_copy(slot + part).start()

        @pl.when(who == 1)
        def _():
            for part in range(n):
                self.core_copy(slot + part).wait_recv()
                self.own[slot + part] = rows[part * CHUNK : (part + 1) * CHUNK] + self.mate[slot + part].astype(F32)

    def all_pieces(self, first, count, term):
        place = self.place
        n = place.per_piece

        def step(index):
            chip, who = first + index // 2, lax.rem(index, 2)
            core = jnp.where(who == 0, 1 - place.core, place.core)
            self.near(chip * n, who, term(place.piece_row(chip, core)))

            @pl.when(who == 1)
            def _():
                for part in range(n):
                    self.low[chip * n + part] = self.own[chip * n + part].astype(BF16)
                    for ahead in range(1, place.chips):
                        self.far_copy(ahead, chip * n + part).start()

        loop(2 * count, step)

    def take(self, slot):
        rows = self.own[slot]
        for ahead in range(1, self.place.chips):
            self.far_copy(ahead, slot).wait_recv()
            rows = rows + self.far[self.stage, ahead - 1, slot].astype(F32)
        self.core_copy(slot).wait_send()
        for ahead in range(1, self.place.chips):
            self.far_copy(ahead, slot).wait_send()
        return rows

    def own_pieces(self, term, go=True):
        place = self.place
        n = place.per_piece

        def step(index):
            ahead, who = lax.rem(index // 2 + 1, place.chips), lax.rem(index, 2)
            core = jnp.where(who == 0, 1 - place.core, place.core)
            self.near(ahead * n, who, term(place.piece_row(place.chip(ahead), core)))

            @pl.when(jnp.logical_and(who == 1, ahead > 0))
            def _():
                for part in range(n):
                    self.low[ahead * n + part] = self.own[ahead * n + part].astype(BF16)
                    if go:
                        self.far_copy(ahead, ahead * n + part).start()

        loop(2 * place.chips, step)

    def own_total(self, part):
        n = self.place.per_piece
        rows = self.own[part]
        for ahead in range(1, self.place.chips):
            slot = ahead * n + part
            self.far_copy(ahead, slot).wait_recv()
            rows = rows + self.far[self.stage, ahead - 1, slot].astype(F32)
        return rows

    def own_end(self, far=True):
        n = self.place.per_piece
        for slot in range(self.place.chunks):
            self.core_copy(slot).wait_send()
            if far and slot >= n:
                self.far_copy(slot // n, slot).wait_send()


class Share:
    def __init__(self, place, ref, send_sems, recv_sems, stage=0):
        self.place, self.ref, self.s, self.r, self.stage = place, ref, send_sems, recv_sems, stage

    def copy(self, slot):
        rows = pl.ds(self.place.row(slot, self.place.core), CHUNK)
        at = (self.stage, slot)
        return remote(self.ref.at[rows], self.ref.at[rows], self.s.at[at], self.r.at[at], self.place.mate)

    def put(self, slot, rows):
        self.ref[pl.ds(self.place.row(slot, self.place.core), CHUNK), :] = rows
        self.copy(slot).start()

    def end(self, first, count):
        loop(count, lambda index: self.copy(first + index).wait())


class Gather:
    def __init__(self, place, own, ref, parts, sems):
        self.place, self.own, self.ref, self.parts = place, own, ref, parts
        self.size = own.shape[0] // parts
        self.s1, self.r1, self.s2, self.r2, self.local = sems

    @staticmethod
    def scratch(chips, parts, name):
        dma = pltpu.SemaphoreType.DMA
        specs = [dma((chips, parts)), dma((chips, parts)), dma((chips - 1, parts)), dma((chips - 1, parts)), dma((1,))]
        return {name + str(index): spec for index, spec in enumerate(specs)}

    def far(self, ahead, part):
        rows = pl.ds(part * self.size, self.size)
        sems = (self.s2.at[ahead - 1, part], self.r2.at[ahead - 1, part])
        return remote(self.own.at[rows], self.ref.at[self.place.tp, rows], *sems, self.place.peer(ahead))

    def near(self, ahead, part):
        place = self.place
        rows = pl.ds(part * self.size, self.size)
        device = lax.rem(place.x + place.chips - ahead, place.chips) * 2 + place.core
        src = self.ref.at[device, rows] if ahead else self.own.at[rows]
        sems = (self.s1.at[ahead, part], self.r1.at[ahead, part])
        return remote(src, self.ref.at[device, rows], *sems, place.mate)

    def keep(self):
        return pltpu.make_async_copy(self.own, self.ref.at[self.place.tp], self.local.at[0])

    def start(self):
        self.keep().start()
        for part in range(self.parts):
            for ahead in range(1, self.place.chips):
                self.far(ahead, part).start()
            self.near(0, part).start()

    def relay(self):
        for ahead in range(1, self.place.chips):
            for part in range(self.parts):
                self.far(ahead, part).wait_recv()
                self.near(ahead, part).start()

    def end(self):
        self.keep().wait()
        for part in range(self.parts):
            for ahead in range(self.place.chips):
                self.near(ahead, part).wait_recv()

    def drain(self):
        for part in range(self.parts):
            for ahead in range(1, self.place.chips):
                self.far(ahead, part).wait_send()
            for ahead in range(self.place.chips):
                self.near(ahead, part).wait_send()


class SeqSum:
    ROWS = 4

    def __init__(self, place, slot, r, name):
        self.place, self.slot = place, slot
        self.near_recv, self.ns, self.nr, self.low, self.mid, self.first, self.second, self.fs, self.fr = [
            getattr(r, name + str(index), None) for index in range(9)
        ]
        self.inner = place.seqs // self.ROWS
        self.row, self.column = place.seq // self.inner, lax.rem(place.seq, self.inner)

    @staticmethod
    def scratch(seqs, dims, dtype, name, near=True, low=True, far=True):
        dma = pltpu.SemaphoreType.DMA
        rows, inner = SeqSum.ROWS, seqs // SeqSum.ROWS
        specs = [
            pltpu.VMEM((inner - 1, rows, *dims), dtype) if near else None,
            dma((inner - 1, rows)) if near else None,
            dma((inner - 1, rows)) if near else None,
            pltpu.VMEM((rows, *dims), dtype) if low else None,
            pltpu.VMEM(dims, dtype) if far else None,
            pltpu.VMEM((2, *dims), dtype) if far else None,
            pltpu.VMEM((1, *dims), dtype) if far else None,
            dma((3,)) if far else None,
            dma((3,)) if far else None,
        ]
        return {name + str(index): spec for index, spec in enumerate(specs) if spec is not None}

    def other_row(self, differs):
        bit, half = lax.rem(self.row, 2), self.row // 2
        return (self.row, self.row + 1 - 2 * bit, self.row + 2 - 4 * half, 3 - self.row)[differs]

    def shard(self, differs, column_ahead=0):
        return self.other_row(differs) * self.inner + lax.rem(self.column + column_ahead, self.inner)

    def near(self, ahead, differs):
        at = (ahead - 1, differs)
        to = {"seq": self.shard(0, ahead)}
        return remote(self.slot(self.shard(differs, ahead)), self.near_recv.at[at], self.ns.at[at], self.nr.at[at], to)

    def each_near(self, act):
        for ahead in range(1, self.inner):
            for differs in (1, 3, 2, 0):
                act(self.near(ahead, differs))

    def start(self):
        self.each_near(lambda copy: copy.start())

    def exchange(self, index):
        sems = (self.fs.at[index], self.fr.at[index])
        if index == 2:
            return remote(self.mid, self.second.at[0], *sems, {"seq": self.shard(2)})
        return remote(self.low.at[(1, 3)[index]], self.first.at[index], *sems, {"seq": self.shard(1)})

    def fetch(self, sems):
        return [
            pltpu.make_async_copy(self.slot(self.shard(differs)), self.low.at[differs], sems.at[differs])
            for differs in range(self.ROWS)
        ]

    def column_rows(self, differs, fetched):
        rows = (self.low.at[differs] if fetched else self.slot(self.shard(differs)))[...].astype(F32)
        for ahead in range(1, self.inner):
            self.near(ahead, differs).wait_recv()
            rows = rows + self.near_recv[ahead - 1, differs].astype(F32)
        return rows

    def combine(self, out, fetched=False, rows_of=None, go=True):
        rows_of = rows_of or (lambda differs: self.column_rows(differs, fetched))
        for differs in (1, 3):
            self.low[differs] = rows_of(differs).astype(self.low.dtype)
            if go:
                self.exchange(differs // 2).start()
        if go:
            self.mid[...] = rows_of(2).astype(self.mid.dtype)
        else:
            self.low[2] = rows_of(2).astype(self.low.dtype)
        out[...] = rows_of(0)

    def middle(self, out):
        self.exchange(1).wait_recv()
        self.mid[...] = (self.mid[...].astype(F32) + self.first[1].astype(F32)).astype(self.mid.dtype)
        self.exchange(2).start()
        self.exchange(0).wait_recv()
        out[...] = out[...] + self.first[0].astype(F32)

    def finish(self, out):
        self.exchange(2).wait_recv()
        out[...] = out[...] + self.second[0].astype(F32)

    def end(self, near=True, far=True):
        if near:
            self.each_near(lambda copy: copy.wait_send())
        if far:
            for index in range(3):
                self.exchange(index).wait_send()


def head_masks():
    lane = lax.broadcasted_iota(jnp.int32, (1, PAIR), 1)
    first = (lane < HEAD_DIM).astype(F32)
    return first, 1.0 - first


def pair_lanes(pair):
    return pl.ds(pl.multiple_of(pair * PAIR, PAIR), PAIR)


def block_rows(block):
    return pl.ds(pl.multiple_of(block * BLOCK, BLOCK), BLOCK)


def causal_tile(keys_first):
    rows = lax.broadcasted_iota(jnp.int32, (BLOCK, BLOCK), 0)
    columns = lax.broadcasted_iota(jnp.int32, (BLOCK, BLOCK), 1)
    allowed = rows <= columns if keys_first else columns <= rows
    return jnp.where(allowed, 0.0, NEG)


def attend(q_ref, block, keys, values, biases, mixed_ref, lse_ref):
    masks = head_masks()
    rows = block_rows(block)
    lane = lax.broadcasted_iota(jnp.int32, (BLOCK, 128), 1)

    def step(pair):
        lanes = pair_lanes(pair)
        queries = q_ref[rows, lanes]
        pair_out = jnp.zeros((BLOCK, PAIR), F32)
        lse_block = jnp.zeros((BLOCK, 128), F32)
        for head in range(2):
            head_queries = queries * masks[head].astype(BF16)
            scores = [dot_nt(head_queries, keys(tile, lanes)) + bias() for tile, bias in enumerate(biases)]
            top = functools.reduce(jnp.maximum, [jnp.max(s, axis=-1, keepdims=True) for s in scores])
            total, out = 0.0, 0.0
            for tile, s in enumerate(scores):
                weights = jnp.exp(s - top)
                total = total + jnp.sum(weights, axis=-1, keepdims=True)
                out = out + dot(weights.astype(BF16), values(tile, lanes))
            pair_out = pair_out + out * masks[head] / total
            lse_block = jnp.where(lane == head, top + jnp.log(total), lse_block)
        mixed_ref[rows, lanes] = pair_out.astype(BF16)
        lse_ref[pair, :, rows] = jnp.transpose(lse_block)[:8]

    loop(q_ref.shape[1] // PAIR, step)


def dots_out(grad_ref, mixed_ref, block, dots_ref):
    masks = head_masks()
    rows = block_rows(block)
    lane = lax.broadcasted_iota(jnp.int32, (BLOCK, 128), 1)

    def step(pair):
        lanes = pair_lanes(pair)
        product = grad_ref[rows, lanes].astype(F32) * mixed_ref[rows, lanes].astype(F32)
        values = jnp.zeros((BLOCK, 128), F32)
        for head in range(2):
            value = jnp.sum(product * masks[head], axis=-1, keepdims=True)
            values = jnp.where(lane == head, value, values)
        dots_ref[pair, :, rows] = jnp.transpose(values)[:8]

    loop(grad_ref.shape[1] // PAIR, step)


def attend_back(q_ref, grad_ref, lse_ref, dots_ref, block, pair, keys, values, bias):
    masks = head_masks()
    lanes, rows = pair_lanes(pair), block_rows(block)
    queries, grads = q_ref[rows, lanes], grad_ref[rows, lanes]
    dq = dk = dv = 0.0
    for head in range(2):
        mask = masks[head].astype(BF16)
        head_queries, head_grads, head_keys = queries * mask, grads * mask, keys * mask
        scores = dot_nt(keys, head_queries) + bias()
        weights = jnp.exp(scores - lse_ref[pair, head : head + 1, rows])
        grad_weights = dot_nt(values, head_grads)
        grad_scores = (weights * (grad_weights - dots_ref[pair, head : head + 1, rows])).astype(BF16)
        dv = dv + dot(weights.astype(BF16), head_grads)
        dk = dk + dot(grad_scores, head_queries)
        dq = dq + dot_tn(grad_scores, head_keys)
    return dq * HEAD_DIM ** (-0.5), dk, dv


def grad_weight(out_ref, first, left_ref, *rights):
    count = left_ref.shape[1]
    step_size = min(256, count)
    width = sum(right.shape[1] for right in rights)

    def step(index):
        columns = pl.ds(pl.multiple_of(index * step_size, step_size), step_size)
        right = rights[0][...] if len(rights) == 1 else jnp.concatenate([right[...] for right in rights], axis=1)
        out_ref[columns, first : first + width] = dot_tn(left_ref[:, columns], right).astype(BF16)

    loop(count // step_size, step)


def scaled(queries):
    return (queries.astype(BF16).astype(F32) * HEAD_DIM ** (-0.5)).astype(BF16)


def half_rows(slot):
    return pl.ds(pl.multiple_of(slot * CHUNK, CHUNK), CHUNK)


def reach_bias(offsets, block, tile):
    return jnp.where(offsets[block * BLOCK] >= (REACH - tile) * BLOCK, 0.0, NEG)


def norm_step(place, r, sums, share, base, res):
    def finish(slot, carry):
        hat, inv_std = hat_of(res[half_rows(slot), :])
        grad_in, gain_sum, shift_sum = norm_back(sums.take(slot), hat, inv_std, r.gain[...])
        rows = base(slot) + grad_in
        r.grad.ref[half_rows(slot), :] = rows
        share.put(slot, rows.astype(BF16))
        return carry[0] + gain_sum, carry[1] + shift_sum

    zero = jnp.zeros((1, r.gain.shape[1]), F32)
    gain_sum, shift_sum = lax.fori_loop(0, place.chunks, finish, (zero, zero))
    r.norm[0:1, :] = gain_sum
    r.norm[1:2, :] = shift_sum


def open_body(chips, seqs, r):
    n1, half = r.n1.ref, (r.half.ref, r.prev.ref)
    tokens = n1.shape[0] // 2
    place = Place(chips, seqs, tokens)
    place.enter(seq="all")
    n, piece = place.per_piece, place.piece
    own_rows = pl.ds(pl.multiple_of(place.x * piece, CHUNK), piece)

    def half_part(chip, part):
        return pl.ds(pl.multiple_of(chip * piece + part * CHUNK, CHUNK), CHUNK)

    def far(which, ahead, part):
        dst = half[which].at[half_part(place.x, part)]
        src = dst if which else r.x.at[pl.ds(part * CHUNK, CHUNK)]
        at = (which, ahead - 1, part)
        return remote(src, dst, r.s2.at[at], r.r2.at[at], place.peer(ahead))

    def pass_on(part):
        src, dst = r.x.at[pl.ds(part * CHUNK, CHUNK)], half[1].at[half_part(place.x, part)]
        return remote(src, dst, r.ss.at[part], r.sr.at[part], {"seq": place.seq + 1})

    def parts(act):
        for part in range(n):
            act(part)

    pl.when(place.has_next)(lambda: parts(lambda part: pass_on(part).start()))
    for part in range(n):
        for ahead in range(1, chips):
            far(0, ahead, part).start()
    grads = Gather(place, r.og_own, r.og, n, [getattr(r, "og_" + str(i)) for i in range(5)])
    grads.start()

    columns = pl.ds(pl.multiple_of(place.tp * r.mem.shape[3], 128), r.mem.shape[3])
    rows_apart = SeqSum.ROWS
    inner = seqs // rows_apart
    seq_row, seq_column = place.seq // inner, lax.rem(place.seq, inner)

    def mem_far(ahead):
        to = {"seq": lax.rem(seq_row + ahead, rows_apart) * inner + seq_column}
        sems = (r.fs.at[ahead - 1], r.fr.at[ahead - 1])
        return remote(r.memory.at[0, :, columns], r.mem.at[place.seq, 0], *sems, to)

    def mem_near(behind, ahead):
        row = lax.rem(seq_row + rows_apart - behind, rows_apart)
        to = {"seq": seq_row * inner + lax.rem(seq_column + ahead, inner)}
        dst = r.mem.at[row * inner + seq_column, 0]
        src = dst if behind else r.memory.at[0, :, columns]
        sems = (r.ns.at[behind, ahead - 1], r.nr.at[behind, ahead - 1])
        return remote(src, dst, *sems, to)

    def mem_pass(behind):
        mem_far(behind).wait_recv()
        for ahead in range(1, inner):
            mem_near(behind, ahead).start()

    def known_copies(ahead):
        to = {"seq": place.shard(ahead)}
        at = [(which, ahead - 1) for which in range(2)]
        return (
            remote(r.mask, r.masks.at[place.seq], r.ms.at[at[0]], r.mr.at[at[0]], to),
            remote(r.page_row, r.pages.at[place.seq], r.ms.at[at[1]], r.mr.at[at[1]], to),
        )

    def known_all(act):
        def step(index):
            for copy in known_copies(index + 1):
                act(copy)

        loop(seqs - 1, step)

    lane = lax.broadcasted_iota(jnp.int32, r.page_row.shape, 1)
    page_row = jnp.zeros(r.page_row.shape, jnp.int32)
    for block in range(tokens // BLOCK):
        page_row = jnp.where(lane == block, r.ids[block * BLOCK], page_row)
    r.page_row[...] = page_row
    own_copies = [
        pltpu.make_async_copy(r.memory.at[0, :, columns], r.mem.at[place.seq, 0], r.local.at[0]),
        pltpu.make_async_copy(r.mask, r.masks.at[place.seq], r.local.at[1]),
        pltpu.make_async_copy(r.page_row, r.pages.at[place.seq], r.local.at[2]),
    ]
    for copy in own_copies:
        copy.start()
    for ahead in (1, 3, 2):
        mem_far(ahead).start()
    for ahead in range(1, inner):
        mem_near(0, ahead).start()
    known_all(lambda copy: copy.start())
    half[0][own_rows, :] = r.x[...]

    def from_chip(ahead):
        return lax.rem(place.x + chips - ahead, chips)

    def near(which, ahead, part):
        row = pl.multiple_of((from_chip(ahead) * 2 + place.core) * piece + part * CHUNK, CHUNK)
        rows = n1.at[pl.ds((1 - which) * tokens + row, CHUNK)]
        at = (which, ahead, part)
        return remote(rows, rows, r.s1.at[at], r.r1.at[at], place.mate)

    def normed(which, ahead, part):
        chip = from_chip(ahead)
        hat, _ = hat_of(half[which][half_part(chip, part), :].astype(F32))
        row = pl.multiple_of((chip * 2 + place.core) * piece + part * CHUNK, CHUNK)
        n1[pl.ds((1 - which) * tokens + row, CHUNK), :] = (hat * r.gain[...] + r.shift[...]).astype(BF16)
        near(which, ahead, part).start()

    def project(which, ahead):
        for part in range(n):
            near(which, ahead, part).wait_recv()
        chip = from_chip(ahead)
        row = pl.multiple_of(chip * 2 * piece, CHUNK)
        rows = pl.ds((1 - which) * tokens + row, 2 * piece)
        rows_in = n1[rows, :]
        r.kext[rows, :] = dot(rows_in, r.wk[...]).astype(BF16)
        r.vext[rows, :] = dot(rows_in, r.wv[...]).astype(BF16)
        if not which:
            r.q[pl.ds(row, 2 * piece), :] = scaled(dot(rows_in, r.wq[...]))

    def step(which, ahead):
        def norm_part(part):
            if ahead:
                far(which, ahead, part).wait_recv()
            normed(which, ahead, part)

        loop(n, norm_part)
        project(which, ahead)

    step(0, 0)
    mem_pass(1)
    for ahead in range(1, chips):
        step(0, ahead)
    r.half.start()
    mem_pass(3)

    @pl.when(jnp.logical_not(place.has_prev))
    def _():
        half[1][own_rows, :] = jnp.zeros((piece, n1.shape[1]), BF16)

    pl.when(place.has_prev)(lambda: parts(lambda part: pass_on(part).wait_recv()))
    for part in range(n):
        for ahead in range(1, chips):
            far(1, ahead, part).start()
    grads.relay()
    step(1, 0)
    mem_pass(2)
    for ahead in range(1, chips):
        step(1, ahead)
    r.prev.start()
    r.n1.start()
    for part in range(n):
        for which in range(2):
            for ahead in range(1, chips):
                far(which, ahead, part).wait_send()
            for ahead in range(chips):
                near(which, ahead, part).wait_send()
    pl.when(place.has_next)(lambda: parts(lambda part: pass_on(part).wait_send()))
    grads.end()
    grads.drain()
    for copy in own_copies:
        copy.wait()
    for behind in range(1, rows_apart):
        mem_far(behind).wait_send()
    for behind in range(rows_apart):
        for ahead in range(1, inner):
            mem_near(behind, ahead).wait()
    known_all(lambda copy: copy.wait())


def opening(chips, seqs, ids, x, og, memory, mask, gain, shift, wq, wk, wv):
    width, dim = wq.shape[1], x.shape[1]
    tokens = ids.shape[0]
    n = tokens // (2 * chips) // CHUNK
    rows, inner = SeqSum.ROWS, seqs // SeqSum.ROWS
    dma = pltpu.SemaphoreType.DMA
    vmem = lambda array: (array, "vmem")
    return call(
        functools.partial(open_body, chips, seqs),
        "opening",
        dict(
            ids=(ids, "smem"),
            x=vmem(x),
            og_own=(og, "hbm"),
            memory=(memory, "hbm"),
            mask=vmem(mask),
            gain=vmem(gain),
            shift=vmem(shift),
            wq=vmem(wq),
            wk=vmem(wk),
            wv=vmem(wv),
        ),
        dict(
            n1=((2 * tokens, dim), BF16, "late"),
            half=((tokens // 2, dim), BF16, "late"),
            prev=((tokens // 2, dim), BF16, "late"),
            q=((tokens, width), BF16, "vmem"),
            kext=((2 * tokens, width), BF16, "vmem"),
            vext=((2 * tokens, width), BF16, "vmem"),
            mem=((seqs, 1, memory.shape[1], dim // (2 * chips)), BF16, "hbm"),
            masks=((seqs, 1, mask.shape[1]), jnp.int32, "vmem"),
            pages=((seqs, 8, 128), jnp.int32, "vmem"),
            og=((2 * chips, tokens // (2 * chips), dim), BF16, "hbm"),
        ),
        dict(
            s1=dma((2, chips, n)),
            r1=dma((2, chips, n)),
            s2=dma((2, chips - 1, n)),
            r2=dma((2, chips - 1, n)),
            ss=dma((n,)),
            sr=dma((n,)),
            ms=dma((2, seqs - 1)),
            mr=dma((2, seqs - 1)),
            fs=dma((rows - 1,)),
            fr=dma((rows - 1,)),
            ns=dma((rows, inner - 1)),
            nr=dma((rows, inner - 1)),
            local=dma((3,)),
            page_row=pltpu.VMEM((8, 128), jnp.int32),
            **Gather.scratch(chips, n, "og_"),
        ),
        0,
        10 * tokens * dim * width,
    )


def forward_body(chips, seqs, r):
    tokens = r.q.shape[0]
    place = Place(chips, seqs, tokens)
    place.enter(seq="row")
    piece, blocks = place.piece, tokens // BLOCK
    per_block, chips_per_block = place.chunks // blocks, chips // blocks
    mem_true = r.mem8.shape[2]
    keys = r.mem_k.shape[0] // blocks
    stages = [Sums(place, r, stage=stage) for stage in range(3)]
    mem = r.mem.ref

    r.mem_own[...] = jnp.zeros_like(r.mem_own)
    r.bias[...] = jnp.full(r.bias.shape, NEG, F32)
    for block in range(blocks):
        rows = pl.ds(block * keys, mem_true)

        def choose(page):
            r.mem_own[rows, :] = jnp.where(r.ids[block * BLOCK] == page, r.mem8[page, 0], r.mem_own[rows, :])

        def mask_of(page, mask):
            return jnp.where(r.ids[block * BLOCK] == page, r.masks[page], mask)

        loop(seqs, choose)
        mask = lax.fori_loop(0, seqs, mask_of, jnp.zeros((1, mem_true), jnp.int32))
        r.bias[block, :, :mem_true] = jnp.broadcast_to(jnp.where(mask > 0, 0.0, NEG), (8, mem_true))
    memory = Gather(place, r.mem_own, mem, 4, [getattr(r, "mem_" + str(i)) for i in range(5)])
    memory.start()
    r.causal[...] = causal_tile(False)

    def self_block(block):
        biases = [functools.partial(reach_bias, r.offsets, block, tile) for tile in range(REACH)]
        attend(
            r.q,
            block,
            lambda tile, lanes: r.kext[block_rows(block + tile), lanes],
            lambda tile, lanes: r.vext[block_rows(block + tile), lanes],
            biases + [lambda: r.causal[...]],
            r.mixed1,
            r.lse1,
        )
        stages[0].all_pieces(
            block * chips_per_block, chips_per_block, lambda row: dot(r.mixed1[pl.ds(row, piece), :], r.wo[...])
        )

    loop(blocks, self_block)

    memory.relay()
    memory.end()
    wide = mem.shape[2]
    for weight, out in ((r.wck, r.mem_k), (r.wcv, r.mem_v)):
        rows = 0.0
        for device in range(2 * chips):
            rows = rows + dot(mem[device], weight[device * wide : (device + 1) * wide, :])
        out[...] = rows.astype(BF16)
    r.mem.start()

    half = r.half.wait()
    n2, res1, res2 = r.n2.ref, r.res1.ref, r.res2.ref
    share = Share(place, n2, r.ss, r.sr, 0)

    def finish_self(slot):
        rows = half[half_rows(slot), :].astype(F32) + stages[0].take(slot)
        res1[half_rows(slot), :] = rows
        hat, _ = hat_of(rows)
        share.put(slot, (hat * r.cross_gain[...] + r.cross_shift[...]).astype(BF16))

    cross_query, cross_output = r.wq.wait(), r.wco.wait()

    def cross_block(block):
        loop(per_block, lambda index: finish_self(block * per_block + index))
        share.end(block * per_block, per_block)
        rows = block_rows(block)
        page = pl.ds(pl.multiple_of(block * keys, 128), keys)
        r.q2[rows, :] = scaled(dot(n2[rows, :], cross_query[...]))
        attend(
            r.q2,
            block,
            lambda tile, lanes: r.mem_k[page, lanes],
            lambda tile, lanes: r.mem_v[page, lanes],
            [lambda: r.bias[block, 0:1, :]],
            r.mixed2,
            r.lse2,
        )
        stages[1].all_pieces(
            block * chips_per_block,
            chips_per_block,
            lambda row: dot(r.mixed2[pl.ds(row, piece), :], cross_output[...]),
        )

    loop(blocks, cross_block)
    r.n2.start()
    r.res1.start()

    share_ffn = Share(place, r.n3, r.ss, r.sr, 1)
    up, down, og = r.up.wait(), r.down.wait(), r.og.wait()
    act = r.act.ref

    def finish_cross(slot):
        rows = res1[half_rows(slot), :] + stages[1].take(slot)
        res2[half_rows(slot), :] = rows
        hat, _ = hat_of(rows)
        share_ffn.put(slot, (hat * r.gain[...] + r.shift[...]).astype(BF16))

    def term(row):
        rows = pl.ds(row, piece)
        pre = dot(r.n3[rows, :], up[...])
        half_erf = 0.5 * lax.erf(pre * (0.5**0.5)) + 0.5
        act[rows, :] = (pre * half_erf).astype(BF16)
        slope = half_erf + pre * jnp.exp(-0.5 * pre * pre) * (0.15915494309189535**0.5)
        grad_act = dot_nt(og[rows, :], down[...])
        low = (grad_act * slope).astype(BF16)
        r.gpre[rows, :] = low
        return dot_nt(low, up[...])

    def ffn_block(block):
        loop(per_block, lambda index: finish_cross(block * per_block + index))
        share_ffn.end(block * per_block, per_block)
        stages[2].all_pieces(block * chips_per_block, chips_per_block, term)

    loop(blocks, ffn_block)
    r.res2.start()
    r.act.start()
    grad_weight(r.g_down, 0, og, act)
    share_rows = r.down_own.shape[0]
    seq_down = SeqSum(
        place, lambda shard: r.g_down.at[pl.ds(pl.multiple_of(shard * share_rows, 8), share_rows)], r, "down_"
    )
    seq_down.low = r.down_low
    seq_down.start()
    grad_weight(r.g_up.ref, 0, r.n3, r.gpre)
    r.g_up.start()

    share_grad = Share(place, r.g.ref, r.ss, r.sr, 2)
    norm_step(
        place,
        r,
        stages[2],
        share_grad,
        lambda slot: og[pl.ds(place.row(slot, place.core), CHUNK), :].astype(F32),
        res2,
    )
    r.grad.start()
    share_grad.end(0, place.chunks)
    r.g.start()
    seq_down.combine(r.down_own, go=False)
    seq_down.end(far=False)
    memory.drain()


def forward(chips, seqs, ids, offsets, a, w):
    tokens, width = a.q.shape
    dim, hidden = w.up.shape
    chunks = tokens // 2 // CHUNK
    blocks = tokens // BLOCK
    mem_true, wide = a.mem.shape[2:]
    keys = -(-mem_true // 128) * 128
    dma = pltpu.SemaphoreType.DMA
    vmem = lambda array: (array, "vmem")
    late = lambda array: (array, "late")
    return call(
        functools.partial(forward_body, chips, seqs),
        "forward",
        dict(
            ids=(ids, "smem"),
            offsets=(offsets, "smem"),
            q=vmem(a.q),
            kext=vmem(a.kext),
            vext=vmem(a.vext),
            mem8=vmem(a.mem),
            masks=vmem(a.masks),
            wo=vmem(w.attn_output),
            wck=vmem(w.cross_key),
            wcv=vmem(w.cross_value),
            cross_gain=vmem(w.cross_gain),
            cross_shift=vmem(w.cross_shift),
            gain=vmem(w.ffn_gain),
            shift=vmem(w.ffn_shift),
            half=late(a.half),
            wq=late(w.cross_query),
            wco=late(w.cross_output),
            up=late(w.up),
            og=late(a.og.reshape(tokens, dim)),
            down=late(w.down),
        ),
        dict(
            mixed1=((tokens, width), BF16, "vmem"),
            lse1=((width // PAIR, 8, tokens), F32, "vmem"),
            res1=((tokens // 2, dim), F32, "late"),
            n2=((tokens, dim), BF16, "late"),
            mem=((2 * chips, blocks * keys, wide), BF16, "late"),
            mem_k=((blocks * keys, width), BF16, "vmem"),
            mem_v=((blocks * keys, width), BF16, "vmem"),
            bias=((blocks, 8, keys), F32, "vmem"),
            q2=((tokens, width), BF16, "vmem"),
            mixed2=((tokens, width), BF16, "vmem"),
            lse2=((width // PAIR, 8, tokens), F32, "vmem"),
            res2=((tokens // 2, dim), F32, "late"),
            act=((tokens, hidden), BF16, "late"),
            grad=((tokens // 2, dim), F32, "late"),
            g=((tokens, dim), BF16, "late"),
            norm=((2, dim), F32, "vmem"),
            g_up=((dim, hidden), BF16, "late"),
            down_low=((SeqSum.ROWS, dim // seqs, hidden), BF16, "vmem"),
            down_own=((dim // seqs, hidden), F32, "vmem"),
        ),
        dict(
            **sum_scratch(chips, tokens, dim, stages=3),
            **Gather.scratch(chips, 4, "mem_"),
            mem_own=pltpu.VMEM((blocks * keys, wide), BF16),
            causal=pltpu.VMEM((BLOCK, BLOCK), F32),
            **SeqSum.scratch(seqs, (dim // seqs, hidden), BF16, "down_", low=False, far=False),
            g_down=pltpu.VMEM((dim, hidden), BF16),
            n3=pltpu.VMEM((tokens, dim), BF16),
            gpre=pltpu.VMEM((tokens, hidden), BF16),
            ss=dma((3, chunks)),
            sr=dma((3, chunks)),
        ),
        1,
        14 * tokens * dim * hidden,
    )


def cross_back_body(chips, seqs, r):
    tokens = r.g_in.shape[0]
    place = Place(chips, seqs, tokens)
    place.enter(seq="all")
    piece, n, blocks = place.piece, place.per_piece, tokens // BLOCK
    share_rows = r.sum_down.shape[0]
    keys = r.mem_k.shape[0] // blocks
    mine = lambda ref: (lambda shard: ref.at[pl.ds(pl.multiple_of(shard * share_rows, 8), share_rows)])
    seq_down = SeqSum(place, None, r, "down_")
    seq_down.low = r.down_low
    fetch_down = [
        pltpu.make_async_copy(r.down_low.at[2], seq_down.mid, r.fetch.at[0, 0]),
        pltpu.make_async_copy(r.down_own, r.sum_down, r.fetch.at[0, 1]),
    ]
    seq_up = SeqSum(place, mine(r.g_up), r, "up_")
    fetch_up = seq_up.fetch(r.fetch.at[1])
    base = pltpu.make_async_copy(r.res_out.at[pl.ds(place.x * piece, piece)], r.base, r.fetch.at[2, 0])
    base.start()
    for index in range(2):
        seq_down.exchange(index).start()
    seq_up.start()
    for copy in fetch_down + fetch_up:
        copy.start()
    sums = Sums(place, r)

    def step(block):
        rows = block_rows(block)
        page = pl.ds(pl.multiple_of(block * keys, 128), keys)
        r.dout[rows, :] = dot_nt(r.g_in[rows, :], r.wo[...]).astype(BF16)
        dots_out(r.dout, r.mixed, block, r.dots)
        bias = jnp.transpose(r.bias[block])[:, 0:1]

        def pair_step(pair):
            lanes = pair_lanes(pair)
            dq, dk, dv = attend_back(
                r.q,
                r.dout,
                r.lse,
                r.dots,
                block,
                pair,
                r.mem_k[page, lanes],
                r.mem_v[page, lanes],
                lambda: bias,
            )
            r.gq[rows, lanes] = dq.astype(BF16)
            r.gk[page, lanes] = dk.astype(BF16)
            r.gv[page, lanes] = dv.astype(BF16)

        loop(r.q.shape[1] // PAIR, pair_step)
        sums.all_pieces(
            block * (chips // blocks),
            chips // blocks,
            lambda row: dot_nt(r.gq[pl.ds(row, piece), :], r.wq[...]),
        )

    loop(blocks, step)

    width = r.q.shape[1]
    wide = r.mem_sum.shape[1]

    def mem_part(chip, core):
        rows = pl.ds(pl.multiple_of((chip * 2 + core) * wide, wide), wide)
        return dot_nt(r.gk[...], r.wck[rows, :]) + dot_nt(r.gv[...], r.wcv[rows, :])

    def mem_near(ahead):
        return remote(r.mem_out.at[ahead], r.mem_mate.at[ahead], r.mns.at[ahead], r.mnr.at[ahead], place.mate)

    def mem_far(ahead):
        sems = (r.mfs.at[ahead - 1], r.mfr.at[ahead - 1])
        return remote(r.mem_mate.at[ahead], r.mem_far.at[ahead - 1], *sems, place.peer(ahead))

    for ahead in range(chips):
        r.mem_out[ahead] = mem_part(place.chip(ahead), 1 - place.core).astype(BF16)
        mem_near(ahead).start()
    for ahead in range(1, chips):
        rows = mem_part(place.chip(ahead), place.core)
        mem_near(ahead).wait_recv()
        r.mem_mate[ahead] = (rows + r.mem_mate[ahead].astype(F32)).astype(BF16)
        mem_far(ahead).start()
    rows = mem_part(place.x, place.core)
    mem_near(0).wait_recv()
    r.mem_sum[...] = rows + r.mem_mate[0].astype(F32)
    for copy in fetch_down:
        copy.wait()
    seq_down.middle(r.sum_down)

    hidden = Sums(place, r, "hidden_")
    act, down = r.act.wait(), r.down.wait()
    hidden.own_pieces(lambda row: dot(act[pl.ds(row, piece), :], down[...]), go=False)
    base.wait()
    for part in range(n):
        rows = pl.ds(part * CHUNK, CHUNK)
        r.out_own[rows, :] = r.base[rows, :] + hidden.own[part]
        for ahead in range(1, chips):
            r.out_low[ahead - 1, part] = hidden.low[ahead * n + part]

    n2, mem = r.n2.wait(), r.mem.wait()
    g_w = r.g_w

    def mem_step(device):
        rows = pl.ds(pl.multiple_of(device * wide, wide), wide)
        both = jnp.concatenate([r.gk[...], r.gv[...]], axis=1)
        g_w[rows, width : 3 * width] = dot_tn(mem[device], both).astype(BF16)

    loop(2 * chips, mem_step)
    grad_weight(g_w, 0, n2, r.gq)
    grad_weight(g_w, 3 * width, r.g_in, r.mixed)
    seq_cross = SeqSum(place, mine(g_w), r, "cross_")
    seq_cross.low = r.cross_low
    seq_cross.start()

    for copy in fetch_up:
        copy.wait()
    seq_up.combine(r.sum_up, fetched=True)
    share = Share(place, r.g.ref, r.s1, r.r1)
    res, grad_in = r.res.wait(), r.grad_in.wait()
    norm_step(place, r, sums, share, lambda slot: grad_in[half_rows(slot), :], res)
    r.grad.start()
    share.end(0, place.chunks)
    r.g.start()
    seq_up.middle(r.sum_up)
    for ahead in range(1, chips):
        mem_far(ahead).wait_recv()
        r.mem_sum[...] = r.mem_sum[...] + r.mem_far[ahead - 1].astype(F32)
    seq_down.finish(r.sum_down)
    seq_up.finish(r.sum_up)
    seq_cross.combine(r.cross_own, go=False)
    seq_down.end(near=False)
    seq_up.end()
    seq_cross.end(far=False)
    hidden.own_end(far=False)
    for ahead in range(chips):
        mem_near(ahead).wait_send()
    for ahead in range(1, chips):
        mem_far(ahead).wait_send()


def cross_back(chips, seqs, a, f, w):
    tokens, dim = f.g.shape
    width = f.q2.shape[1]
    hidden = f.act.shape[1]
    chunks = tokens // 2 // CHUNK
    mem_rows = f.mem_k.shape[0]
    rows = SeqSum.ROWS
    dma = pltpu.SemaphoreType.DMA
    vmem = lambda array: (array, "vmem")
    late = lambda array: (array, "late")
    hbm = lambda array: (array, "hbm")
    return call(
        functools.partial(cross_back_body, chips, seqs),
        "cross_back",
        dict(
            g_in=vmem(f.g),
            wo=vmem(w.cross_output),
            q=vmem(f.q2),
            mem_k=vmem(f.mem_k),
            mem_v=vmem(f.mem_v),
            bias=vmem(f.bias),
            mixed=vmem(f.mixed2),
            lse=vmem(f.lse2),
            wq=vmem(w.cross_query),
            gain=vmem(w.cross_gain),
            wck=vmem(w.cross_key),
            wcv=vmem(w.cross_value),
            act=late(f.act),
            down=late(w.down),
            mem=late(f.mem),
            n2=late(f.n2),
            res=late(f.res1),
            grad_in=late(f.grad),
            res_out=hbm(f.res2),
            g_up=hbm(f.g_up),
            down_low=hbm(f.down_low),
            down_own=hbm(f.down_own),
        ),
        dict(
            grad=((tokens // 2, dim), F32, "late"),
            g=((tokens, dim), BF16, "late"),
            norm=((2, dim), F32, "vmem"),
            cross_low=((rows, dim // seqs, 4 * width), BF16, "vmem"),
            cross_own=((dim // seqs, 4 * width), F32, "vmem"),
            mem_sum=((mem_rows, f.mem.shape[2]), F32, "vmem"),
            sum_up=((dim // seqs, hidden), F32, "vmem"),
            sum_down=((dim // seqs, hidden), F32, "vmem"),
            out_own=((tokens // (2 * chips), dim), F32, "vmem"),
            out_low=((chips - 1, tokens // (2 * chips) // CHUNK, CHUNK, dim), BF16, "vmem"),
        ),
        dict(
            **sum_scratch(chips, tokens, dim),
            **sum_scratch(chips, tokens, dim, "hidden_"),
            **SeqSum.scratch(seqs, (dim // seqs, 4 * width), BF16, "cross_", low=False, far=False),
            g_w=pltpu.VMEM((dim, 4 * width), BF16),
            **SeqSum.scratch(seqs, (dim // seqs, hidden), BF16, "up_"),
            **SeqSum.scratch(seqs, (dim // seqs, hidden), BF16, "down_", near=False, low=False),
            mem_out=pltpu.VMEM((chips, mem_rows, f.mem.shape[2]), BF16),
            mem_mate=pltpu.VMEM((chips, mem_rows, f.mem.shape[2]), BF16),
            mem_far=pltpu.VMEM((chips - 1, mem_rows, f.mem.shape[2]), BF16),
            mns=dma((chips,)),
            mnr=dma((chips,)),
            mfs=dma((chips - 1,)),
            mfr=dma((chips - 1,)),
            gq=pltpu.VMEM((tokens, width), BF16),
            gk=pltpu.VMEM((mem_rows, width), BF16),
            gv=pltpu.VMEM((mem_rows, width), BF16),
            dout=pltpu.VMEM((tokens, width), BF16),
            dots=pltpu.VMEM((width // PAIR, 8, tokens), F32),
            base=pltpu.VMEM((tokens // (2 * chips), dim), F32),
            s1=dma((1, chunks)),
            r1=dma((1, chunks)),
            fetch=dma((3, rows)),
        ),
        2,
        12 * tokens * dim * width,
    )


def close_body(chips, seqs, r):
    tokens, width = r.q.shape
    place = Place(chips, seqs, tokens)
    place.enter(seq="all", all_tp=True)
    piece, n, blocks = place.piece, place.per_piece, tokens // BLOCK
    pairs = width // PAIR
    share_rows = r.sum_w.shape[0]
    mine = lambda ref: (lambda shard: ref.at[pl.ds(pl.multiple_of(shard * share_rows, 8), share_rows)])

    mem_rows = r.mem_sum.shape[0]
    keys = mem_rows // blocks
    sent = r.page_sum.shape[0]
    inner = seqs // SeqSum.ROWS
    seq_row, seq_column = place.seq // inner, lax.rem(place.seq, inner)

    def page_of(shard, block):
        return r.pages[shard, 0:1, block : block + 1]

    def page_near(ahead):
        to = {"seq": seq_row * inner + lax.rem(seq_column + ahead, inner)}
        return remote(r.page_out.at[ahead - 1], r.page_in.at[ahead - 1], r.pns.at[ahead - 1], r.pnr.at[ahead - 1], to)

    for ahead in range(1, inner):
        column = lax.rem(seq_column + ahead, inner)
        for block in range(blocks):
            page = r.ids[block * BLOCK]
            there = jnp.where(lax.rem(page, inner) == column, 1.0, 0.0)
            rows = r.mem_sum[block * keys : block * keys + sent, :]
            r.page_out[ahead - 1, block] = (rows * there).astype(BF16)
        page_near(ahead).start()
    seq_page = SeqSum(place, None, r, "page_")

    seq_cross = SeqSum(place, None, r, "cross_")
    seq_cross.low = r.cross_low
    for index in range(2):
        seq_cross.exchange(index).start()

    def out_copy(ahead, part):
        at = (ahead - 1, part)
        return remote(r.out_low.at[at], r.out_far.at[at], r.hs.at[at], r.hr.at[at], place.peer(ahead))

    for part in range(n):
        for ahead in range(1, chips):
            out_copy(ahead, part).start()
    fetches = [
        pltpu.make_async_copy(r.grad_in.at[pl.ds(place.x * piece, piece)], r.grad_own, r.fetch.at[0]),
        pltpu.make_async_copy(r.cross_low.at[2], seq_cross.mid, r.fetch.at[1]),
        pltpu.make_async_copy(r.cross_own, r.sum_w, r.fetch.at[2]),
        pltpu.make_async_copy(r.out_own, r.out_sum, r.fetch.at[3]),
    ]
    for fetch in fetches:
        fetch.start()

    def open_block(block):
        rows = block_rows(block)
        r.dout[rows, :] = dot_nt(r.g_in[rows, :], r.wo[...]).astype(BF16)
        dots_out(r.dout, r.mixed, block, r.dots)

    loop(blocks, open_block)
    r.causal[...] = causal_tile(True)
    r.dq[...] = jnp.zeros_like(r.dq)
    r.dk[...] = jnp.zeros_like(r.dk)
    r.dv[...] = jnp.zeros_like(r.dv)

    def tile_back(block, tile):
        rows, key_rows = block_rows(block), block_rows(block + tile)
        diagonal = jnp.where(tile == REACH, 1.0, 0.0)
        bias = jnp.where(tile == REACH, 0.0, reach_bias(r.offsets, block, tile))

        def step(pair):
            lanes = pair_lanes(pair)
            dq, dk, dv = attend_back(
                r.q,
                r.dout,
                r.lse,
                r.dots,
                block,
                pair,
                r.kext[key_rows, lanes],
                r.vext[key_rows, lanes],
                lambda: r.causal[...] * diagonal + bias,
            )
            r.dq[rows, lanes] = r.dq[rows, lanes] + dq
            r.dk[key_rows, lanes] = r.dk[key_rows, lanes] + dk
            r.dv[key_rows, lanes] = r.dv[key_rows, lanes] + dv

        loop(pairs, step)

    def kv_term(first):
        def term(row):
            rows = pl.ds(first + row, piece)
            return dot_nt(r.gkv[0, rows, :], r.wk[...]) + dot_nt(r.gkv[1, rows, :], r.wv[...])

        return term

    sums_prev = Sums(place, r, "prev_")

    def page_rows(differs):
        page = seq_page.other_row(differs) * inner + seq_column
        rows = 0.0
        for block in range(blocks):
            same = (page_of(place.seq, block) == page).astype(F32)
            rows = rows + r.mem_sum[block * keys : block * keys + sent, :] * same
            for ahead in range(1, inner):
                shard = seq_row * inner + lax.rem(seq_column + inner - ahead, inner)
                same = (page_of(shard, block) == page).astype(F32)
                rows = rows + r.page_in[ahead - 1, block].astype(F32) * same
        return rows

    def between():
        r.gkv[0, :tokens, :] = r.dk[:tokens, :].astype(BF16)
        r.gkv[1, :tokens, :] = r.dv[:tokens, :].astype(BF16)
        sums_prev.own_pieces(kv_term(0))
        for ahead in range(1, inner):
            page_near(ahead).wait_recv()
        seq_page.combine(r.page_sum, rows_of=page_rows)
        for fetch in fetches:
            fetch.wait()
        seq_cross.middle(r.sum_w)

    def tile_step(index):
        first = index < 3
        block = jnp.where(first, index // 2, (index - 2) // 2)
        tile_back(block, jnp.where(first, lax.rem(index, 2), REACH - lax.rem(index + 1, 2)))
        pl.when(index == 2)(between)

    loop(6, tile_step)
    r.gkv[0, tokens:, :] = r.dk[tokens:, :].astype(BF16)
    r.gkv[1, tokens:, :] = r.dv[tokens:, :].astype(BF16)

    n1 = r.n1.wait()
    grad_weight(r.g_kv, 0, n1, r.gkv.at[0], r.gkv.at[1])
    seq_kv = SeqSum(place, mine(r.g_kv), r, "kv_")
    seq_kv.start()

    def shift_copy(part):
        rows = pl.ds(part * CHUNK, CHUNK)
        sems = (r.ks.at[part], r.kr.at[part])
        return remote(r.shift_out.at[rows], r.shift_in.at[rows], *sems, {"seq": place.seq - 1})

    def shifts(act):
        for part in range(n):
            act(shift_copy(part))

    for part in range(n):
        r.shift_out[pl.ds(part * CHUNK, CHUNK), :] = sums_prev.own_total(part).astype(BF16)
        pl.when(place.has_prev)(lambda: shift_copy(part).start())

    @pl.when(jnp.logical_not(place.has_next))
    def _():
        r.shift_in[...] = jnp.zeros_like(r.shift_in)

    r.gq[...] = r.dq[...].astype(BF16)
    grad_weight(r.g_q, 0, n1.at[pl.ds(tokens, tokens)], r.gq)
    seq_q = SeqSum(place, mine(r.g_q), r, "q_")
    seq_q.start()
    own_kv = kv_term(tokens)
    sums = Sums(place, r)
    sums.own_pieces(lambda row: dot_nt(r.gq[pl.ds(row, piece), :], r.wq[...]) + own_kv(row))
    grad_weight(r.g_out, 0, r.g_in, r.mixed)
    seq_out = SeqSum(place, mine(r.g_out), r, "out_")
    seq_out.start()
    seq_page.middle(r.page_sum)

    half, prev = r.half.wait(), r.prev.wait()

    def norm_rows(slot, carry):
        ahead, part = slot // n, lax.rem(slot, n)
        mine_rows = pl.ds(pl.multiple_of(place.chip(ahead) * piece + part * CHUNK, CHUNK), CHUNK)
        gain_sum, shift_sum = carry
        for part_sums, ref in ((sums, half), (sums_prev, prev)):
            hat, _ = hat_of(ref[mine_rows, :].astype(F32))
            rows = part_sums.own[slot]
            gain_sum = gain_sum + jnp.sum(rows * hat, axis=0, keepdims=True)
            shift_sum = shift_sum + jnp.sum(rows, axis=0, keepdims=True)
        return gain_sum, shift_sum

    zero = jnp.zeros((1, r.gain.shape[1]), F32)
    norms = list(lax.fori_loop(0, place.chunks, norm_rows, (zero, zero)))
    norms += [ref[row : row + 1, :] * (1.0 / chips) for ref in (r.norm_cross, r.norm_ffn) for row in range(2)]
    columns = r.norm_out.shape[2]
    for shard in range(seqs):
        for row, values in enumerate(norms):
            r.norm_out[shard, row : row + 1, :] = values[:, shard * columns : (shard + 1) * columns]
        r.norm_out[shard, 6:8, :] = jnp.zeros((2, columns), F32)

    def norm_seq(ahead):
        shard = place.shard(ahead)
        sems = (r.nss.at[ahead - 1], r.nsr.at[ahead - 1])
        return remote(r.norm_out.at[shard], r.norm_seq.at[ahead - 1], *sems, {"seq": shard})

    for ahead in range(1, seqs):
        norm_seq(ahead).start()
    seq_kv.combine(r.sum_kv)
    seq_q.combine(r.sum_q)
    norm_rows_in = r.norm_out[place.seq]
    for ahead in range(1, seqs):
        norm_seq(ahead).wait_recv()
        norm_rows_in = norm_rows_in + r.norm_seq[ahead - 1]
    r.norm_sum[...] = norm_rows_in

    def norm_tp(ahead):
        to = {"tp": lax.rem(place.tp + ahead, 2 * chips)}
        return remote(r.norm_sum, r.norm_tp.at[ahead - 1], r.nts.at[ahead - 1], r.ntr.at[ahead - 1], to)

    for ahead in range(1, 2 * chips):
        norm_tp(ahead).start()
    seq_out.combine(r.sum_out)
    seq_kv.middle(r.sum_kv)
    seq_q.middle(r.sum_q)
    seq_out.middle(r.sum_out)

    pl.when(place.has_next)(lambda: shifts(lambda copy: copy.wait_recv()))

    def grad_part(part):
        rows = half_rows(part)
        mine_rows = pl.ds(pl.multiple_of(place.x * piece + part * CHUNK, CHUNK), CHUNK)
        hat, inv_std = hat_of(half[mine_rows, :].astype(F32))
        rows_in = sums.own_total(part) + r.shift_in[rows, :].astype(F32)
        rows_in, _, _ = norm_back(rows_in, hat, inv_std, r.gain[...])
        r.grad[rows, :] = r.grad_own[rows, :] + rows_in

    loop(n, grad_part)
    for part in range(n):
        rows = pl.ds(part * CHUNK, CHUNK)
        out_rows = r.out_sum[rows, :]
        for ahead in range(1, chips):
            out_copy(ahead, part).wait_recv()
            out_rows = out_rows + r.out_far[ahead - 1, part].astype(F32)
        r.out[rows, :] = out_rows.astype(BF16)
    seq_cross.finish(r.sum_w)
    seq_page.finish(r.page_sum)
    r.grad_mem[...] = r.page_sum[: r.grad_mem.shape[0], :]
    seq_out.finish(r.sum_out)
    seq_kv.finish(r.sum_kv)
    seq_q.finish(r.sum_q)
    rows = r.norm_sum[...]
    for ahead in range(1, 2 * chips):
        norm_tp(ahead).wait_recv()
        rows = rows + r.norm_tp[ahead - 1]
    r.norms[...] = rows

    for ahead in range(1, 2 * chips):
        norm_tp(ahead).wait_send()
    for seq_sum in (seq_out, seq_kv, seq_q):
        seq_sum.end()
    seq_cross.end(near=False)
    for part in range(n):
        for ahead in range(1, chips):
            out_copy(ahead, part).wait_send()
    seq_page.end(near=False)
    for ahead in range(1, seqs):
        norm_seq(ahead).wait_send()
    for ahead in range(1, inner):
        page_near(ahead).wait_send()
    sums_prev.own_end()
    sums.own_end()
    pl.when(place.has_prev)(lambda: shifts(lambda copy: copy.wait_send()))


def closing(chips, seqs, ids, offsets, a, f, e, mem_true, w):
    tokens, width = a.q.shape
    dim = w.attn_output.shape[1]
    blocks = tokens // BLOCK
    own = tokens // (2 * chips)
    mem_rows, wide = e.mem_sum.shape
    rows, inner = SeqSum.ROWS, seqs // SeqSum.ROWS
    sent = -(-mem_true // 16) * 16
    dma = pltpu.SemaphoreType.DMA
    vmem = lambda array: (array, "vmem")
    late = lambda array: (array, "late")
    hbm = lambda array: (array, "hbm")
    return call(
        functools.partial(close_body, chips, seqs),
        "closing",
        dict(
            ids=(ids, "smem"),
            offsets=(offsets, "smem"),
            cross_low=hbm(e.cross_low),
            cross_own=hbm(e.cross_own),
            out_low=hbm(e.out_low),
            out_own=hbm(e.out_own),
            mem_sum=vmem(e.mem_sum),
            g_in=vmem(e.g),
            wo=vmem(w.attn_output),
            q=vmem(a.q),
            kext=vmem(a.kext),
            vext=vmem(a.vext),
            mixed=vmem(f.mixed1),
            lse=vmem(f.lse1),
            wq=vmem(w.attn_query),
            wk=vmem(w.attn_key),
            wv=vmem(w.attn_value),
            gain=vmem(w.self_gain),
            norm_cross=vmem(e.norm),
            norm_ffn=vmem(f.norm),
            pages=vmem(a.pages),
            n1=late(a.n1),
            half=late(a.half),
            prev=late(a.prev),
            grad_in=hbm(e.grad),
        ),
        dict(
            grad=((own, dim), F32, "vmem"),
            out=((own, dim), BF16, "vmem"),
            norms=((8, dim // seqs), F32, "vmem"),
            sum_w=((dim // seqs, 4 * width), F32, "vmem"),
            sum_q=((dim // seqs, width), F32, "vmem"),
            sum_kv=((dim // seqs, 2 * width), F32, "vmem"),
            sum_out=((dim // seqs, width), F32, "vmem"),
            grad_mem=((mem_true, wide), F32, "vmem"),
        ),
        dict(
            **sum_scratch(chips, tokens, dim, "prev_"),
            **sum_scratch(chips, tokens, dim),
            **SeqSum.scratch(seqs, (dim // seqs, 4 * width), BF16, "cross_", near=False, low=False),
            out_sum=pltpu.VMEM((own, dim), F32),
            out_far=pltpu.VMEM((chips - 1, own // CHUNK, CHUNK, dim), BF16),
            hs=dma((chips - 1, own // CHUNK)),
            hr=dma((chips - 1, own // CHUNK)),
            **SeqSum.scratch(seqs, (dim // seqs, width), BF16, "q_"),
            **SeqSum.scratch(seqs, (dim // seqs, 2 * width), BF16, "kv_"),
            **SeqSum.scratch(seqs, (dim // seqs, width), BF16, "out_"),
            **SeqSum.scratch(seqs, (sent, wide), BF16, "page_", near=False),
            norm_seq=pltpu.VMEM((seqs - 1, 8, dim // seqs), F32),
            nss=dma((seqs - 1,)),
            nsr=dma((seqs - 1,)),
            page_out=pltpu.VMEM((inner - 1, blocks, sent, wide), BF16),
            page_in=pltpu.VMEM((inner - 1, blocks, sent, wide), BF16),
            page_sum=pltpu.VMEM((sent, wide), F32),
            pns=dma((inner - 1,)),
            pnr=dma((inner - 1,)),
            causal=pltpu.VMEM((BLOCK, BLOCK), F32),
            dout=pltpu.VMEM((tokens, width), BF16),
            dots=pltpu.VMEM((width // PAIR, 8, tokens), F32),
            dq=pltpu.VMEM((tokens, width), F32),
            dk=pltpu.VMEM((2 * tokens, width), F32),
            dv=pltpu.VMEM((2 * tokens, width), F32),
            gq=pltpu.VMEM((tokens, width), BF16),
            gkv=pltpu.VMEM((2, 2 * tokens, width), BF16),
            g_q=pltpu.VMEM((dim, width), BF16),
            g_kv=pltpu.VMEM((dim, 2 * width), BF16),
            g_out=pltpu.VMEM((dim, width), BF16),
            grad_own=pltpu.VMEM((own, dim), F32),
            fetch=dma((4,)),
            shift_out=pltpu.VMEM((own, dim), BF16),
            shift_in=pltpu.VMEM((own, dim), BF16),
            ks=dma((own // CHUNK,)),
            kr=dma((own // CHUNK,)),
            norm_out=pltpu.VMEM((seqs, 8, dim // seqs), F32),
            norm_sum=pltpu.VMEM((8, dim // seqs), F32),
            norm_tp=pltpu.VMEM((2 * chips - 1, 8, dim // seqs), F32),
            nts=dma((2 * chips - 1,)),
            ntr=dma((2 * chips - 1,)),
        ),
        3,
        20 * tokens * 3 * BLOCK * width,
    )


def layout_body(width, per_tp, *refs):
    sources, results, places, sems = refs[:10], refs[10:-11], refs[-11:-1], refs[-1]
    copies = [pltpu.make_async_copy(src, dst, sems.at[i]) for i, (src, dst) in enumerate(zip(sources, places))]
    for copy in copies:
        copy.start()
    for copy in copies:
        copy.wait()
    sum_q, sum_kv, sum_out, sum_w, sum_up, sum_down, grad, out, grad_mem, norms = places
    (out_out, grad_out, mem_out, q_out, k_out, v_out, o_out, cq_out, ck_out, cv_out, co_out, up_out, down_out) = results[:-6]
    out_out[...] = out[...]
    grad_out[...] = grad[...]
    mem_out[0] = grad_mem[...]
    q_out[...] = sum_q[...]
    k_out[...] = sum_kv[:, :width]
    v_out[...] = sum_kv[:, width:]
    o_out[...] = jnp.transpose(sum_out[...])
    for piece, ref in enumerate((cq_out, ck_out, cv_out)):
        ref[...] = sum_w[:, piece * width : (piece + 1) * width]
    co_out[...] = jnp.transpose(sum_w[:, 3 * width :])
    up_out[...] = sum_up[...]
    down_out[...] = jnp.transpose(sum_down[...])
    columns = norms.shape[1]
    first = lax.axis_index("tp") * per_tp
    from_column = lax.broadcasted_iota(jnp.int32, (columns, per_tp), 0)
    to_column = lax.broadcasted_iota(jnp.int32, (columns, per_tp), 1)
    pick = (from_column == to_column + first).astype(F32)
    mine = jnp.dot(norms[...], pick, precision=lax.Precision.HIGHEST, preferred_element_type=F32)
    for row, ref in enumerate(results[-6:]):
        ref[...] = mine[row : row + 1, :]


def layout(tps, width, c, e):
    share_rows, hidden = e.sum_up.shape
    own, dim = c.grad.shape
    per_tp = share_rows // tps
    weights = [(share_rows, width)] * 3 + [(width, share_rows)]
    dims = [(own, dim), (own, dim), (1, *c.grad_mem.shape), *weights, *weights, (share_rows, hidden), (hidden, share_rows)]
    types = [BF16] + [F32] * (len(dims) - 1)
    dims += [(1, per_tp)] * 6
    types += [F32] * 6
    sources = (c.sum_q, c.sum_kv, c.sum_out, c.sum_w, e.sum_up, e.sum_down, c.grad, c.out, c.grad_mem, c.norms)
    return pl.pallas_call(
        functools.partial(layout_body, width, per_tp),
        name="layout",
        out_shape=[jax.ShapeDtypeStruct(d, t) for d, t in zip(dims, types)],
        in_specs=[pl.BlockSpec(memory_space=pltpu.HBM)] * len(sources),
        out_specs=[VMEM] * len(dims),
        scratch_shapes=[pltpu.VMEM(source.shape, source.dtype) for source in sources]
        + [pltpu.SemaphoreType.DMA((len(sources),))],
        compiler_params=pltpu.CompilerParams(vmem_limit_bytes=62 << 20),
    )(*sources)


def on_device(
    hidden_in,
    memory,
    page_ids,
    token_offsets,
    memory_mask,
    attn_query,
    attn_key,
    attn_value,
    attn_output,
    cross_query,
    cross_key,
    cross_value,
    cross_output,
    ffn_up,
    ffn_down,
    self_gain,
    self_shift,
    cross_gain,
    cross_shift,
    ffn_gain,
    ffn_shift,
    out_grad,
):
    tps, seqs = lax.axis_size("tp"), lax.axis_size("seq")
    chips = tps // 2
    width = attn_query.shape[1]
    w = Refs()
    w.attn_query, w.attn_key, w.attn_value, w.attn_output = attn_query, attn_key, attn_value, attn_output
    w.cross_query, w.cross_key, w.cross_value, w.cross_output = cross_query, cross_key, cross_value, cross_output
    w.up, w.down = ffn_up, ffn_down
    w.self_gain, w.self_shift = self_gain.reshape(1, -1), self_shift.reshape(1, -1)
    w.cross_gain, w.cross_shift = cross_gain.reshape(1, -1), cross_shift.reshape(1, -1)
    w.ffn_gain, w.ffn_shift = ffn_gain.reshape(1, -1), ffn_shift.reshape(1, -1)

    a = opening(
        chips,
        seqs,
        page_ids,
        hidden_in,
        out_grad,
        memory,
        memory_mask,
        w.self_gain,
        w.self_shift,
        attn_query,
        attn_key,
        attn_value,
    )
    f = forward(chips, seqs, page_ids, token_offsets, a, w)
    e = cross_back(chips, seqs, a, f, w)
    c = closing(chips, seqs, page_ids, token_offsets, a, f, e, memory.shape[1], w)
    results = layout(tps, width, c, e)
    return (
        results[0],
        results[1],
        results[2],
        *results[3:11],
        results[11],
        results[12],
        *[values.reshape(-1) for values in results[13:]],
    )


def solution(mesh):
    both = ("seq", "tp")
    in_specs = (
        P(both, None),
        P("seq", None, None),
        P("seq"),
        P("seq"),
        P("seq", None),
        P(None, "tp"),
        P(None, "tp"),
        P(None, "tp"),
        P("tp", None),
        P(None, "tp"),
        P(None, "tp"),
        P(None, "tp"),
        P("tp", None),
        P(None, "tp"),
        P("tp", None),
        P(),
        P(),
        P(),
        P(),
        P(),
        P(),
        P(both, None),
    )
    out_specs = (
        P(both, None),
        P(both, None),
        P("seq", None, "tp"),
        P("seq", "tp"),
        P("seq", "tp"),
        P("seq", "tp"),
        P("tp", "seq"),
        P("seq", "tp"),
        P("seq", "tp"),
        P("seq", "tp"),
        P("tp", "seq"),
        P("seq", "tp"),
        P("tp", "seq"),
        P(both),
        P(both),
        P(both),
        P(both),
        P(both),
        P(both),
    )
    return jax.shard_map(on_device, mesh=mesh, in_specs=in_specs, out_specs=out_specs, check_vma=False)
```
